128 devices in a mesh: req: 4 (over z), blk: 32 (over y, x, core).
Axes of the slice: x: 4, y: 4, z: 4, core: 2. Of those that a mesh axis runs over, the one named last changes fastest.
Arguments:
- tree_input: bfloat16 [6144, 1280], P(('req', 'blk')), may hold values from -6 to 6
- cache: bfloat16 [4, 2, 65536, 1280], P('req', None, 'blk'), may hold values from -1200 to 1200, as said below
- page_table: int32 [4, 512], P('req'), may hold values from 0 to 511, each once within a row
- lengths: int32 [4, 32], P('req'), may hold values from 1 to 32768, 57344 in all within a row
- parents: int32 [128, 48], P(('req', 'blk')), may hold values from 0 to 29, as said below
- accept_leaf: int32 [4, 32], P('req'), may hold values from 0 to 47
- w_qkv: bfloat16 [1280, 3840], P(None, 'blk'), may hold values from -0.15625 to 0.15625
- w_out: bfloat16 [1280, 1280], P(None, 'blk'), may hold values from -0.15625 to 0.15625
- w_up: bfloat16 [1280, 1280], P(None, 'blk'), may hold values from -0.15625 to 0.15625
- w_down: bfloat16 [1280, 1280], P('blk'), may hold values from -0.15625 to 0.15625
- w_draft: bfloat16 [4, 1280, 1280], P(None, None, 'blk'), may hold values from -0.15625 to 0.15625
- w_patch: bfloat16 [1280, 1280], P(None, 'req'), may hold values from -0.15625 to 0.15625
Outputs:
- layer_out: bfloat16 [6144, 1280], P(('req', 'blk'))
- drafts: bfloat16 [4, 6144, 1280], P(None, ('req', 'blk'))
- cache_new: bfloat16 [4, 2, 65536, 1280], P('req', None, 'blk')
The draws below stay inside these ranges and needn't reach their ends.
Inputs may be any that keep to these rules, and one draw needn't show every extreme that they name: `cache`: keys of the pool may hold a few rows of far larger size. `parents`: node 0 is its own parent. The nodes form 5 levels of sizes 1, 4, 10, 15, 18 in index order, and every other node's parent lies in the level before its own. `page_table`: row g holds the pool pages of group g; request r's pages are the npages_r entries after those of requests before it (see the steps), and page p is held by index p // 16 of blk.
All inputs are finite; a program needn't handle non-finite values.
Results may differ from the reference program's by a relative error of at most 0.018.
The reference program's roundings to bfloat16 on the way count: a program that leaves them out, or rounds other values in their place, can miss the bound.
Values may be sent and summed in bfloat16 or wider, within the bound.
A program may use at most 192 MiB of HBM per device.

```python
import math
import jax
import jax.numpy as jnp
import numpy as np
from jax import lax

D = 1280
H = 16
HD = 80
FF = 1280
OUTW = 1280
KHEADS = 4
TREE = 48
DEPTH = 5
PAGE = 128
GROUP_REQS = 32
REQS = 128
ROWS = 6144
POOL_PAGES = 512
SLOTS = 65536
LEN_TOTAL = 57344
MAXLEN = 32768
N_REQ = 4


def draw_cache(key, part):
    shape = (N_REQ, 2, SLOTS, D)
    base = jnp.clip(jax.random.normal(jax.random.fold_in(key, 11), shape, jnp.float32), -6.0, 6.0)
    key_side = (jnp.arange(2) == 0).reshape(1, 2, 1, 1)
    base = base * jnp.where(key_side, 2.5, 1.0)
    return base.astype(jnp.bfloat16)


def draw_parents(key, part):
    starts = np.array([0, 1, 5, 15, 30, 48])
    level = np.searchsorted(starts, np.arange(48), side='right') - 1
    lowest = np.where(level > 0, starts[np.maximum(level - 1, 0)], 0)
    spread = np.where(level > 0, starts[level] - lowest, 1)
    offset = jax.random.randint(jax.random.fold_in(key, 17), (REQS, TREE), 0, 1 << 20)
    return (jnp.asarray(lowest, jnp.int32)[None, :] + offset % jnp.asarray(spread, jnp.int32)[None, :]).astype(jnp.int32)


def plant(entries, rng, low, largest):
    spot = [jax.random.randint(jax.random.fold_in(rng, axis), (), 0, length) for axis, length in enumerate(entries.shape)]
    widest = entries.shape.index(max(entries.shape))
    beside = spot[:widest] + [(spot[widest] + 1) % entries.shape[widest]] + spot[widest + 1:]
    return entries.at[tuple(spot)].set(low).at[tuple(beside)].set(largest)


def levels(rng, extent, shards, least, largest):
    def one(axis_at, parts):
        steps = jax.random.uniform(jax.random.fold_in(jax.random.fold_in(rng, 6), axis_at), (parts,), jnp.float32, least / len(shards), largest / len(shards))
        return jnp.repeat(jnp.exp(steps), extent[axis_at] // parts).reshape((-1,) + (1,) * (len(extent) - axis_at - 1))

    gain = one(*shards[0])
    for cut in shards[1:]:
        gain = gain * one(*cut)
    return gain


def profile(number_of, total, most, lean):
    portions = [(1 << 20) // math.isqrt(grade ** lean) + 1 for grade in range(2, number_of + 1)]
    surplus, counts = total - most - (number_of - 1), [1] * (number_of - 1)
    while surplus > 0:
        movable = [i for i in range(number_of - 1) if counts[i] < most]
        whole, left = sum([portions[i] for i in movable]), surplus
        for i in movable:
            extra = min(most - counts[i], max(1, left * portions[i] // whole), surplus)
            counts[i] = counts[i] + extra
            surplus = surplus - extra
    return np.array([most] + counts)


def ragged(stream_key, count, total, reach, slope):
    if count == 2:
        one = jax.random.randint(stream_key, (), max(1, total - reach), min(reach, total - 1) + 1)
        return jnp.stack([one, total - one])
    sizes = jnp.asarray(profile(count, total, reach, slope), jnp.int32)
    twos = (count - 1) // 2
    source_of, sink = sizes[1:1 + 2 * twos:2], sizes[2:2 + 2 * twos:2]
    margin = jnp.minimum(source_of - 1, reach - sink)
    shifted = jax.random.randint(jax.random.fold_in(stream_key, 1), (twos,), 0, 1 << 20) % (margin + 1)
    sizes = sizes.at[1:1 + 2 * twos:2].set(source_of - shifted).at[2:2 + 2 * twos:2].set(sink + shifted)
    return sizes[jax.random.permutation(jax.random.fold_in(stream_key, 2), count)]


def noise(key, dims, scale, most, cuts=(), kind=jnp.bfloat16):
    gain = levels(key, dims, cuts, -0.22, 0.18) if cuts else 1.0
    values = jax.random.normal(key, dims, jnp.float32) * scale * gain
    return jnp.minimum(jnp.maximum(values, -most), most).astype(kind)


def setup_inputs(seed: int = 0) -> dict:
    splits = jax.random.split(jax.random.key(seed), 13)
    tree_input = noise(splits[0], (ROWS, D), 1.0, 6.0, ((0, 128),))
    cache = draw_cache(jax.random.fold_in(splits[12], 71), 0)
    page_table = jax.vmap(lambda own: jax.random.permutation(own, POOL_PAGES))(jax.random.split(splits[2], N_REQ)).reshape((N_REQ, POOL_PAGES)).astype(jnp.int32)
    lengths = jax.vmap(lambda own: ragged(own, GROUP_REQS, LEN_TOTAL, MAXLEN, 2))(jax.random.split(splits[3], N_REQ)).reshape((N_REQ, GROUP_REQS)).astype(jnp.int32)
    parents = draw_parents(jax.random.fold_in(splits[12], 71), 0)
    accept_leaf = plant(jax.random.randint(splits[5], (N_REQ, GROUP_REQS), 0, TREE), jax.random.fold_in(splits[5], 1), 0, TREE - 1).astype(jnp.int32)
    w_qkv = noise(splits[6], (D, 3 * D), D ** -0.5, 0.15625, ((1, 32),))
    w_out = noise(splits[7], (D, D), D ** -0.5, 0.15625, ((1, 32),))
    w_up = noise(splits[8], (D, FF), D ** -0.5, 0.15625, ((1, 32),))
    w_down = noise(splits[9], (FF, D), FF ** -0.5, 0.15625, ((0, 32),))
    w_draft = noise(splits[10], (KHEADS, D, D), D ** -0.5, 0.15625, ((2, 32),))
    w_patch = noise(splits[11], (D, OUTW), D ** -0.5, 0.15625, ((1, 4),))
    return {"tree_input": tree_input, "cache": cache, "page_table": page_table, "lengths": lengths, "parents": parents, "accept_leaf": accept_leaf, "w_qkv": w_qkv, "w_out": w_out, "w_up": w_up, "w_down": w_down, "w_draft": w_draft, "w_patch": w_patch}


EPS = 1e-06
NEG = -1e+30

def rms_rows(values):
    wide = values.astype(jnp.float32)
    return (wide * lax.rsqrt(lax.optimization_barrier(jnp.mean(wide * wide, axis=-1, keepdims=True)) + EPS)).astype(jnp.bfloat16)

def ancestors(parent_rows):
    nodes = jnp.arange(TREE, dtype=jnp.int32)
    current = jnp.broadcast_to(nodes, parent_rows.shape).astype(jnp.int32)
    marks = current[:, :, None] == nodes[None, None, :]
    for level in range(DEPTH - 1):
        current = jnp.take_along_axis(parent_rows, current, axis=1)
        marks = marks | (current[:, :, None] == nodes[None, None, :])
    return marks

def group_step(inputs):
    query, key_new, value_new, pool, page_row, length_row, parent_rows, leaf_row = inputs
    requests = length_row.shape[0]
    pool_count = page_row.shape[0]
    scale = 1.0 / math.sqrt(HD)
    npages = (length_row + DEPTH + PAGE - 1) // PAGE
    page_ends = jnp.cumsum(npages).astype(jnp.int32)
    offsets = (page_ends - npages).astype(jnp.int32)
    inverse = jnp.zeros((pool_count,), jnp.int32).at[page_row].set(jnp.arange(pool_count, dtype=jnp.int32))
    owner = lax.optimization_barrier(jnp.sum((page_ends[None, :] <= inverse[:, None]).astype(jnp.int32), axis=1))
    owner_hot = owner[:, None] == jnp.arange(requests, dtype=jnp.int32)[None, :]
    safe_owner = jnp.minimum(owner, requests - 1)
    page_len = jnp.where(owner < requests, length_row[safe_owner], 0)
    page_slot = inverse - offsets[safe_owner]
    positions = page_slot[:, None] * PAGE + jnp.arange(PAGE, dtype=jnp.int32)[None, :]
    valid = positions < page_len[:, None]
    query4 = query.reshape(requests, TREE, H, HD).astype(jnp.float32)
    keys = pool[0].reshape(pool_count, PAGE, H, HD).astype(jnp.float32)
    values = pool[1].reshape(pool_count, PAGE, H, HD).astype(jnp.float32)
    query_page = query4[safe_owner]
    scores = jnp.einsum('pqhd,pthd->pqht', query_page, keys, precision=lax.Precision.HIGHEST) * scale
    masked = jnp.where(valid[:, None, None, :], scores, NEG)
    page_max = lax.optimization_barrier(jnp.max(masked, axis=-1))
    cache_max = lax.optimization_barrier(jnp.max(jnp.where(owner_hot[:, :, None, None], page_max[:, None], NEG), axis=0))
    key4 = key_new.reshape(requests, TREE, H, HD).astype(jnp.float32)
    value4 = value_new.reshape(requests, TREE, H, HD).astype(jnp.float32)
    marks = ancestors(parent_rows)
    tree_scores = jnp.einsum('rqhd,rkhd->rqhk', query4, key4, precision=lax.Precision.HIGHEST) * scale
    tree_masked = jnp.where(marks[:, :, None, :], tree_scores, NEG)
    row_top = jnp.maximum(cache_max, lax.optimization_barrier(jnp.max(tree_masked, axis=-1)))
    page_top = row_top[safe_owner]
    weights = jnp.where(valid[:, None, None, :], jnp.exp(masked - page_top[..., None]), 0.0)
    weights_low = lax.optimization_barrier(weights.astype(jnp.bfloat16)).astype(jnp.float32)
    hot = owner_hot.astype(jnp.float32)
    cache_den = jnp.einsum('pr,pqh->rqh', hot, lax.optimization_barrier(jnp.sum(weights, axis=-1)), precision=lax.Precision.HIGHEST)
    page_num = jnp.einsum('pqht,pthd->pqhd', weights_low, values, precision=lax.Precision.HIGHEST)
    cache_num = jnp.einsum('pr,pqhd->rqhd', hot, page_num, precision=lax.Precision.HIGHEST)
    tree_weights = jnp.where(marks[:, :, None, :], jnp.exp(tree_masked - row_top[..., None]), 0.0)
    tree_low = lax.optimization_barrier(tree_weights.astype(jnp.bfloat16)).astype(jnp.float32)
    denom = cache_den + lax.optimization_barrier(jnp.sum(tree_weights, axis=-1))
    numer = cache_num + jnp.einsum('rqhk,rkhd->rqhd', tree_low, value4, precision=lax.Precision.HIGHEST)
    attended = (numer / denom[..., None]).reshape(requests * TREE, H * HD).astype(jnp.bfloat16)
    chosen = marks[jnp.arange(requests), leaf_row]
    ranks = jnp.cumsum(chosen.astype(jnp.int32), axis=1) - 1
    written = length_row[:, None] + ranks
    page_index = page_row[jnp.clip(offsets[:, None] + written // PAGE, 0, pool_count - 1)]
    target = jnp.where(chosen, page_index * PAGE + written % PAGE, pool_count * PAGE).reshape(-1)
    new_keys = pool[0].at[target].set(key_new, mode='drop')
    new_values = pool[1].at[target].set(value_new, mode='drop')
    return (attended, jnp.stack([new_keys, new_values]))

def reference(tree_input, cache, page_table, lengths, parents, accept_leaf, w_qkv, w_out, w_up, w_down, w_draft, w_patch):
    width = tree_input.shape[1]
    groups = lengths.shape[0]
    normed = rms_rows(tree_input)
    projected = jnp.dot(normed, w_qkv, preferred_element_type=jnp.float32).astype(jnp.bfloat16)

    def by_group(block):
        return block.reshape(groups, -1, block.shape[-1])
    attended, cache_new = lax.map(group_step, (by_group(projected[:, :width]), by_group(projected[:, width:2 * width]), by_group(projected[:, 2 * width:]), cache, page_table, lengths, parents.reshape(groups, -1, TREE), accept_leaf))
    attended = attended.reshape(-1, width)
    proj = jnp.dot(attended, w_out, preferred_element_type=jnp.float32).astype(jnp.bfloat16)
    mid = (tree_input.astype(jnp.float32) + proj.astype(jnp.float32)).astype(jnp.bfloat16)
    hidden = jax.nn.gelu(jnp.dot(rms_rows(mid), w_up, preferred_element_type=jnp.float32)).astype(jnp.bfloat16)
    layer_out = (mid.astype(jnp.float32) + jnp.dot(hidden, w_down, preferred_element_type=jnp.float32)).astype(jnp.bfloat16)
    draft_normed = rms_rows(layer_out)
    branch = jax.nn.silu(jnp.einsum('nd,kdc->knc', draft_normed.astype(jnp.float32), w_draft.astype(jnp.float32))).astype(jnp.bfloat16)
    drafted = (layer_out.astype(jnp.float32)[None] + branch.astype(jnp.float32)).astype(jnp.bfloat16)
    drafts = jnp.einsum('knd,do->kno', drafted.astype(jnp.float32), w_patch.astype(jnp.float32)).astype(jnp.bfloat16)
    return (layer_out, drafts, cache_new)
```

```python
import math

import jax
import jax.numpy as jnp
from jax import lax
from jax.experimental import pallas as pl
from jax.experimental.pallas import tpu as pltpu
from jax.sharding import PartitionSpec as P

H = 16
HD = 80
TREE = 48
DEPTH = 5
PAGE = 128
BLK = 32
WIDTH = H * HD

EPS = 1e-06
LOWEST = -8388608.0
LEVEL_START = (0, 1, 5, 15, 30, 48)
MESH = pl.DeviceIdType.MESH
ROWSLOT = ((0, 0), (-1, 0), (1, 0), (2, 0))


def rms_rows(values):
    wide = values.astype(jnp.float32)
    return (wide * lax.rsqrt(jnp.mean(wide * wide, axis=-1, keepdims=True) + EPS)).astype(
        jnp.bfloat16
    )


def dot_t(left, right):
    return lax.dot_general(
        left, right, (((1,), (1,)), ((), ())), preferred_element_type=jnp.float32
    )


class Spot:
    def __init__(self):
        self.me = lax.axis_index("blk")
        self.core = self.me % 2
        x = (self.me // 2) % 4
        y = self.me // 8
        self.one = x + self.core * (y - x)
        self.two = y + self.core * (x - y)
        self.sibling = self.me + 1 - 2 * self.core

    def at(self, a, b):
        return self.core + 2 * self.chip(a, b)

    def chip(self, a, b):
        one = (self.one + a + 4) % 4
        two = (self.two + b + 4) % 4
        return (1 + 3 * self.core) * one + (4 - 3 * self.core) * two


def greet_plane(spot):
    barrier = pltpu.get_barrier_semaphore()
    for who in (spot.at(1, 0), spot.at(-1, 0), spot.at(0, 1), spot.at(0, -1), spot.sibling):
        pl.semaphore_signal(barrier, inc=1, device_id={"blk": who}, device_id_type=MESH)
    pl.semaphore_wait(barrier, 5)


def numbered(names):
    return {name: i for i, name in enumerate(names)}


GATHER = numbered(
    ["L", "R", "OA", "OB"]
    + [f"{kind}{k}" for k in range(4) for kind in ("D", "U", "PA", "PB")]
    + [f"S{k}" for k in range(16)]
)


def sender(sent, ssem, rsem, events):
    def put(event, src, dst, who):
        copy = pltpu.make_async_remote_copy(
            src_ref=src,
            dst_ref=dst,
            send_sem=ssem(events[event]),
            recv_sem=rsem(events[event]),
            device_id={"blk": who},
            device_id_type=MESH,
        )
        copy.start()
        sent[event] = copy

    return put


def gather_steps(spot, shard, view, ssem, rsem, lsem, cut):
    sent = {}
    send = sender(sent, ssem, rsem, GATHER)

    def put(event, src, slot, who, half=None):
        dst = view(slot)
        if half is not None:
            src, dst = cut(src, half), cut(dst, half)
        send(event, src, dst, who)

    right, left = spot.at(1, 0), spot.at(-1, 0)
    up, down = spot.at(0, 1), spot.at(0, -1)
    local = pltpu.make_async_copy(shard, view(spot.me), lsem)
    local.start()
    put("L", shard, spot.me, right)
    put("R", shard, spot.me, left)
    put("D0", shard, spot.me, up)
    put("U0", shard, spot.me, down)
    put("S0", shard, spot.me, spot.sibling)
    yield
    for k, event in ((1, "L"), (2, "R")):
        slot = spot.at(*ROWSLOT[k])
        sent[event].wait_recv()
        if k == 1:
            put("OA", view(slot), slot, right, 0)
        else:
            put("OB", view(slot), slot, left, 1)
        put(f"D{k}", view(slot), slot, up)
        put(f"U{k}", view(slot), slot, down)
        put(f"S{k}", view(slot), slot, spot.sibling)
        yield

    def column(k):
        a = ROWSLOT[k][0]
        slot = spot.at(a, -1)
        sent[f"D{k}"].wait_recv()
        put(f"PA{k}", view(slot), slot, up, 0)
        put(f"S{4 + k}", view(slot), slot, spot.sibling)
        slot = spot.at(a, 1)
        sent[f"U{k}"].wait_recv()
        put(f"PB{k}", view(slot), slot, down, 1)
        put(f"S{8 + k}", view(slot), slot, spot.sibling)

    column(0)
    yield
    sent["OA"].wait_recv()
    sent["OB"].wait_recv()
    slot = spot.at(2, 0)
    put("D3", view(slot), slot, up)
    put("U3", view(slot), slot, down)
    put("S3", view(slot), slot, spot.sibling)
    yield
    for k in (1, 2, 3):
        column(k)
        yield
    for k in range(4):
        slot = spot.at(ROWSLOT[k][0], 2)
        sent[f"PA{k}"].wait_recv()
        sent[f"PB{k}"].wait_recv()
        put(f"S{12 + k}", view(slot), slot, spot.sibling)
        yield
    for k in range(16):
        sent[f"S{k}"].wait_recv()
    local.wait()
    for event in GATHER:
        sent[event].wait_send()


def run_all(steps):
    steps = list(steps)
    while steps:
        alive = []
        for step in steps:
            try:
                next(step)
                alive.append(step)
            except StopIteration:
                pass
        steps = alive


def row_halves(rows):
    first = ((rows // 2) + 7) // 8 * 8

    def cut(ref, half):
        return ref.at[pl.ds(0, first)] if half == 0 else ref.at[pl.ds(first, rows - first)]

    return cut


def gather_all(spot, ins, outs, ssem, rsem, lsem):
    count = len(GATHER)
    return [
        gather_steps(
            spot,
            ins[i],
            lambda slot, i=i: outs[i].at[slot],
            lambda e, i=i: ssem.at[i * count + e],
            lambda e, i=i: rsem.at[i * count + e],
            lsem.at[i],
            row_halves(ins[i].shape[0]),
        )
        for i in range(len(ins))
    ]


def gather_sems(arrays):
    return [
        pltpu.SemaphoreType.DMA((arrays * len(GATHER),)),
        pltpu.SemaphoreType.DMA((arrays * len(GATHER),)),
        pltpu.SemaphoreType.DMA((arrays,)),
    ]


ANY = pl.BlockSpec(memory_space=pl.ANY)
VMEM = pl.BlockSpec(memory_space=pltpu.VMEM)


def all_gather(shards, collective_id, name):
    count = len(shards)

    def kernel(*refs):
        spot = Spot()
        greet_plane(spot)
        run_all(gather_all(spot, refs[:count], refs[count : 2 * count], *refs[2 * count :]))

    return pl.pallas_call(
        kernel,
        out_shape=[jax.ShapeDtypeStruct((BLK,) + s.shape, s.dtype) for s in shards],
        in_specs=[ANY] * count,
        out_specs=[ANY] * count,
        scratch_shapes=gather_sems(count),
        compiler_params=pltpu.CompilerParams(collective_id=collective_id, has_side_effects=True),
        name=name,
    )(*shards)


def window(w):
    return 128 * (5 * (w // 4) + w % 4), 32 * (w % 4)


def attend_kernel(
    tables, query_ref, cache_ref, proj_ref, marks_ref, num_ref, stats_ref, new_ref, acc, tops, dens
):
    step = pl.program_id(0)
    pages = pl.num_programs(0) - 1
    owner = tables[0, step]
    start = tables[1, step]
    length = tables[2, step]
    count = tables[3, step]
    factor = math.log2(math.e) / math.sqrt(HD)

    @pl.when(step == 0)
    def _():
        tops[...] = jnp.full_like(tops, LOWEST)
        dens[...] = jnp.zeros_like(dens)

        @pl.loop(0, BLK)
        def _(r):
            acc[r] = jnp.zeros(acc.shape[1:], acc.dtype)

    lanes = lax.broadcasted_iota(jnp.int32, (TREE, 128), 1)
    columns = lax.broadcasted_iota(jnp.int32, (TREE, 256), 1)

    def merge(query, key_at, value_at, seen):
        tops_old = tops[owner]
        dens_old = dens[owner]
        tops_new, dens_new = tops_old, dens_old
        for w in range(8):
            first, begin = window(w)
            here = [
                (columns >= begin + HD * i) & (columns < begin + HD * (i + 1)) for i in range(2)
            ]
            picked = query(first)
            stacked = jnp.concatenate(
                [picked * here[i].astype(jnp.float32).astype(jnp.bfloat16) for i in range(2)],
                axis=0,
            )
            scores = dot_t(stacked, key_at(first)) * factor
            weights = []
            scales = []
            for i in range(2):
                head = 2 * w + i
                part = jnp.where(seen, scores[i * TREE : (i + 1) * TREE], LOWEST)
                before = tops_old[:, head : head + 1]
                top = jnp.maximum(before, jnp.ceil(jnp.max(part, axis=1, keepdims=True)))
                weight = jnp.where(seen, jnp.exp2(part - top), 0.0)
                scale = jnp.exp2(before - top)
                total = dens_old[:, head : head + 1] * scale + jnp.sum(
                    weight, axis=1, keepdims=True
                )
                tops_new = jnp.where(lanes == head, top, tops_new)
                dens_new = jnp.where(lanes == head, total, dens_new)
                weights.append(weight.astype(jnp.bfloat16))
                scales.append(scale)
            added = jnp.dot(
                jnp.concatenate(weights, axis=0),
                value_at(first),
                preferred_element_type=jnp.float32,
            )
            window_scale = jnp.where(here[0], scales[0], jnp.where(here[1], scales[1], 1.0))
            window_sum = jnp.where(
                here[0], added[:TREE], jnp.where(here[1], added[TREE:], 0.0)
            )
            old = acc[owner, :, pl.ds(first, 256)]
            acc[owner, :, pl.ds(first, 256)] = old * window_scale + window_sum
        tops[owner] = tops_new
        dens[owner] = dens_new

    @pl.when(step < pages)
    def _():
        seen = lax.broadcasted_iota(jnp.int32, (TREE, PAGE), 1) + start < length
        merge(
            lambda first: query_ref[0, pl.ds(0, TREE), pl.ds(first, 256)],
            lambda first: cache_ref[0, 0, :, pl.ds(first, 256)],
            lambda first: cache_ref[0, 1, :, pl.ds(first, 256)],
            seen,
        )
        row0 = length - start
        touched = (row0 < PAGE) & (row0 + count > 0)

        @pl.when(jnp.logical_not(touched))
        def _():
            new_ref[...] = cache_ref[...]

        @pl.when(touched)
        def _():
            ahead = lax.broadcasted_iota(jnp.int32, (PAGE, 8), 0) - row0
            nth = lax.broadcasted_iota(jnp.int32, (PAGE, 8), 1)
            hot = ((ahead == nth) & (nth < count)).astype(jnp.float32).astype(jnp.bfloat16)
            rows = lax.broadcasted_iota(jnp.int32, (PAGE, WIDTH), 0) - row0
            hit = (rows >= 0) & (rows < count)
            for i in range(2):
                fresh = jnp.dot(
                    hot,
                    query_ref[0, pl.ds(TREE + 8 * i, 8), :],
                    preferred_element_type=jnp.float32,
                )
                kept = cache_ref[0, i].astype(jnp.float32)
                new_ref[0, i] = jnp.where(hit, fresh, kept).astype(jnp.bfloat16)

    @pl.when(step == pages)
    def _():
        merge(
            lambda first: query_ref[0, pl.ds(0, TREE), pl.ds(first, 256)],
            lambda first: proj_ref[:, pl.ds(WIDTH + first, 256)],
            lambda first: proj_ref[:, pl.ds(2 * WIDTH + first, 256)],
            marks_ref[...] > 0.5,
        )

        @pl.loop(0, BLK)
        def _(r):
            num_ref[r] = acc[r].astype(jnp.bfloat16)
            stats_ref[r] = jnp.where(lanes < 64, tops[r], pltpu.roll(dens[r], 64, 1))


def attend(tables, gathered, cache, projected, marks):
    pages = cache.shape[2] // PAGE
    rows = gathered.shape[1]
    page_block = pl.BlockSpec(
        (1, 2, PAGE, WIDTH), lambda p, t: (0, 0, jnp.minimum(p, pages - 1), 0)
    )
    whole3 = lambda p, t: (0, 0, 0)
    return pl.pallas_call(
        attend_kernel,
        out_shape=[
            jax.ShapeDtypeStruct((BLK, TREE, WIDTH), jnp.bfloat16),
            jax.ShapeDtypeStruct((BLK, TREE, 128), jnp.float32),
            jax.ShapeDtypeStruct(cache.shape, cache.dtype),
        ],
        grid_spec=pltpu.PrefetchScalarGridSpec(
            num_scalar_prefetch=1,
            grid=(pages + 1,),
            in_specs=[
                pl.BlockSpec((1, rows, WIDTH), lambda p, t: (t[4, p], 0, 0)),
                page_block,
                pl.BlockSpec((TREE, 3 * WIDTH), lambda p, t: (0, 0)),
                pl.BlockSpec((TREE, TREE), lambda p, t: (0, 0)),
            ],
            out_specs=[
                pl.BlockSpec((BLK, TREE, WIDTH), whole3),
                pl.BlockSpec((BLK, TREE, 128), whole3),
                page_block,
            ],
            scratch_shapes=[
                pltpu.VMEM((BLK, TREE, WIDTH), jnp.float32),
                pltpu.VMEM((BLK, TREE, 128), jnp.float32),
                pltpu.VMEM((BLK, TREE, 128), jnp.float32),
            ],
        ),
        compiler_params=pltpu.CompilerParams(vmem_limit_bytes=48 * 1024 * 1024),
        name="attend",
    )(tables, gathered, cache, projected, marks)


PAIR_ORDER = (
    [(2, b) for b in range(4)]
    + [(1, 2), (1, 3), (-1, 0), (-1, 1)]
    + [(1, 0), (1, 1), (-1, 2), (-1, 3)]
    + [(0, b) for b in range(4)]
)
REDUCE = numbered(
    [f"{kind}{i}{s}" for kind, n in (("P", 16), ("T", 4), ("L", 4), ("R", 4)) for i in range(n) for s in "ns"]
    + [f"{kind}{s}" for kind in ("t0", "t1", "l", "r") for s in "ns"]
)


def split_stats(stats):
    return stats, pltpu.roll(stats, 64, 1)


def combine(parts, spread):
    stats = [split_stats(s) for _, s in parts]
    lanes = lax.broadcasted_iota(jnp.int32, stats[0][0].shape, 1)
    top = stats[0][0]
    for s, _ in stats[1:]:
        top = jnp.maximum(top, s)
    total = None
    num = None
    for (n, _), (s, d) in zip(parts, stats):
        scale = jnp.where(lanes < H, jnp.exp2(jnp.minimum(s - top, 0.0)), 0.0)
        wide = jnp.dot(scale.astype(jnp.bfloat16), spread, preferred_element_type=jnp.float32)
        d = d * scale
        n = n.astype(jnp.float32) * wide
        total = d if total is None else total + d
        num = n if num is None else num + n
    return num, top, total


def join_stats(top, total):
    lanes = lax.broadcasted_iota(jnp.int32, top.shape, 1)
    return jnp.where(lanes < H, top, pltpu.roll(jnp.where(lanes < H, total, 0.0), 64, 1))


def reduce_steps(spot, num, stats, out, spread, bufs, ssem, rsem):
    pair_n, pair_s, work_n, work_s, thru_n, thru_s, left_n, left_s, right_n, right_s = bufs[:10]
    fin_n, fin_s, two_n, two_s = bufs[10:]
    sent = {}
    send = sender(sent, ssem, rsem, REDUCE)

    def put(event, src_n, src_s, dst_n, dst_s, who):
        send(event + "n", src_n, dst_n, who)
        send(event + "s", src_s, dst_s, who)

    def took(event):
        sent[event + "n"].wait_recv()
        sent[event + "s"].wait_recv()

    right, left = spot.at(1, 0), spot.at(-1, 0)
    up, down = spot.at(0, 1), spot.at(0, -1)
    other = (1 - spot.core) * 16
    mine = spot.core * 16
    for i, (a, b) in enumerate(PAIR_ORDER):
        c = other + spot.chip(b, a)
        put(f"P{i}", num.at[c], stats.at[c], pair_n.at[i], pair_s.at[i], spot.sibling)
    yield

    def store(dst_n, dst_s, parts):
        n, top, total = combine(parts, spread())
        dst_n[...] = n.astype(jnp.bfloat16)
        dst_s[...] = join_stats(top, total)

    place = {pair: i for i, pair in enumerate(PAIR_ORDER)}
    for i, (a, b) in enumerate(PAIR_ORDER):
        took(f"P{i}")
        c = mine + spot.chip(a, b)
        store(
            work_n.at[i], work_s.at[i], [(num[c], stats[c]), (pair_n[i], pair_s[i])]
        )
        if a == 2:
            put(
                f"T{b}", work_n.at[i], work_s.at[i], thru_n.at[b], thru_s.at[b],
                right if b < 2 else left,
            )
        elif (a == 1 and b >= 2):
            put(f"L{b}", work_n.at[i], work_s.at[i], left_n.at[b], left_s.at[b], right)
        elif (a == -1 and b < 2):
            put(f"R{b}", work_n.at[i], work_s.at[i], right_n.at[b], right_s.at[b], left)
        yield
    for b in range(4):
        took(f"T{b}")
        a = 1 if b < 2 else -1
        i = place[(a, b)]
        store(
            work_n.at[i], work_s.at[i], [(work_n[i], work_s[i]), (thru_n[b], thru_s[b])]
        )
        if a == 1:
            put(f"L{b}", work_n.at[i], work_s.at[i], left_n.at[b], left_s.at[b], right)
        else:
            put(f"R{b}", work_n.at[i], work_s.at[i], right_n.at[b], right_s.at[b], left)
        yield
    cuts = (pl.ds(0, 32), pl.ds(32, 16))
    for b in (2, 1, 3, 0):
        took(f"L{b}")
        took(f"R{b}")
        i = place[(0, b)]
        store(
            fin_n.at[b],
            fin_s.at[b],
            [(work_n[i], work_s[i]), (left_n[b], left_s[b]), (right_n[b], right_s[b])],
        )
        if b == 2:
            for half, who in ((0, up), (1, down)):
                put(
                    f"t{half}",
                    fin_n.at[2, cuts[half]],
                    fin_s.at[2, cuts[half]],
                    two_n.at[0, cuts[half]],
                    two_s.at[0, cuts[half]],
                    who,
                )
        yield
    for half, b in ((0, 1), (1, 3)):
        took(f"t{half}")
        rows = cuts[half]
        store(
            fin_n.at[b, rows],
            fin_s.at[b, rows],
            [(fin_n[b, rows], fin_s[b, rows]), (two_n[0, rows], two_s[0, rows])],
        )
        if b == 1:
            put("l", fin_n.at[1], fin_s.at[1], two_n.at[1], two_s.at[1], up)
        else:
            put("r", fin_n.at[3], fin_s.at[3], two_n.at[2], two_s.at[2], down)
        yield
    took("l")
    took("r")
    n, top, total = combine(
        [(fin_n[0], fin_s[0]), (two_n[1], two_s[1]), (two_n[2], two_s[2])], spread()
    )
    lanes = lax.broadcasted_iota(jnp.int32, total.shape, 1)
    inverse = jnp.where(lanes < H, 1.0 / jnp.where(lanes < H, total, 1.0), 0.0)
    wide = jnp.dot(
        inverse,
        spread().astype(jnp.float32),
        preferred_element_type=jnp.float32,
        precision=lax.Precision.HIGHEST,
    )
    out[...] = (n * wide).astype(jnp.bfloat16)
    for event in REDUCE:
        sent[event].wait_send()


def reduce_and_gather(num, stats, spread, shards, collective_id):
    count = len(shards)

    def kernel(num_ref, stats_ref, spread_ref, *refs):
        ins = refs[:count]
        out = refs[count]
        outs = refs[count + 1 : 2 * count + 1]
        scratch = refs[2 * count + 1 :]
        spot = Spot()
        greet_plane(spot)
        ssem, rsem = scratch[:2]
        steps = [
            reduce_steps(
                spot,
                num_ref,
                stats_ref,
                out,
                lambda: spread_ref[...],
                scratch[5:],
                lambda e: ssem.at[e],
                lambda e: rsem.at[e],
            )
        ]
        run_all(steps + gather_all(spot, ins, outs, *scratch[2:5]))

    def block(n):
        return [
            pltpu.VMEM((n, TREE, WIDTH), jnp.bfloat16),
            pltpu.VMEM((n, TREE, 128), jnp.float32),
        ]

    return pl.pallas_call(
        kernel,
        out_shape=[jax.ShapeDtypeStruct((TREE, WIDTH), jnp.bfloat16)]
        + [jax.ShapeDtypeStruct((BLK,) + s.shape, s.dtype) for s in shards],
        in_specs=[VMEM, VMEM, VMEM] + [ANY] * count,
        out_specs=[VMEM] + [ANY] * count,
        scratch_shapes=[
            pltpu.SemaphoreType.DMA((len(REDUCE),)),
            pltpu.SemaphoreType.DMA((len(REDUCE),)),
        ]
        + gather_sems(count)
        + block(16)
        + block(16)
        + block(4)
        + block(4)
        + block(4)
        + block(4)
        + block(3),
        compiler_params=pltpu.CompilerParams(
            collective_id=collective_id,
            has_side_effects=True,
            vmem_limit_bytes=48 * 1024 * 1024,
        ),
        name="reduce_and_gather",
    )(num, stats, spread, *shards)


def greet_column(at):
    barrier = pltpu.get_barrier_semaphore()
    for d in (1, 2, 3):
        pl.semaphore_signal(
            barrier, inc=1, device_id={"req": (at + d) % 4}, device_id_type=MESH
        )
    pl.semaphore_wait(barrier, 3)


def column_kernel(exchange):
    def kernel(block, out, ssem, rsem, lsem):
        at = lax.axis_index("req")
        greet_column(at)
        copies = []
        for d in (2, 1, 3):
            to = (at + d) % 4
            copy = pltpu.make_async_remote_copy(
                src_ref=block.at[to] if exchange else block,
                dst_ref=out.at[at],
                send_sem=ssem.at[d - 1],
                recv_sem=rsem.at[d - 1],
                device_id={"req": to},
                device_id_type=MESH,
            )
            copy.start()
            copies.append(copy)
        local = pltpu.make_async_copy(block.at[at] if exchange else block, out.at[at], lsem)
        local.start()
        local.wait()
        for copy in copies:
            copy.wait()

    return kernel


def over_column(block, exchange, collective_id, name):
    shape = block.shape if exchange else (4,) + block.shape
    return pl.pallas_call(
        column_kernel(exchange),
        out_shape=jax.ShapeDtypeStruct(shape, block.dtype),
        in_specs=[VMEM],
        out_specs=VMEM,
        scratch_shapes=[
            pltpu.SemaphoreType.DMA((3,)),
            pltpu.SemaphoreType.DMA((3,)),
            pltpu.SemaphoreType.DMA,
        ],
        compiler_params=pltpu.CompilerParams(
            collective_id=collective_id, has_side_effects=True
        ),
        name=name,
    )(block)


def ancestors(parent_row):
    nodes = jnp.arange(TREE, dtype=jnp.int32)
    step = (parent_row[:, None] == nodes[None, :]).astype(jnp.float32)
    current = jnp.eye(TREE, dtype=jnp.float32)
    marks = current
    for _ in range(DEPTH - 1):
        current = jnp.dot(current, step)
        marks = jnp.maximum(marks, current)
    return marks


def on_device(
    tree_input,
    cache,
    page_table,
    lengths,
    parents,
    accept_leaf,
    w_qkv,
    w_out,
    w_up,
    w_down,
    w_draft,
    w_patch,
):
    myself = lax.axis_index("blk")
    width = WIDTH
    pool_pages = cache.shape[2] // PAGE
    patch = lax.all_gather(w_patch.T, "req", axis=0, tiled=True)
    normed = rms_rows(tree_input)
    (qkv,) = all_gather([w_qkv.T], 1, "gather_qkv")
    projected = dot_t(normed, qkv.reshape(3 * width, width)).astype(jnp.bfloat16)

    page_row = page_table[0]
    length_row = lengths[0]
    leaf_row = accept_leaf[0]
    requests = length_row.shape[0]
    total_pages = page_row.shape[0]
    npages = (length_row + DEPTH + PAGE - 1) // PAGE
    before = jnp.arange(requests)[:, None] >= jnp.arange(requests)[None, :]
    page_ends = jnp.sum(jnp.where(before, npages[None, :], 0), axis=1)
    offsets = page_ends - npages
    local_ids = myself * pool_pages + jnp.arange(pool_pages, dtype=jnp.int32)
    located = page_row[None, :] == local_ids[:, None]
    where_at = jnp.sum(
        jnp.where(located, jnp.arange(total_pages, dtype=jnp.int32)[None, :], 0), axis=1
    )
    owner = jnp.sum((page_ends[None, :] <= where_at[:, None]).astype(jnp.int32), axis=1)
    owner_hot = owner[:, None] == jnp.arange(requests, dtype=jnp.int32)[None, :]
    safe_owner = jnp.minimum(owner, requests - 1)
    level_marks = jnp.asarray(LEVEL_START[1:-1], jnp.int32)
    accepted = 1 + jnp.sum((leaf_row[:, None] >= level_marks[None, :]).astype(jnp.int32), axis=1)

    def of_owner(row):
        return jnp.sum(jnp.where(owner_hot, row[None, :], 0), axis=1)

    def with_tree(row, last):
        return jnp.concatenate([row, jnp.reshape(jnp.asarray(last, jnp.int32), (1,))])

    owners = with_tree(safe_owner, myself)
    tables = jnp.stack(
        [
            owners % 2 * 16 + owners // 2,
            with_tree((where_at - of_owner(offsets)) * PAGE, 0),
            with_tree(of_owner(length_row), 0),
            with_tree(of_owner(accepted), 0),
            owners,
        ]
    )
    marks = ancestors(parents[0])
    my_leaf = jnp.sum(jnp.where(jnp.arange(requests) == myself, leaf_row, 0))
    nodes = jnp.arange(TREE, dtype=jnp.int32)
    chosen = jnp.sum(jnp.where(nodes[:, None] == my_leaf, marks, 0.0), axis=0)
    ranks = jnp.sum(jnp.where(nodes[:, None] <= nodes[None, :], chosen[:, None], 0.0), axis=0) - 1
    picker = jnp.where(
        (chosen[None, :] > 0.5) & (ranks[None, :] == jnp.arange(8, dtype=jnp.float32)[:, None]),
        1.0,
        0.0,
    ).astype(jnp.bfloat16)
    send_rows = jnp.dot(
        picker, projected[:, width:], preferred_element_type=jnp.float32
    ).astype(jnp.bfloat16)
    (gathered,) = all_gather(
        [jnp.concatenate([projected[:, :width], send_rows[:, :width], send_rows[:, width:]])],
        2,
        "gather_query",
    )
    num, stats, cache_new = attend(tables, gathered, cache, projected, marks)
    spread = (
        jnp.arange(128, dtype=jnp.int32)[:, None]
        == jnp.arange(width, dtype=jnp.int32)[None, :] // HD
    ).astype(jnp.bfloat16)
    draft_mine = lax.dynamic_index_in_dim(
        w_draft.transpose(0, 2, 1), lax.axis_index("req"), 0, keepdims=False
    )
    attended, full_out, full_up, full_down, full_draft = reduce_and_gather(
        num, stats, spread, [w_out.T, w_up.T, w_down, draft_mine], 3
    )
    full_out, full_up, full_down, full_draft = (
        w.reshape(width, width) for w in (full_out, full_up, full_down, full_draft)
    )
    proj = dot_t(attended, full_out).astype(jnp.bfloat16)
    mid = (tree_input.astype(jnp.float32) + proj.astype(jnp.float32)).astype(jnp.bfloat16)
    hidden = jax.nn.gelu(dot_t(rms_rows(mid), full_up)).astype(jnp.bfloat16)
    feedforward = jnp.dot(hidden, full_down, preferred_element_type=jnp.float32)
    layer_out = (mid.astype(jnp.float32) + feedforward).astype(jnp.bfloat16)
    rows = over_column(layer_out, False, 4, "gather_rows").reshape(4 * TREE, width)
    branch = jax.nn.silu(dot_t(rms_rows(rows), full_draft)).astype(jnp.bfloat16)
    drafted = (rows.astype(jnp.float32) + branch.astype(jnp.float32)).astype(jnp.bfloat16)
    head = dot_t(drafted, patch).astype(jnp.bfloat16)
    drafts = over_column(head.reshape(4, TREE, width), True, 5, "return_rows")
    return (layer_out, drafts, cache_new)


def solution(mesh):
    in_specs = (
        P(("req", "blk"), None),
        P("req", None, "blk", None),
        P("req", None),
        P("req", None),
        P(("req", "blk"), None),
        P("req", None),
        P(None, "blk"),
        P(None, "blk"),
        P(None, "blk"),
        P("blk", None),
        P(None, None, "blk"),
        P(None, "req"),
    )
    out_specs = (
        P(("req", "blk"), None),
        P(None, ("req", "blk"), None),
        P("req", None, "blk", None),
    )
    return jax.shard_map(
        on_device, mesh=mesh, in_specs=in_specs, out_specs=out_specs, check_vma=False
    )
```

```python
import math

import jax
import jax.numpy as jnp
from jax import lax
from jax.experimental import pallas as pl
from jax.experimental.pallas import tpu as pltpu
from jax.sharding import PartitionSpec as P

H = 16
HD = 80
TREE = 48
DEPTH = 5
PAGE = 128
BLK = 32
WIDTH = H * HD

EPS = 1e-06
LOWEST = -8388608.0
LEVEL_START = (0, 1, 5, 15, 30, 48)
MESH = pl.DeviceIdType.MESH
ROWSLOT = ((0, 0), (-1, 0), (1, 0), (2, 0))


def rms_rows(values):
    wide = values.astype(jnp.float32)
    return (wide * lax.rsqrt(jnp.mean(wide * wide, axis=-1, keepdims=True) + EPS)).astype(
        jnp.bfloat16
    )


def dot_t(left, right):
    return lax.dot_general(
        left, right, (((1,), (1,)), ((), ())), preferred_element_type=jnp.float32
    )


class Spot:
    def __init__(self):
        self.me = lax.axis_index("blk")
        self.core = self.me % 2
        x = (self.me // 2) % 4
        y = self.me // 8
        self.one = x + self.core * (y - x)
        self.two = y + self.core * (x - y)
        self.sibling = self.me + 1 - 2 * self.core

    def at(self, a, b):
        return self.core + 2 * self.chip(a, b)

    def chip(self, a, b):
        one = (self.one + a + 4) % 4
        two = (self.two + b + 4) % 4
        return (1 + 3 * self.core) * one + (4 - 3 * self.core) * two


def greet_plane(spot, column=False):
    barrier = pltpu.get_barrier_semaphore()
    for who in (spot.at(1, 0), spot.at(-1, 0), spot.at(0, 1), spot.at(0, -1), spot.sibling):
        pl.semaphore_signal(barrier, inc=1, device_id={"blk": who}, device_id_type=MESH)
    if column:
        at = lax.axis_index("req")
        for d in (1, 2, 3):
            pl.semaphore_signal(
                barrier, inc=1, device_id={"req": (at + d) % 4}, device_id_type=MESH
            )
    pl.semaphore_wait(barrier, 8 if column else 5)


def numbered(names):
    return {name: i for i, name in enumerate(names)}


GATHER = numbered(
    ["L", "R", "OA", "OB"]
    + [f"{kind}{k}" for k in range(4) for kind in ("D", "U", "PA", "PB")]
    + [f"S{k}" for k in range(16)]
)


def sender(sent, ssem, rsem, events):
    def put(event, src, dst, who):
        copy = pltpu.make_async_remote_copy(
            src_ref=src,
            dst_ref=dst,
            send_sem=ssem(events[event]),
            recv_sem=rsem(events[event]),
            device_id={"blk": who},
            device_id_type=MESH,
        )
        copy.start()
        sent[event] = copy

    return put


def gather_steps(spot, shard, view, ssem, rsem, lsem, cut):
    sent = {}
    send = sender(sent, ssem, rsem, GATHER)

    def put(event, src, slot, who, half=None):
        dst = view(slot)
        if half is not None:
            src, dst = cut(src, half), cut(dst, half)
        send(event, src, dst, who)

    right, left = spot.at(1, 0), spot.at(-1, 0)
    up, down = spot.at(0, 1), spot.at(0, -1)
    local = pltpu.make_async_copy(shard, view(spot.me), lsem)
    local.start()
    put("L", shard, spot.me, right)
    put("R", shard, spot.me, left)
    put("D0", shard, spot.me, up)
    put("U0", shard, spot.me, down)
    put("S0", shard, spot.me, spot.sibling)
    yield
    for k, event in ((1, "L"), (2, "R")):
        slot = spot.at(*ROWSLOT[k])
        sent[event].wait_recv()
        if k == 1:
            put("OA", view(slot), slot, right, 0)
        else:
            put("OB", view(slot), slot, left, 1)
        put(f"D{k}", view(slot), slot, up)
        put(f"U{k}", view(slot), slot, down)
        put(f"S{k}", view(slot), slot, spot.sibling)
        yield

    def column(k):
        a = ROWSLOT[k][0]
        slot = spot.at(a, -1)
        sent[f"D{k}"].wait_recv()
        put(f"PA{k}", view(slot), slot, up, 0)
        put(f"S{4 + k}", view(slot), slot, spot.sibling)
        slot = spot.at(a, 1)
        sent[f"U{k}"].wait_recv()
        put(f"PB{k}", view(slot), slot, down, 1)
        put(f"S{8 + k}", view(slot), slot, spot.sibling)

    column(0)
    yield
    sent["OA"].wait_recv()
    sent["OB"].wait_recv()
    slot = spot.at(2, 0)
    put("D3", view(slot), slot, up)
    put("U3", view(slot), slot, down)
    put("S3", view(slot), slot, spot.sibling)
    yield
    for k in (1, 2, 3):
        column(k)
        yield
    for k in range(4):
        slot = spot.at(ROWSLOT[k][0], 2)
        sent[f"PA{k}"].wait_recv()
        sent[f"PB{k}"].wait_recv()
        put(f"S{12 + k}", view(slot), slot, spot.sibling)
        yield
    for k in range(16):
        sent[f"S{k}"].wait_recv()
    local.wait()
    for event in GATHER:
        sent[event].wait_send()


def run_all(steps):
    steps = list(steps)
    while steps:
        alive = []
        for step in steps:
            try:
                next(step)
                alive.append(step)
            except StopIteration:
                pass
        steps = alive


def row_halves(rows):
    first = ((rows // 2) + 7) // 8 * 8

    def cut(ref, half):
        return ref.at[pl.ds(0, first)] if half == 0 else ref.at[pl.ds(first, rows - first)]

    return cut


def gather_all(spot, ins, outs, ssem, rsem, lsem):
    count = len(GATHER)
    return [
        gather_steps(
            spot,
            ins[i],
            lambda slot, i=i: outs[i].at[slot],
            lambda e, i=i: ssem.at[i * count + e],
            lambda e, i=i: rsem.at[i * count + e],
            lsem.at[i],
            row_halves(ins[i].shape[0]),
        )
        for i in range(len(ins))
    ]


def gather_sems(arrays):
    return [
        pltpu.SemaphoreType.DMA((arrays * len(GATHER),)),
        pltpu.SemaphoreType.DMA((arrays * len(GATHER),)),
        pltpu.SemaphoreType.DMA((arrays,)),
    ]


def column_steps(spot, shard, out, ssem, rsem, lsem):
    at = lax.axis_index("req")
    half = shard.shape[0] // 2
    rows = pl.ds(pl.multiple_of(spot.core * half, 8), half)
    local = pltpu.make_async_copy(shard, out.at[at], lsem)
    local.start()
    copies = []
    for i, d in enumerate((2, 1, 3)):
        copy = pltpu.make_async_remote_copy(
            src_ref=shard.at[rows],
            dst_ref=out.at[at, rows],
            send_sem=ssem.at[i],
            recv_sem=rsem.at[i],
            device_id={"req": (at + d) % 4},
            device_id_type=MESH,
        )
        copy.start()
        copies.append(copy)
    for _ in range(3):
        yield
    for i, d in ((1, 1), (2, 3), (0, 2)):
        copies[i].wait_recv()
        slot = (at - d + 4) % 4
        copy = pltpu.make_async_remote_copy(
            src_ref=out.at[slot, rows],
            dst_ref=out.at[slot, rows],
            send_sem=ssem.at[3 + i],
            recv_sem=rsem.at[3 + i],
            device_id={"blk": spot.sibling},
            device_id_type=MESH,
        )
        copy.start()
        copies.append(copy)
        yield
    local.wait()
    for copy in copies[3:]:
        copy.wait_recv()
    for copy in copies:
        copy.wait_send()


ANY = pl.BlockSpec(memory_space=pl.ANY)
VMEM = pl.BlockSpec(memory_space=pltpu.VMEM)


def all_gather(shards, column, collective_id, name):
    count = len(shards)
    both = shards + column

    def kernel(*refs):
        ins = refs[: len(both)]
        outs = refs[len(both) : 2 * len(both)]
        scratch = refs[2 * len(both) :]
        spot = Spot()
        greet_plane(spot, bool(column))
        steps = gather_all(spot, ins[:count], outs[:count], *scratch[:3])
        if column:
            steps.append(column_steps(spot, ins[count], outs[count], *scratch[3:]))
        run_all(steps)

    return pl.pallas_call(
        kernel,
        out_shape=[jax.ShapeDtypeStruct((BLK,) + s.shape, s.dtype) for s in shards]
        + [jax.ShapeDtypeStruct((4,) + s.shape, s.dtype) for s in column],
        in_specs=[ANY] * len(both),
        out_specs=[ANY] * len(both),
        scratch_shapes=gather_sems(count)
        + [
            pltpu.SemaphoreType.DMA((6,)),
            pltpu.SemaphoreType.DMA((6,)),
            pltpu.SemaphoreType.DMA,
        ][: 3 * len(column)],
        compiler_params=pltpu.CompilerParams(collective_id=collective_id, has_side_effects=True),
        name=name,
    )(*both)


def window(w):
    return 128 * (5 * (w // 4) + w % 4), 32 * (w % 4)


def attend_kernel(
    tables, query_ref, cache_ref, proj_ref, marks_ref, num_ref, stats_ref, new_ref,
    masked, scores, weights, tops, dens, scales, acc,
):
    step = pl.program_id(0)
    slot = tables[0, step]
    start = tables[1, step]
    length = tables[2, step]
    count = tables[3, step]
    fresh = tables[6, step] > 0
    final = tables[7, step] > 0
    tree = tables[8, step] > 0
    factor = math.log2(math.e) / math.sqrt(HD)
    lanes = lax.broadcasted_iota(jnp.int32, (TREE, 128), 1)
    columns = lax.broadcasted_iota(jnp.int32, (TREE, 256), 1)
    pair = 2 * TREE

    def inside(w, i):
        begin = window(w)[1] + HD * i
        return (columns >= begin) & (columns < begin + HD)

    @pl.when(step == 0)
    def _():
        @pl.loop(0, BLK)
        def _(r):
            num_ref[r] = jnp.zeros(num_ref.shape[1:], num_ref.dtype)
            stats_ref[r] = jnp.where(lanes < 64, LOWEST, 0.0)

    @pl.when(fresh)
    def _():
        tops[...] = jnp.full_like(tops, LOWEST)
        dens[...] = jnp.zeros_like(dens)
        acc[...] = jnp.zeros_like(acc)
        for w in range(8):
            picked = query_ref[0, pl.ds(0, TREE), pl.ds(window(w)[0], 256)]
            for i in range(2):
                one = inside(w, i).astype(jnp.float32).astype(jnp.bfloat16)
                masked[w, pl.ds(TREE * i, TREE)] = picked * one

    def merge(key_at, value_at, seen, keys):
        for w in range(8):
            scores[pl.ds(pair * w, pair), pl.ds(0, keys)] = dot_t(
                masked[w], key_at(window(w)[0])
            )
        for part in range(4):
            rows = pl.ds(2 * pair * part, 2 * pair)
            shown = jnp.concatenate([seen] * 4, axis=0) if seen.shape[0] > 1 else seen
            part_scores = jnp.where(shown, scores[rows, pl.ds(0, keys)] * factor, LOWEST)
            before = tops[rows, :]
            top = jnp.maximum(
                before, jnp.ceil(jnp.max(part_scores, axis=1, keepdims=True))
            )
            weight = jnp.where(shown, jnp.exp2(part_scores - top[:, :keys]), 0.0)
            scale = jnp.exp2(before - top)
            tops[rows, :] = top
            scales[rows, :] = scale
            dens[rows, :] = dens[rows, :] * scale + jnp.sum(weight, axis=1, keepdims=True)
            weights[rows, pl.ds(0, keys)] = weight.astype(jnp.bfloat16)
        for w in range(8):
            rows = pl.ds(pair * w, pair)
            added = jnp.dot(
                weights[rows, pl.ds(0, keys)],
                value_at(window(w)[0]),
                preferred_element_type=jnp.float32,
            )
            scale = scales[rows, :]
            acc[w] = acc[w] * jnp.concatenate([scale, scale], axis=1) + added

    @pl.when(jnp.logical_not(tree))
    def _():
        seen = lax.broadcasted_iota(jnp.int32, (1, PAGE), 1) + start < length
        merge(
            lambda first: cache_ref[0, 0, :, pl.ds(first, 256)],
            lambda first: cache_ref[0, 1, :, pl.ds(first, 256)],
            seen,
            PAGE,
        )
        row0 = length - start
        touched = (row0 < PAGE) & (row0 + count > 0)

        @pl.when(jnp.logical_not(touched))
        def _():
            new_ref[...] = cache_ref[...]

        @pl.when(touched)
        def _():
            ahead = lax.broadcasted_iota(jnp.int32, (PAGE, 8), 0) - row0
            nth = lax.broadcasted_iota(jnp.int32, (PAGE, 8), 1)
            hot = ((ahead == nth) & (nth < count)).astype(jnp.float32).astype(jnp.bfloat16)
            rows = lax.broadcasted_iota(jnp.int32, (PAGE, WIDTH), 0) - row0
            hit = (rows >= 0) & (rows < count)
            for i in range(2):
                taken = jnp.dot(
                    hot,
                    query_ref[0, pl.ds(TREE + 8 * i, 8), :],
                    preferred_element_type=jnp.float32,
                )
                kept = cache_ref[0, i].astype(jnp.float32)
                new_ref[0, i] = jnp.where(hit, taken, kept).astype(jnp.bfloat16)

    @pl.when(tree)
    def _():
        merge(
            lambda first: proj_ref[:, pl.ds(WIDTH + first, 256)],
            lambda first: proj_ref[:, pl.ds(2 * WIDTH + first, 256)],
            marks_ref[...] > 0.5,
            TREE,
        )

    @pl.when(final)
    def _():
        carried = None
        for w in range(8):
            picked = jnp.where(
                inside(w, 0),
                acc[w, pl.ds(0, TREE), :],
                jnp.where(inside(w, 1), acc[w, pl.ds(TREE, TREE), :], 0.0),
            )
            head = picked[:, :128]
            if w % 4:
                head = head + carried
            carried = picked[:, 128:]
            num_ref[slot, :, pl.ds(window(w)[0], 128)] = head.astype(jnp.bfloat16)
            if w % 4 == 3:
                num_ref[slot, :, pl.ds(window(w)[0] + 128, 128)] = carried.astype(jnp.bfloat16)
        stats = jnp.full((TREE, 128), LOWEST, jnp.float32)
        for head in range(H):
            rows = pl.ds(TREE * head, TREE)
            stats = jnp.where(lanes == head, tops[rows, :], stats)
            stats = jnp.where(lanes == 64 + head, dens[rows, :], stats)
        stats_ref[slot] = stats


def attend(tables, gathered, cache, projected, marks):
    steps = tables.shape[1]
    rows = gathered.shape[1]
    page_block = pl.BlockSpec((1, 2, PAGE, WIDTH), lambda p, t: (0, 0, t[5, p], 0))
    whole3 = lambda p, t: (0, 0, 0)
    lines = 2 * TREE * 8
    return pl.pallas_call(
        attend_kernel,
        out_shape=[
            jax.ShapeDtypeStruct((BLK, TREE, WIDTH), jnp.bfloat16),
            jax.ShapeDtypeStruct((BLK, TREE, 128), jnp.float32),
            jax.ShapeDtypeStruct(cache.shape, cache.dtype),
        ],
        grid_spec=pltpu.PrefetchScalarGridSpec(
            num_scalar_prefetch=1,
            grid=(steps,),
            in_specs=[
                pl.BlockSpec((1, rows, WIDTH), lambda p, t: (t[4, p], 0, 0)),
                page_block,
                pl.BlockSpec((TREE, 3 * WIDTH), lambda p, t: (0, 0)),
                pl.BlockSpec((TREE, TREE), lambda p, t: (0, 0)),
            ],
            out_specs=[
                pl.BlockSpec((BLK, TREE, WIDTH), whole3),
                pl.BlockSpec((BLK, TREE, 128), whole3),
                page_block,
            ],
            scratch_shapes=[
                pltpu.VMEM((8, 2 * TREE, 256), jnp.bfloat16),
                pltpu.VMEM((lines, 128), jnp.float32),
                pltpu.VMEM((lines, 128), jnp.bfloat16),
                pltpu.VMEM((lines, 128), jnp.float32),
                pltpu.VMEM((lines, 128), jnp.float32),
                pltpu.VMEM((lines, 128), jnp.float32),
                pltpu.VMEM((8, 2 * TREE, 256), jnp.float32),
            ],
        ),
        compiler_params=pltpu.CompilerParams(vmem_limit_bytes=48 * 1024 * 1024),
        name="attend",
    )(tables, gathered, cache, projected, marks)


PAIR_ORDER = (
    [(2, b) for b in range(4)]
    + [(1, 2), (1, 3), (-1, 0), (-1, 1)]
    + [(1, 0), (1, 1), (-1, 2), (-1, 3)]
    + [(0, b) for b in range(4)]
)
REDUCE = numbered(
    [f"{kind}{i}{s}" for kind, n in (("P", 16), ("T", 4), ("L", 4), ("R", 4)) for i in range(n) for s in "ns"]
    + [f"{kind}{s}" for kind in ("t0", "t1", "l", "r") for s in "ns"]
)


def split_stats(stats):
    return stats, pltpu.roll(stats, 64, 1)


def combine(parts, spread):
    stats = [split_stats(s) for _, s in parts]
    lanes = lax.broadcasted_iota(jnp.int32, stats[0][0].shape, 1)
    top = stats[0][0]
    for s, _ in stats[1:]:
        top = jnp.maximum(top, s)
    total = None
    num = None
    for (n, _), (s, d) in zip(parts, stats):
        scale = jnp.where(lanes < H, jnp.exp2(jnp.minimum(s - top, 0.0)), 0.0)
        wide = jnp.dot(scale.astype(jnp.bfloat16), spread, preferred_element_type=jnp.float32)
        d = d * scale
        n = n.astype(jnp.float32) * wide
        total = d if total is None else total + d
        num = n if num is None else num + n
    return num, top, total


def join_stats(top, total):
    lanes = lax.broadcasted_iota(jnp.int32, top.shape, 1)
    return jnp.where(lanes < H, top, pltpu.roll(jnp.where(lanes < H, total, 0.0), 64, 1))


def reduce_steps(spot, num, stats, out, spread, bufs, ssem, rsem):
    pair_n, pair_s, work_n, work_s, thru_n, thru_s, left_n, left_s, right_n, right_s = bufs[:10]
    fin_n, fin_s, two_n, two_s = bufs[10:]
    sent = {}
    send = sender(sent, ssem, rsem, REDUCE)

    def put(event, src_n, src_s, dst_n, dst_s, who):
        send(event + "n", src_n, dst_n, who)
        send(event + "s", src_s, dst_s, who)

    def took(event):
        sent[event + "n"].wait_recv()
        sent[event + "s"].wait_recv()

    right, left = spot.at(1, 0), spot.at(-1, 0)
    up, down = spot.at(0, 1), spot.at(0, -1)
    other = (1 - spot.core) * 16
    mine = spot.core * 16
    for i, (a, b) in enumerate(PAIR_ORDER):
        c = other + spot.chip(b, a)
        put(f"P{i}", num.at[c], stats.at[c], pair_n.at[i], pair_s.at[i], spot.sibling)
    yield

    def store(dst_n, dst_s, parts):
        n, top, total = combine(parts, spread())
        dst_n[...] = n.astype(jnp.bfloat16)
        dst_s[...] = join_stats(top, total)

    place = {pair: i for i, pair in enumerate(PAIR_ORDER)}
    for i, (a, b) in enumerate(PAIR_ORDER):
        took(f"P{i}")
        c = mine + spot.chip(a, b)
        store(
            work_n.at[i], work_s.at[i], [(num[c], stats[c]), (pair_n[i], pair_s[i])]
        )
        if a == 2:
            put(
                f"T{b}", work_n.at[i], work_s.at[i], thru_n.at[b], thru_s.at[b],
                right if b < 2 else left,
            )
        elif (a == 1 and b >= 2):
            put(f"L{b}", work_n.at[i], work_s.at[i], left_n.at[b], left_s.at[b], right)
        elif (a == -1 and b < 2):
            put(f"R{b}", work_n.at[i], work_s.at[i], right_n.at[b], right_s.at[b], left)
        yield
    for b in range(4):
        took(f"T{b}")
        a = 1 if b < 2 else -1
        i = place[(a, b)]
        store(
            work_n.at[i], work_s.at[i], [(work_n[i], work_s[i]), (thru_n[b], thru_s[b])]
        )
        if a == 1:
            put(f"L{b}", work_n.at[i], work_s.at[i], left_n.at[b], left_s.at[b], right)
        else:
            put(f"R{b}", work_n.at[i], work_s.at[i], right_n.at[b], right_s.at[b], left)
        yield
    cuts = (pl.ds(0, 32), pl.ds(32, 16))
    for b in (2, 1, 3, 0):
        took(f"L{b}")
        took(f"R{b}")
        i = place[(0, b)]
        store(
            fin_n.at[b],
            fin_s.at[b],
            [(work_n[i], work_s[i]), (left_n[b], left_s[b]), (right_n[b], right_s[b])],
        )
        if b == 2:
            for half, who in ((0, up), (1, down)):
                put(
                    f"t{half}",
                    fin_n.at[2, cuts[half]],
                    fin_s.at[2, cuts[half]],
                    two_n.at[0, cuts[half]],
                    two_s.at[0, cuts[half]],
                    who,
                )
        yield
    for half, b in ((0, 1), (1, 3)):
        took(f"t{half}")
        rows = cuts[half]
        store(
            fin_n.at[b, rows],
            fin_s.at[b, rows],
            [(fin_n[b, rows], fin_s[b, rows]), (two_n[0, rows], two_s[0, rows])],
        )
        if b == 1:
            put("l", fin_n.at[1], fin_s.at[1], two_n.at[1], two_s.at[1], up)
        else:
            put("r", fin_n.at[3], fin_s.at[3], two_n.at[2], two_s.at[2], down)
        yield
    took("l")
    took("r")
    n, top, total = combine(
        [(fin_n[0], fin_s[0]), (two_n[1], two_s[1]), (two_n[2], two_s[2])], spread()
    )
    lanes = lax.broadcasted_iota(jnp.int32, total.shape, 1)
    inverse = jnp.where(lanes < H, 1.0 / jnp.where(lanes < H, total, 1.0), 0.0)
    wide = jnp.dot(
        inverse,
        spread().astype(jnp.float32),
        preferred_element_type=jnp.float32,
        precision=lax.Precision.HIGHEST,
    )
    out[...] = (n * wide).astype(jnp.bfloat16)
    for event in REDUCE:
        sent[event].wait_send()


def reduce_and_gather(num, stats, spread, shards, collective_id):
    count = len(shards)

    def kernel(num_ref, stats_ref, spread_ref, *refs):
        ins = refs[:count]
        out = refs[count]
        outs = refs[count + 1 : 2 * count + 1]
        scratch = refs[2 * count + 1 :]
        spot = Spot()
        greet_plane(spot)
        ssem, rsem = scratch[:2]
        steps = [
            reduce_steps(
                spot,
                num_ref,
                stats_ref,
                out,
                lambda: spread_ref[...],
                scratch[5:],
                lambda e: ssem.at[e],
                lambda e: rsem.at[e],
            )
        ]
        run_all(steps + gather_all(spot, ins, outs, *scratch[2:5]))

    def block(n):
        return [
            pltpu.VMEM((n, TREE, WIDTH), jnp.bfloat16),
            pltpu.VMEM((n, TREE, 128), jnp.float32),
        ]

    return pl.pallas_call(
        kernel,
        out_shape=[jax.ShapeDtypeStruct((TREE, WIDTH), jnp.bfloat16)]
        + [jax.ShapeDtypeStruct((BLK,) + s.shape, s.dtype) for s in shards],
        in_specs=[VMEM, VMEM, VMEM] + [ANY] * count,
        out_specs=[VMEM] + [ANY] * count,
        scratch_shapes=[
            pltpu.SemaphoreType.DMA((len(REDUCE),)),
            pltpu.SemaphoreType.DMA((len(REDUCE),)),
        ]
        + (gather_sems(count) if count else [pltpu.SemaphoreType.DMA] * 3)
        + block(16)
        + block(16)
        + block(4)
        + block(4)
        + block(4)
        + block(4)
        + block(3),
        compiler_params=pltpu.CompilerParams(
            collective_id=collective_id,
            has_side_effects=True,
            vmem_limit_bytes=48 * 1024 * 1024,
        ),
        name="reduce_and_gather",
    )(num, stats, spread, *shards)


def greet_column(at):
    barrier = pltpu.get_barrier_semaphore()
    for d in (1, 2, 3):
        pl.semaphore_signal(
            barrier, inc=1, device_id={"req": (at + d) % 4}, device_id_type=MESH
        )
    pl.semaphore_wait(barrier, 3)


def column_kernel(exchange):
    def kernel(block, out, ssem, rsem, lsem):
        at = lax.axis_index("req")
        greet_column(at)
        copies = []
        for d in (2, 1, 3):
            to = (at + d) % 4
            copy = pltpu.make_async_remote_copy(
                src_ref=block.at[to] if exchange else block,
                dst_ref=out.at[at],
                send_sem=ssem.at[d - 1],
                recv_sem=rsem.at[d - 1],
                device_id={"req": to},
                device_id_type=MESH,
            )
            copy.start()
            copies.append(copy)
        local = pltpu.make_async_copy(block.at[at] if exchange else block, out.at[at], lsem)
        local.start()
        local.wait()
        for copy in copies:
            copy.wait()

    return kernel


def over_column(block, exchange, collective_id, name):
    shape = block.shape if exchange else (4,) + block.shape
    return pl.pallas_call(
        column_kernel(exchange),
        out_shape=jax.ShapeDtypeStruct(shape, block.dtype),
        in_specs=[VMEM],
        out_specs=VMEM,
        scratch_shapes=[
            pltpu.SemaphoreType.DMA((3,)),
            pltpu.SemaphoreType.DMA((3,)),
            pltpu.SemaphoreType.DMA,
        ],
        compiler_params=pltpu.CompilerParams(
            collective_id=collective_id, has_side_effects=True
        ),
        name=name,
    )(block)


def ancestors(parent_row):
    nodes = jnp.arange(TREE, dtype=jnp.int32)
    step = (parent_row[:, None] == nodes[None, :]).astype(jnp.float32)
    current = jnp.eye(TREE, dtype=jnp.float32)
    marks = current
    for _ in range(DEPTH - 1):
        current = jnp.dot(current, step)
        marks = jnp.maximum(marks, current)
    return marks


def on_device(
    tree_input,
    cache,
    page_table,
    lengths,
    parents,
    accept_leaf,
    w_qkv,
    w_out,
    w_up,
    w_down,
    w_draft,
    w_patch,
):
    myself = lax.axis_index("blk")
    width = WIDTH
    pool_pages = cache.shape[2] // PAGE
    normed = rms_rows(tree_input)
    draft_mine = lax.dynamic_index_in_dim(
        w_draft.transpose(0, 2, 1), lax.axis_index("req"), 0, keepdims=False
    )
    qkv, full_out, full_up, full_down, full_draft, patch = all_gather(
        [w_qkv.T, w_out.T, w_up.T, w_down, draft_mine], [w_patch.T], 1, "gather_weights"
    )
    full_out, full_up, full_down, full_draft, patch = (
        w.reshape(width, width) for w in (full_out, full_up, full_down, full_draft, patch)
    )
    projected = dot_t(normed, qkv.reshape(3 * width, width)).astype(jnp.bfloat16)

    page_row = page_table[0]
    length_row = lengths[0]
    leaf_row = accept_leaf[0]
    requests = length_row.shape[0]
    total_pages = page_row.shape[0]
    npages = (length_row + DEPTH + PAGE - 1) // PAGE
    before = jnp.arange(requests)[:, None] >= jnp.arange(requests)[None, :]
    page_ends = jnp.sum(jnp.where(before, npages[None, :], 0), axis=1)
    offsets = page_ends - npages
    local_ids = myself * pool_pages + jnp.arange(pool_pages, dtype=jnp.int32)
    located = page_row[None, :] == local_ids[:, None]
    where_at = jnp.sum(
        jnp.where(located, jnp.arange(total_pages, dtype=jnp.int32)[None, :], 0), axis=1
    )
    owner = jnp.sum((page_ends[None, :] <= where_at[:, None]).astype(jnp.int32), axis=1)
    owner_hot = owner[:, None] == jnp.arange(requests, dtype=jnp.int32)[None, :]
    safe_owner = jnp.minimum(owner, requests - 1)
    level_marks = jnp.asarray(LEVEL_START[1:-1], jnp.int32)
    accepted = 1 + jnp.sum((leaf_row[:, None] >= level_marks[None, :]).astype(jnp.int32), axis=1)

    def of_owner(row):
        return jnp.sum(jnp.where(owner_hot, row[None, :], 0), axis=1)

    my_end = jnp.sum(jnp.where(jnp.arange(requests) == myself, page_ends, 0))

    def with_tree(row, last):
        return jnp.concatenate([row, jnp.reshape(jnp.asarray(last, jnp.int32), (1,))])

    spots = with_tree(2 * where_at, 2 * my_end - 1)
    rank = jnp.sum((spots[None, :] < spots[:, None]).astype(jnp.int32), axis=1)
    sorted_hot = rank[None, :] == jnp.arange(pool_pages + 1, dtype=jnp.int32)[:, None]
    owners = with_tree(safe_owner, myself)
    page_ids = with_tree(jnp.arange(pool_pages, dtype=jnp.int32), -1)
    unsorted = jnp.stack(
        [
            owners % 2 * 16 + owners // 2,
            with_tree((where_at - of_owner(offsets)) * PAGE, 0),
            with_tree(of_owner(length_row), 0),
            with_tree(of_owner(accepted), 0),
            owners,
            page_ids,
        ]
    )
    table = jnp.sum(jnp.where(sorted_hot[None], unsorted[:, None, :], 0), axis=2)
    owners, page_ids = table[4], table[5]
    changes = (owners[1:] != owners[:-1]).astype(jnp.int32)
    one = jnp.ones((1,), jnp.int32)
    beside = jnp.concatenate([page_ids[1:2], page_ids[:-1]])
    tables = jnp.concatenate(
        [
            table[:5],
            jnp.where(page_ids < 0, beside, page_ids)[None],
            jnp.concatenate([one, changes])[None],
            jnp.concatenate([changes, one])[None],
            (page_ids < 0).astype(jnp.int32)[None],
        ]
    )
    marks = ancestors(parents[0])
    my_leaf = jnp.sum(jnp.where(jnp.arange(requests) == myself, leaf_row, 0))
    nodes = jnp.arange(TREE, dtype=jnp.int32)
    chosen = jnp.sum(jnp.where(nodes[:, None] == my_leaf, marks, 0.0), axis=0)
    ranks = jnp.sum(jnp.where(nodes[:, None] <= nodes[None, :], chosen[:, None], 0.0), axis=0) - 1
    picker = jnp.where(
        (chosen[None, :] > 0.5) & (ranks[None, :] == jnp.arange(8, dtype=jnp.float32)[:, None]),
        1.0,
        0.0,
    ).astype(jnp.bfloat16)
    send_rows = jnp.dot(
        picker, projected[:, width:], preferred_element_type=jnp.float32
    ).astype(jnp.bfloat16)
    (gathered,) = all_gather(
        [jnp.concatenate([projected[:, :width], send_rows[:, :width], send_rows[:, width:]])],
        [],
        2,
        "gather_query",
    )
    num, stats, cache_new = attend(tables, gathered, cache, projected, marks)
    spread = (
        jnp.arange(128, dtype=jnp.int32)[:, None]
        == jnp.arange(width, dtype=jnp.int32)[None, :] // HD
    ).astype(jnp.bfloat16)
    (attended,) = reduce_and_gather(num, stats, spread, [], 3)
    proj = dot_t(attended, full_out).astype(jnp.bfloat16)
    mid = (tree_input.astype(jnp.float32) + proj.astype(jnp.float32)).astype(jnp.bfloat16)
    hidden = jax.nn.gelu(dot_t(rms_rows(mid), full_up)).astype(jnp.bfloat16)
    feedforward = jnp.dot(hidden, full_down, preferred_element_type=jnp.float32)
    layer_out = (mid.astype(jnp.float32) + feedforward).astype(jnp.bfloat16)
    rows = over_column(layer_out, False, 4, "gather_rows").reshape(4 * TREE, width)
    branch = jax.nn.silu(dot_t(rms_rows(rows), full_draft)).astype(jnp.bfloat16)
    drafted = (rows.astype(jnp.float32) + branch.astype(jnp.float32)).astype(jnp.bfloat16)
    head = dot_t(drafted, patch).astype(jnp.bfloat16)
    drafts = over_column(head.reshape(4, TREE, width), True, 5, "return_rows")
    return (layer_out, drafts, cache_new)


def solution(mesh):
    in_specs = (
        P(("req", "blk"), None),
        P("req", None, "blk", None),
        P("req", None),
        P("req", None),
        P(("req", "blk"), None),
        P("req", None),
        P(None, "blk"),
        P(None, "blk"),
        P(None, "blk"),
        P("blk", None),
        P(None, None, "blk"),
        P(None, "req"),
    )
    out_specs = (
        P(("req", "blk"), None),
        P(None, ("req", "blk"), None),
        P("req", None, "blk", None),
    )
    return jax.shard_map(
        on_device, mesh=mesh, in_specs=in_specs, out_specs=out_specs, check_vma=False
    )
```

```python
import math

import jax
import jax.numpy as jnp
from jax import lax
from jax.experimental import pallas as pl
from jax.experimental.pallas import tpu as pltpu
from jax.sharding import PartitionSpec as P

H = 16
HD = 80
TREE = 48
DEPTH = 5
PAGE = 128
BLK = 32
WIDTH = H * HD

EPS = 1e-06
LOWEST = -8388608.0
LEVEL_START = (0, 1, 5, 15, 30, 48)
MESH = pl.DeviceIdType.MESH
ROWSLOT = ((0, 0), (-1, 0), (1, 0), (2, 0))


def rms_rows(values):
    wide = values.astype(jnp.float32)
    return (wide * lax.rsqrt(jnp.mean(wide * wide, axis=-1, keepdims=True) + EPS)).astype(
        jnp.bfloat16
    )


def dot_t(left, right):
    return lax.dot_general(
        left, right, (((1,), (1,)), ((), ())), preferred_element_type=jnp.float32
    )


class Spot:
    def __init__(self):
        self.me = lax.axis_index("blk")
        self.core = self.me % 2
        x = (self.me // 2) % 4
        y = self.me // 8
        self.one = x + self.core * (y - x)
        self.two = y + self.core * (x - y)
        self.sibling = self.me + 1 - 2 * self.core

    def at(self, a, b):
        return self.core + 2 * self.chip(a, b)

    def chip(self, a, b):
        one = (self.one + a + 4) % 4
        two = (self.two + b + 4) % 4
        return (1 + 3 * self.core) * one + (4 - 3 * self.core) * two


def greet_plane(spot, column=False):
    barrier = pltpu.get_barrier_semaphore()
    for who in (spot.at(1, 0), spot.at(-1, 0), spot.at(0, 1), spot.at(0, -1), spot.sibling):
        pl.semaphore_signal(barrier, inc=1, device_id={"blk": who}, device_id_type=MESH)
    if column:
        at = lax.axis_index("req")
        for d in (1, 3):
            pl.semaphore_signal(
                barrier, inc=1, device_id={"req": (at + d) % 4}, device_id_type=MESH
            )
    pl.semaphore_wait(barrier, 7 if column else 5)


def numbered(names):
    return {name: i for i, name in enumerate(names)}


GATHER = numbered(
    ["L", "R", "OA", "OB"]
    + [f"{kind}{k}" for k in range(4) for kind in ("D", "U", "PA", "PB")]
    + [f"S{k}" for k in range(16)]
)


def sender(sent, ssem, rsem, events):
    def put(event, src, dst, who):
        copy = pltpu.make_async_remote_copy(
            src_ref=src,
            dst_ref=dst,
            send_sem=ssem(events[event]),
            recv_sem=rsem(events[event]),
            device_id={"blk": who},
            device_id_type=MESH,
        )
        copy.start()
        sent[event] = copy

    return put


def gather_steps(spot, shard, view, ssem, rsem, lsem, cut):
    sent = {}
    send = sender(sent, ssem, rsem, GATHER)

    def put(event, src, slot, who, half=None):
        dst = view(slot)
        if half is not None:
            src, dst = cut(src, half), cut(dst, half)
        send(event, src, dst, who)

    right, left = spot.at(1, 0), spot.at(-1, 0)
    up, down = spot.at(0, 1), spot.at(0, -1)
    local = pltpu.make_async_copy(shard, view(spot.me), lsem)
    local.start()
    put("L", shard, spot.me, right)
    put("R", shard, spot.me, left)
    put("D0", shard, spot.me, up)
    put("U0", shard, spot.me, down)
    put("S0", shard, spot.me, spot.sibling)
    yield
    for k, event in ((1, "L"), (2, "R")):
        slot = spot.at(*ROWSLOT[k])
        sent[event].wait_recv()
        if k == 1:
            put("OA", view(slot), slot, right, 0)
        else:
            put("OB", view(slot), slot, left, 1)
        put(f"D{k}", view(slot), slot, up)
        put(f"U{k}", view(slot), slot, down)
        put(f"S{k}", view(slot), slot, spot.sibling)
        yield

    def column(k):
        a = ROWSLOT[k][0]
        slot = spot.at(a, -1)
        sent[f"D{k}"].wait_recv()
        put(f"PA{k}", view(slot), slot, up, 0)
        put(f"S{4 + k}", view(slot), slot, spot.sibling)
        slot = spot.at(a, 1)
        sent[f"U{k}"].wait_recv()
        put(f"PB{k}", view(slot), slot, down, 1)
        put(f"S{8 + k}", view(slot), slot, spot.sibling)

    column(0)
    yield
    sent["OA"].wait_recv()
    sent["OB"].wait_recv()
    slot = spot.at(2, 0)
    put("D3", view(slot), slot, up)
    put("U3", view(slot), slot, down)
    put("S3", view(slot), slot, spot.sibling)
    yield
    for k in (1, 2, 3):
        column(k)
        yield
    for k in range(4):
        slot = spot.at(ROWSLOT[k][0], 2)
        sent[f"PA{k}"].wait_recv()
        sent[f"PB{k}"].wait_recv()
        put(f"S{12 + k}", view(slot), slot, spot.sibling)
        yield
    for k in range(16):
        sent[f"S{k}"].wait_recv()
    local.wait()
    for event in GATHER:
        sent[event].wait_send()


def run_all(steps):
    steps = list(steps)
    while steps:
        alive = []
        for step in steps:
            try:
                next(step)
                alive.append(step)
            except StopIteration:
                pass
        steps = alive


def row_halves(rows):
    first = ((rows // 2) + 7) // 8 * 8

    def cut(ref, half):
        return ref.at[pl.ds(0, first)] if half == 0 else ref.at[pl.ds(first, rows - first)]

    return cut


def gather_all(spot, ins, outs, ssem, rsem, lsem):
    count = len(GATHER)
    return [
        gather_steps(
            spot,
            ins[i],
            lambda slot, i=i: outs[i].at[slot],
            lambda e, i=i: ssem.at[i * count + e],
            lambda e, i=i: rsem.at[i * count + e],
            lsem.at[i],
            row_halves(ins[i].shape[0]),
        )
        for i in range(len(ins))
    ]


def gather_sems(arrays):
    return [
        pltpu.SemaphoreType.DMA((arrays * len(GATHER),)),
        pltpu.SemaphoreType.DMA((arrays * len(GATHER),)),
        pltpu.SemaphoreType.DMA((arrays,)),
    ]


COLUMN = numbered(["L", "R", "OA", "OB", "S1", "S2", "S3"])


def column_steps(spot, shard, out, ssem, rsem, lsem):
    at = lax.axis_index("req")
    above, below = (at + 1) % 4, (at + 3) % 4
    half = shard.shape[0] // 2
    base = spot.core * half
    rows = pl.ds(pl.multiple_of(base, 8), half)
    parts = [pl.ds(pl.multiple_of(base + i * (half // 2), 8), half // 2) for i in range(2)]
    sent = {}

    def put(event, src, slot, part, device):
        copy = pltpu.make_async_remote_copy(
            src_ref=src,
            dst_ref=out.at[slot, part],
            send_sem=ssem.at[COLUMN[event]],
            recv_sem=rsem.at[COLUMN[event]],
            device_id=device,
            device_id_type=MESH,
        )
        copy.start()
        sent[event] = copy

    local = pltpu.make_async_copy(shard, out.at[at], lsem)
    local.start()
    put("L", shard.at[rows], at, rows, {"req": above})
    put("R", shard.at[rows], at, rows, {"req": below})
    for _ in range(2):
        yield
    sent["L"].wait_recv()
    put("OA", out.at[below, parts[0]], below, parts[0], {"req": above})
    put("S1", out.at[below, rows], below, rows, {"blk": spot.sibling})
    sent["R"].wait_recv()
    put("OB", out.at[above, parts[1]], above, parts[1], {"req": below})
    put("S2", out.at[above, rows], above, rows, {"blk": spot.sibling})
    for _ in range(3):
        yield
    sent["OA"].wait_recv()
    sent["OB"].wait_recv()
    far = (at + 2) % 4
    put("S3", out.at[far, rows], far, rows, {"blk": spot.sibling})
    yield
    local.wait()
    for event in ("S1", "S2", "S3"):
        sent[event].wait_recv()
    for event in COLUMN:
        sent[event].wait_send()


ANY = pl.BlockSpec(memory_space=pl.ANY)
VMEM = pl.BlockSpec(memory_space=pltpu.VMEM)


def all_gather(shards, collective_id, name):
    count = len(shards)

    def kernel(*refs):
        spot = Spot()
        greet_plane(spot)
        run_all(gather_all(spot, refs[:count], refs[count : 2 * count], *refs[2 * count :]))

    return pl.pallas_call(
        kernel,
        out_shape=[jax.ShapeDtypeStruct((BLK,) + s.shape, s.dtype) for s in shards],
        in_specs=[VMEM] * count,
        out_specs=[ANY] * count,
        scratch_shapes=gather_sems(count),
        compiler_params=pltpu.CompilerParams(collective_id=collective_id, has_side_effects=True),
        name=name,
    )(*shards)


def iota(shape, dim):
    return lax.broadcasted_iota(jnp.int32, shape, dim)


def to_column(row):
    n = row.shape[1]
    return jnp.sum(jnp.where(iota((n, n), 0) == iota((n, n), 1), row, 0), axis=1, keepdims=True)


def to_row(column):
    n = column.shape[0]
    return jnp.sum(jnp.where(iota((n, n), 0) == iota((n, n), 1), column, 0), axis=0, keepdims=True)


def tree_marks(parent_row, leaf):
    square = (TREE, TREE)
    climb = (to_column(parent_row) == iota(square, 1)).astype(jnp.float32)
    current = (iota(square, 0) == iota(square, 1)).astype(jnp.float32)
    marks = current
    for _ in range(DEPTH - 1):
        current = jnp.dot(current, climb, preferred_element_type=jnp.float32)
        marks = jnp.maximum(marks, current)
    chosen = jnp.sum(jnp.where(iota(square, 0) == leaf, marks, 0.0), axis=0, keepdims=True)
    upto = jnp.where(iota(square, 0) <= iota(square, 1), to_column(chosen), 0.0)
    nth = (jnp.sum(upto, axis=0, keepdims=True) - 1.0).astype(jnp.int32)
    picker = (chosen > 0.5) & (nth == iota((16, TREE), 0))
    return marks, picker.astype(jnp.float32)


def page_tables(page_row, length_row, leaf_row, myself, pool_pages):
    requests = length_row.shape[1]
    npages = (length_row + (DEPTH + PAGE - 1)) // PAGE
    square = (requests, requests)
    ends = jnp.sum(
        jnp.where(iota(square, 0) <= iota(square, 1), to_column(npages), 0), axis=0, keepdims=True
    )
    offsets = ends - npages
    my_end = jnp.sum(jnp.where(iota((1, requests), 1) == myself, ends, 0), axis=1, keepdims=True)
    accepted = 1 + sum((leaf_row >= first).astype(jnp.int32) for first in LEVEL_START[1:-1])
    lines = 24
    line = iota((lines, 1), 0)
    slots = page_row.shape[1]
    located = page_row == myself * pool_pages + iota((lines, slots), 0)
    where_at = jnp.sum(jnp.where(located, iota((lines, slots), 1), 0), axis=1, keepdims=True)
    owner = jnp.sum((ends <= where_at).astype(jnp.int32), axis=1, keepdims=True)
    hot = owner == iota((lines, requests), 1)

    def of_owner(row):
        return jnp.sum(jnp.where(hot, row, 0), axis=1, keepdims=True)

    is_tree = line == pool_pages
    spare = line > pool_pages
    owner_or_me = jnp.where(is_tree, myself, jnp.minimum(owner, requests - 1))
    place = owner_or_me % 2 * (requests // 2) + owner_or_me // 2
    start = jnp.where(is_tree, 0, (where_at - of_owner(offsets)) * PAGE)
    length = jnp.where(is_tree, 0, of_owner(length_row))
    count = jnp.where(is_tree, 0, of_owner(accepted))
    spots = jnp.where(is_tree, 2 * my_end - 1, jnp.where(spare, 4 * slots + line, 2 * where_at))
    rank = jnp.sum((to_row(spots) < spots).astype(jnp.int32), axis=1, keepdims=True)
    wide = (lines, 128)

    def in_order(column):
        return jnp.sum(jnp.where(rank == iota(wide, 1), column, 0), axis=0, keepdims=True)

    def as_it_lies(column):
        return jnp.sum(jnp.where(line == iota(wide, 1), column, 0), axis=0, keepdims=True)

    columns = [place, start, length, count, owner_or_me, line]
    rows = [in_order(column) for column in columns]
    lane = iota((1, 128), 1)
    fresh = ((rows[4] != pltpu.roll(rows[4], 1, 1)) | (lane == 0)).astype(jnp.int32)
    last = jnp.max(
        jnp.where((place == iota(wide, 1)) & jnp.logical_not(spare), rank, -1),
        axis=0,
        keepdims=True,
    )
    last = jnp.where(last < 0, pool_pages + 1, last)
    rows += [fresh, fresh, in_order(is_tree.astype(jnp.int32)), last]
    return rows, [as_it_lies(column) for column in (owner_or_me, start, length, count)]


def prepare(shard, patch, tree_input, page_row, length_row, leaf_row, parent_row, pool_pages):
    def kernel(
        shard_ref, patch_ref, x_ref, page_ref, length_ref, leaf_ref, parent_ref,
        full_ref, full_patch_ref, normed_ref, steps_ref, pages_ref, marks_ref, picker_ref,
        *scratch,
    ):
        spot = Spot()
        greet_plane(spot, True)
        steps = gather_all(spot, [shard_ref], [full_ref], *scratch[:3])
        steps.append(column_steps(spot, patch_ref, full_patch_ref, *scratch[3:]))
        for one in steps:
            next(one)
        normed_ref[...] = rms_rows(x_ref[...])
        leaf = jnp.sum(
            jnp.where(iota(leaf_ref.shape, 1) == spot.me, leaf_ref[...], 0), axis=1, keepdims=True
        )
        marks_ref[...], picker = tree_marks(parent_ref[...], leaf)
        picker_ref[...] = picker.astype(jnp.bfloat16)
        in_order, as_they_lie = page_tables(
            page_ref[...], length_ref[...], leaf_ref[...], spot.me, pool_pages
        )
        for k, row in enumerate(in_order):
            steps_ref[pl.ds(k, 1), :] = row
        for k, row in enumerate(as_they_lie):
            pages_ref[pl.ds(k, 1), :] = row
        run_all(steps)

    return pl.pallas_call(
        kernel,
        out_shape=[
            jax.ShapeDtypeStruct((BLK,) + shard.shape, shard.dtype),
            jax.ShapeDtypeStruct((4,) + patch.shape, patch.dtype),
            jax.ShapeDtypeStruct(tree_input.shape, jnp.bfloat16),
            jax.ShapeDtypeStruct((10, 128), jnp.int32),
            jax.ShapeDtypeStruct((4, 128), jnp.int32),
            jax.ShapeDtypeStruct((TREE, TREE), jnp.float32),
            jax.ShapeDtypeStruct((16, TREE), jnp.bfloat16),
        ],
        in_specs=[VMEM] * 7,
        out_specs=[ANY, ANY] + [VMEM] * 5,
        scratch_shapes=gather_sems(1)
        + [
            pltpu.SemaphoreType.DMA((len(COLUMN),)),
            pltpu.SemaphoreType.DMA((len(COLUMN),)),
            pltpu.SemaphoreType.DMA,
        ],
        compiler_params=pltpu.CompilerParams(collective_id=1, has_side_effects=True),
        name="prepare",
    )(shard, patch, tree_input, page_row, length_row, leaf_row, parent_row)


def window(w):
    return 128 * (5 * (w // 4) + w % 4), 32 * (w % 4)


def append_kernel(tables, rows_ref, cache_ref, new_ref, kept, rows, load, save, more):
    pages = kept.shape[0]

    def page_of(ref, p, i):
        return ref.at[0, i, pl.ds(p * PAGE, PAGE)]

    def loads(p):
        return [
            pltpu.make_async_copy(page_of(cache_ref, p, i), kept.at[p, i], load.at[2 * p + i])
            for i in range(2)
        ]

    def saves(p):
        return [
            pltpu.make_async_copy(kept.at[p, i], page_of(new_ref, p, i), save.at[2 * p + i])
            for i in range(2)
        ]

    for p in range(pages):
        for copy in loads(p):
            copy.start()
    for p in range(pages):
        for copy in loads(p):
            copy.wait()
        row0 = tables[2, p] - tables[1, p]
        count = tables[3, p]

        @pl.when((row0 < PAGE) & (row0 + count > 0))
        def _():
            fetch = pltpu.make_async_copy(rows_ref.at[tables[0, p], pl.ds(TREE, 16)], rows, more)
            fetch.start()
            fetch.wait()
            ahead = lax.broadcasted_iota(jnp.int32, (PAGE, 8), 0) - row0
            nth = lax.broadcasted_iota(jnp.int32, (PAGE, 8), 1)
            hot = ((ahead == nth) & (nth < count)).astype(jnp.float32).astype(jnp.bfloat16)
            index = lax.broadcasted_iota(jnp.int32, (PAGE, WIDTH), 0) - row0
            hit = (index >= 0) & (index < count)
            for i in range(2):
                taken = jnp.dot(
                    hot, rows[pl.ds(8 * i, 8), :], preferred_element_type=jnp.float32
                )
                old = kept[p, i].astype(jnp.float32)
                kept[p, i] = jnp.where(hit, taken, old).astype(jnp.bfloat16)

        for copy in saves(p):
            copy.start()
    for p in range(pages):
        for copy in saves(p):
            copy.wait()


def append(tables, gathered, cache):
    pages = cache.shape[2] // PAGE
    return pl.pallas_call(
        append_kernel,
        out_shape=jax.ShapeDtypeStruct(cache.shape, cache.dtype),
        in_specs=[pl.BlockSpec(memory_space=pltpu.SMEM), ANY, ANY],
        out_specs=ANY,
        scratch_shapes=[
            pltpu.VMEM((pages, 2, PAGE, WIDTH), jnp.bfloat16),
            pltpu.VMEM((16, WIDTH), jnp.bfloat16),
            pltpu.SemaphoreType.DMA((2 * pages,)),
            pltpu.SemaphoreType.DMA((2 * pages,)),
            pltpu.SemaphoreType.DMA,
        ],
        compiler_params=pltpu.CompilerParams(vmem_limit_bytes=32 * 1024 * 1024),
        name="append",
    )(tables, gathered, cache)


PAIR = 2 * TREE
LINES = 8 * PAIR


def attend_scratch(pages):
    return [
        pltpu.VMEM((2, pages + 1, PAGE, WIDTH), jnp.bfloat16),
        pltpu.VMEM((BLK, TREE + 16, WIDTH), jnp.bfloat16),
        pltpu.SemaphoreType.DMA((2 * pages + 1,)),
        pltpu.VMEM((8, PAIR, 256), jnp.bfloat16),
        pltpu.VMEM((8, PAIR, 256), jnp.bfloat16),
        pltpu.VMEM((TREE, PAGE), jnp.float32),
        pltpu.VMEM((LINES, 128), jnp.float32),
        pltpu.VMEM((LINES, 128), jnp.bfloat16),
        pltpu.VMEM((LINES, 128), jnp.float32),
        pltpu.VMEM((LINES, 128), jnp.float32),
        pltpu.VMEM((LINES, 128), jnp.float32),
        pltpu.VMEM((8, PAIR, 256), jnp.float32),
        pltpu.VMEM((pages + 2, TREE, WIDTH), jnp.bfloat16),
        pltpu.VMEM((pages + 2, TREE, 128), jnp.float32),
    ]


def attend_steps(tables, query_ref, cache_ref, proj_ref, marks_ref, bufs, pause):
    (kept, query, load, ones, masked, marks, scores, weights, tops, dens, scales, acc, sums, stats) = bufs
    pages = cache_ref.shape[2] // PAGE
    factor = math.log2(math.e) / math.sqrt(HD)
    lanes = lax.broadcasted_iota(jnp.int32, (TREE, 128), 1)
    columns = lax.broadcasted_iota(jnp.int32, (TREE, 256), 1)
    copies = [
        pltpu.make_async_copy(
            cache_ref.at[0, i, pl.ds(p * PAGE, PAGE)], kept.at[i, p], load.at[i * pages + p]
        )
        for i in range(2)
        for p in range(pages)
    ]
    copies.append(pltpu.make_async_copy(query_ref, query, load.at[2 * pages]))
    for copy in copies:
        copy.start()
    yield

    def inside(w, i):
        begin = window(w)[1] + HD * i
        return (columns >= begin) & (columns < begin + HD)

    for w in range(8):
        for i in range(2):
            ones[w, pl.ds(TREE * i, TREE)] = (
                inside(w, i).astype(jnp.float32).astype(jnp.bfloat16)
            )
    for i in range(2):
        kept[i, pages, pl.ds(0, TREE)] = proj_ref[:, pl.ds((1 + i) * WIDTH, WIDTH)]
        kept[i, pages, pl.ds(TREE, PAGE - TREE)] = jnp.zeros((PAGE - TREE, WIDTH), jnp.bfloat16)
    marks[...] = jnp.zeros_like(marks)
    marks[:, pl.ds(0, TREE)] = marks_ref[...]
    tops[...] = jnp.full_like(tops, LOWEST)
    dens[...] = jnp.zeros_like(dens)
    acc[...] = jnp.zeros_like(acc)
    sums[pages + 1] = jnp.zeros((TREE, WIDTH), jnp.bfloat16)
    stats[pages + 1] = jnp.where(lanes < 64, LOWEST, 0.0)
    for copy in copies:
        copy.wait()

    def step(j, carry):
        start, length, owner = tables[1, j], tables[2, j], tables[4, j]
        page, fresh, tree = tables[5, j], tables[6, j] > 0, tables[8, j] > 0
        for w in range(8):
            picked = query[owner, pl.ds(0, TREE), pl.ds(window(w)[0], 256)]
            for i in range(2):
                half = pl.ds(TREE * i, TREE)
                masked[w, half] = picked * ones[w, half]
        for w in range(8):
            scores[pl.ds(PAIR * w, PAIR), :] = dot_t(
                masked[w], kept[0, page, :, pl.ds(window(w)[0], 256)]
            )
        near = (lanes + start < length).astype(jnp.float32)
        seen = jnp.where(tree, marks[...], near)
        shown = jnp.concatenate([seen] * 4, axis=0) > 0.5
        for part in range(4):
            rows = pl.ds(2 * PAIR * part, 2 * PAIR)
            part_scores = jnp.where(shown, scores[rows, :] * factor, LOWEST)
            before = jnp.where(fresh, LOWEST, tops[rows, :])
            top = jnp.maximum(before, jnp.ceil(jnp.max(part_scores, axis=1, keepdims=True)))
            weight = jnp.where(shown, jnp.exp2(part_scores - top), 0.0)
            scale = jnp.where(fresh, 0.0, jnp.exp2(before - top))
            tops[rows, :] = top
            scales[rows, :] = scale
            dens[rows, :] = dens[rows, :] * scale + jnp.sum(weight, axis=1, keepdims=True)
            weights[rows, :] = weight.astype(jnp.bfloat16)
        carried = None
        for w in range(8):
            rows = pl.ds(PAIR * w, PAIR)
            added = jnp.dot(
                weights[rows, :],
                kept[1, page, :, pl.ds(window(w)[0], 256)],
                preferred_element_type=jnp.float32,
            )
            scale = scales[rows, :]
            total = acc[w] * jnp.concatenate([scale, scale], axis=1) + added
            acc[w] = total
            picked = jnp.where(
                inside(w, 0), total[:TREE], jnp.where(inside(w, 1), total[TREE:], 0.0)
            )
            head = picked[:, :128]
            if w % 4:
                head = head + carried
            carried = picked[:, 128:]
            sums[j, :, pl.ds(window(w)[0], 128)] = head.astype(jnp.bfloat16)
            if w % 4 == 3:
                sums[j, :, pl.ds(window(w)[0] + 128, 128)] = carried.astype(jnp.bfloat16)
        row = jnp.full((TREE, 128), LOWEST, jnp.float32)
        for head in range(H):
            rows = pl.ds(TREE * head, TREE)
            row = jnp.where(lanes == head, tops[rows, :], row)
            row = jnp.where(lanes == 64 + head, dens[rows, :], row)
        stats[j] = row
        return carry

    first = 0
    for last in pause + (pages + 1,):
        lax.fori_loop(first, last, step, 0)
        first = last
        if last <= pages:
            yield


PAIR_ORDER = (
    [(2, b) for b in range(4)]
    + [(1, 2), (1, 3), (-1, 0), (-1, 1)]
    + [(1, 0), (1, 1), (-1, 2), (-1, 3)]
    + [(0, b) for b in range(4)]
)
REDUCE = numbered(
    [f"{kind}{i}{s}" for kind, n in (("P", 16), ("T", 4), ("L", 4), ("R", 4)) for i in range(n) for s in "ns"]
    + [f"{kind}{s}" for kind in ("t0", "t1", "l", "r") for s in "ns"]
)


PAUSES = (3, 6, 9, 12, 14)
ADVANCES = (0, 6, 10, 14, 18, 22)


def split_stats(stats):
    return stats, pltpu.roll(stats, 64, 1)


def combine(parts, spread):
    stats = [split_stats(s) for _, s in parts]
    lanes = lax.broadcasted_iota(jnp.int32, stats[0][0].shape, 1)
    top = stats[0][0]
    for s, _ in stats[1:]:
        top = jnp.maximum(top, s)
    total = None
    num = None
    for (n, _), (s, d) in zip(parts, stats):
        scale = jnp.where(lanes < H, jnp.exp2(jnp.minimum(s - top, 0.0)), 0.0)
        wide = jnp.dot(scale.astype(jnp.bfloat16), spread, preferred_element_type=jnp.float32)
        d = d * scale
        n = n.astype(jnp.float32) * wide
        total = d if total is None else total + d
        num = n if num is None else num + n
    return num, top, total


def join_stats(top, total):
    lanes = lax.broadcasted_iota(jnp.int32, top.shape, 1)
    return jnp.where(lanes < H, top, pltpu.roll(jnp.where(lanes < H, total, 0.0), 64, 1))


def reduce_steps(spot, tables, sums, stats, out, spread, bufs, ssem, rsem):
    pair_n, pair_s, work_n, work_s, thru_n, thru_s, left_n, left_s, right_n, right_s = bufs[:10]
    fin_n, fin_s, two_n, two_s, out_n, out_s = bufs[10:]
    sent = {}
    send = sender(sent, ssem, rsem, REDUCE)

    def put(event, src_n, src_s, dst_n, dst_s, who):
        send(event + "n", src_n, dst_n, who)
        send(event + "s", src_s, dst_s, who)

    def took(event):
        sent[event + "n"].wait_recv()
        sent[event + "s"].wait_recv()

    right, left = spot.at(1, 0), spot.at(-1, 0)
    up, down = spot.at(0, 1), spot.at(0, -1)
    other = (1 - spot.core) * 16
    mine = spot.core * 16
    for i, (a, b) in enumerate(PAIR_ORDER):
        found = tables[9, other + spot.chip(b, a)]
        out_n[i] = sums[found]
        out_s[i] = stats[found]
        put(f"P{i}", out_n.at[i], out_s.at[i], pair_n.at[i], pair_s.at[i], spot.sibling)
    yield

    def store(dst_n, dst_s, parts):
        n, top, total = combine(parts, spread())
        dst_n[...] = n.astype(jnp.bfloat16)
        dst_s[...] = join_stats(top, total)

    place = {pair: i for i, pair in enumerate(PAIR_ORDER)}
    for i, (a, b) in enumerate(PAIR_ORDER):
        took(f"P{i}")
        found = tables[9, mine + spot.chip(a, b)]
        store(
            work_n.at[i], work_s.at[i], [(sums[found], stats[found]), (pair_n[i], pair_s[i])]
        )
        if a == 2:
            put(
                f"T{b}", work_n.at[i], work_s.at[i], thru_n.at[b], thru_s.at[b],
                right if b < 2 else left,
            )
        elif (a == 1 and b >= 2):
            put(f"L{b}", work_n.at[i], work_s.at[i], left_n.at[b], left_s.at[b], right)
        elif (a == -1 and b < 2):
            put(f"R{b}", work_n.at[i], work_s.at[i], right_n.at[b], right_s.at[b], left)
        yield
    for b in range(4):
        took(f"T{b}")
        a = 1 if b < 2 else -1
        i = place[(a, b)]
        store(
            work_n.at[i], work_s.at[i], [(work_n[i], work_s[i]), (thru_n[b], thru_s[b])]
        )
        if a == 1:
            put(f"L{b}", work_n.at[i], work_s.at[i], left_n.at[b], left_s.at[b], right)
        else:
            put(f"R{b}", work_n.at[i], work_s.at[i], right_n.at[b], right_s.at[b], left)
        yield
    cuts = (pl.ds(0, 32), pl.ds(32, 16))
    for b in (2, 1, 3, 0):
        took(f"L{b}")
        took(f"R{b}")
        i = place[(0, b)]
        store(
            fin_n.at[b],
            fin_s.at[b],
            [(work_n[i], work_s[i]), (left_n[b], left_s[b]), (right_n[b], right_s[b])],
        )
        if b == 2:
            for half, who in ((0, up), (1, down)):
                put(
                    f"t{half}",
                    fin_n.at[2, cuts[half]],
                    fin_s.at[2, cuts[half]],
                    two_n.at[0, cuts[half]],
                    two_s.at[0, cuts[half]],
                    who,
                )
        yield
    for half, b in ((0, 1), (1, 3)):
        took(f"t{half}")
        rows = cuts[half]
        store(
            fin_n.at[b, rows],
            fin_s.at[b, rows],
            [(fin_n[b, rows], fin_s[b, rows]), (two_n[0, rows], two_s[0, rows])],
        )
        if b == 1:
            put("l", fin_n.at[1], fin_s.at[1], two_n.at[1], two_s.at[1], up)
        else:
            put("r", fin_n.at[3], fin_s.at[3], two_n.at[2], two_s.at[2], down)
        yield
    took("l")
    took("r")
    n, top, total = combine(
        [(fin_n[0], fin_s[0]), (two_n[1], two_s[1]), (two_n[2], two_s[2])], spread()
    )
    lanes = lax.broadcasted_iota(jnp.int32, total.shape, 1)
    inverse = jnp.where(lanes < H, 1.0 / jnp.where(lanes < H, total, 1.0), 0.0)
    wide = jnp.dot(
        inverse,
        spread().astype(jnp.float32),
        preferred_element_type=jnp.float32,
        precision=lax.Precision.HIGHEST,
    )
    out[...] = (n * wide).astype(jnp.bfloat16)
    for event in REDUCE:
        sent[event].wait_send()


def attend_and_reduce(tables, gathered, cache, projected, marks, spread, shards, collective_id):
    count = len(shards)
    pages = cache.shape[2] // PAGE

    def block(n):
        return [
            pltpu.VMEM((n, TREE, WIDTH), jnp.bfloat16),
            pltpu.VMEM((n, TREE, 128), jnp.float32),
        ]

    parts = [
        [pltpu.SemaphoreType.DMA((len(REDUCE),))] * 2,
        gather_sems(count),
        attend_scratch(pages),
        block(16) + block(16) + block(4) + block(4) + block(4) + block(4) + block(3) + block(16),
    ]

    def kernel(tables_ref, query_ref, cache_ref, proj_ref, marks_ref, spread_ref, *refs):
        ins = refs[:count]
        out = refs[count]
        outs = refs[count + 1 : 2 * count + 1]
        left = list(refs[2 * count + 1 :])
        scratch = []
        for part in parts:
            scratch.append(left[: len(part)])
            left = left[len(part) :]
        (ssem, rsem), gather_scratch, attend_bufs, reduce_bufs = scratch
        spot = Spot()
        work = attend_steps(
            tables_ref, query_ref, cache_ref, proj_ref, marks_ref, attend_bufs, PAUSES
        )
        next(work)
        greet_plane(spot)
        gathers = gather_all(spot, ins, outs, *gather_scratch)

        def advance():
            for one in gathers:
                next(one, None)

        advance()
        for _ in work:
            advance()
        for i, _ in enumerate(
            reduce_steps(
                spot,
                tables_ref,
                attend_bufs[-2],
                attend_bufs[-1],
                out,
                lambda: spread_ref[...],
                reduce_bufs,
                lambda e: ssem.at[e],
                lambda e: rsem.at[e],
            )
        ):
            if i in ADVANCES:
                advance()
        run_all(gathers)

    return pl.pallas_call(
        kernel,
        out_shape=[jax.ShapeDtypeStruct((TREE, WIDTH), jnp.bfloat16)]
        + [jax.ShapeDtypeStruct((BLK,) + s.shape, s.dtype) for s in shards],
        in_specs=[pl.BlockSpec(memory_space=pltpu.SMEM), ANY, ANY, VMEM, VMEM, VMEM] + [VMEM] * count,
        out_specs=[VMEM] + [ANY] * count,
        scratch_shapes=[ref for part in parts for ref in part],
        compiler_params=pltpu.CompilerParams(
            collective_id=collective_id,
            has_side_effects=True,
            vmem_limit_bytes=52 * 1024 * 1024,
        ),
        name="attend_and_reduce",
    )(tables, gathered, cache, projected, marks, spread, *shards)


def greet_column(at):
    barrier = pltpu.get_barrier_semaphore()
    for d in (1, 2, 3):
        pl.semaphore_signal(
            barrier, inc=1, device_id={"req": (at + d) % 4}, device_id_type=MESH
        )
    pl.semaphore_wait(barrier, 3)


def column_kernel(exchange):
    def kernel(block, out, ssem, rsem, lsem):
        at = lax.axis_index("req")
        greet_column(at)
        copies = []
        for d in (2, 1, 3):
            to = (at + d) % 4
            copy = pltpu.make_async_remote_copy(
                src_ref=block.at[to] if exchange else block,
                dst_ref=out.at[at],
                send_sem=ssem.at[d - 1],
                recv_sem=rsem.at[d - 1],
                device_id={"req": to},
                device_id_type=MESH,
            )
            copy.start()
            copies.append(copy)
        local = pltpu.make_async_copy(block.at[at] if exchange else block, out.at[at], lsem)
        local.start()
        local.wait()
        for copy in copies:
            copy.wait()

    return kernel


def over_column(block, exchange, collective_id, name):
    shape = block.shape if exchange else (4,) + block.shape
    return pl.pallas_call(
        column_kernel(exchange),
        out_shape=jax.ShapeDtypeStruct(shape, block.dtype),
        in_specs=[VMEM],
        out_specs=VMEM,
        scratch_shapes=[
            pltpu.SemaphoreType.DMA((3,)),
            pltpu.SemaphoreType.DMA((3,)),
            pltpu.SemaphoreType.DMA,
        ],
        compiler_params=pltpu.CompilerParams(
            collective_id=collective_id, has_side_effects=True
        ),
        name=name,
    )(block)


def on_device(
    tree_input,
    cache,
    page_table,
    lengths,
    parents,
    accept_leaf,
    w_qkv,
    w_out,
    w_up,
    w_down,
    w_draft,
    w_patch,
):
    width = WIDTH
    pool_pages = cache.shape[2] // PAGE
    draft_mine = lax.dynamic_index_in_dim(
        w_draft.transpose(0, 2, 1), lax.axis_index("req"), 0, keepdims=False
    )
    qkv, patch, normed, tables, pages, marks, picker = prepare(
        w_qkv.T, w_patch.T, tree_input, page_table, lengths, accept_leaf, parents, pool_pages
    )
    projected = dot_t(normed, qkv.reshape(3 * width, width)).astype(jnp.bfloat16)
    send_rows = jnp.dot(
        picker[:8], projected[:, width:], preferred_element_type=jnp.float32
    ).astype(jnp.bfloat16)
    (gathered,) = all_gather(
        [jnp.concatenate([projected[:, :width], send_rows[:, :width], send_rows[:, width:]])],
        2,
        "gather_query",
    )
    cache_new = append(pages, gathered, cache)
    spread = (
        jnp.arange(128, dtype=jnp.int32)[:, None]
        == jnp.arange(width, dtype=jnp.int32)[None, :] // HD
    ).astype(jnp.bfloat16)
    attended, full_out, full_up, full_down, full_draft = attend_and_reduce(
        tables,
        gathered,
        cache,
        projected,
        marks,
        spread,
        [w_out.T, w_up.T, w_down, draft_mine],
        3,
    )
    full_out, full_up, full_down, full_draft, patch = (
        w.reshape(width, width) for w in (full_out, full_up, full_down, full_draft, patch)
    )
    proj = dot_t(attended, full_out).astype(jnp.bfloat16)
    mid = (tree_input.astype(jnp.float32) + proj.astype(jnp.float32)).astype(jnp.bfloat16)
    hidden = jax.nn.gelu(dot_t(rms_rows(mid), full_up)).astype(jnp.bfloat16)
    feedforward = jnp.dot(hidden, full_down, preferred_element_type=jnp.float32)
    layer_out = (mid.astype(jnp.float32) + feedforward).astype(jnp.bfloat16)
    rows = over_column(layer_out, False, 4, "gather_rows").reshape(4 * TREE, width)
    branch = jax.nn.silu(dot_t(rms_rows(rows), full_draft)).astype(jnp.bfloat16)
    drafted = (rows.astype(jnp.float32) + branch.astype(jnp.float32)).astype(jnp.bfloat16)
    head = dot_t(drafted, patch).astype(jnp.bfloat16)
    drafts = over_column(head.reshape(4, TREE, width), True, 5, "return_rows")
    return (layer_out, drafts, cache_new)


def solution(mesh):
    in_specs = (
        P(("req", "blk"), None),
        P("req", None, "blk", None),
        P("req", None),
        P("req", None),
        P(("req", "blk"), None),
        P("req", None),
        P(None, "blk"),
        P(None, "blk"),
        P(None, "blk"),
        P("blk", None),
        P(None, None, "blk"),
        P(None, "req"),
    )
    out_specs = (
        P(("req", "blk"), None),
        P(None, ("req", "blk"), None),
        P("req", None, "blk", None),
    )
    return jax.shard_map(
        on_device, mesh=mesh, in_specs=in_specs, out_specs=out_specs, check_vma=False
    )
```

```python
import math

import jax
import jax.numpy as jnp
from jax import lax
from jax.experimental import pallas as pl
from jax.experimental.pallas import tpu as pltpu
from jax.sharding import PartitionSpec as P

H = 16
HD = 80
TREE = 48
DEPTH = 5
PAGE = 128
BLK = 32
WIDTH = H * HD

EPS = 1e-06
LOWEST = -8388608.0
LEVEL_START = (0, 1, 5, 15, 30, 48)
MESH = pl.DeviceIdType.MESH
ROWSLOT = ((0, 0), (-1, 0), (1, 0), (2, 0))


def rms_rows(values):
    wide = values.astype(jnp.float32)
    return (wide * lax.rsqrt(jnp.mean(wide * wide, axis=-1, keepdims=True) + EPS)).astype(
        jnp.bfloat16
    )


def dot_t(left, right):
    return lax.dot_general(
        left, right, (((1,), (1,)), ((), ())), preferred_element_type=jnp.float32
    )


class Spot:
    def __init__(self):
        self.me = lax.axis_index("blk")
        self.core = self.me % 2
        x = (self.me // 2) % 4
        y = self.me // 8
        self.one = x + self.core * (y - x)
        self.two = y + self.core * (x - y)
        self.sibling = self.me + 1 - 2 * self.core

    def at(self, a, b):
        return self.core + 2 * self.chip(a, b)

    def chip(self, a, b):
        one = (self.one + a + 4) % 4
        two = (self.two + b + 4) % 4
        return (1 + 3 * self.core) * one + (4 - 3 * self.core) * two


def greet_plane(spot, column=False):
    barrier = pltpu.get_barrier_semaphore()
    for who in (spot.at(1, 0), spot.at(-1, 0), spot.at(0, 1), spot.at(0, -1), spot.sibling):
        pl.semaphore_signal(barrier, inc=1, device_id={"blk": who}, device_id_type=MESH)
    if column:
        at = lax.axis_index("req")
        for d in (1, 3):
            pl.semaphore_signal(
                barrier, inc=1, device_id={"req": (at + d) % 4}, device_id_type=MESH
            )
    pl.semaphore_wait(barrier, 7 if column else 5)


def numbered(names):
    return {name: i for i, name in enumerate(names)}


GATHER = numbered(
    ["L", "R", "OA", "OB"]
    + [f"{kind}{k}" for k in range(4) for kind in ("D", "U", "PA", "PB")]
    + [f"S{k}" for k in range(16)]
)


def sender(sent, ssem, rsem, events):
    def put(event, src, dst, who):
        copy = pltpu.make_async_remote_copy(
            src_ref=src,
            dst_ref=dst,
            send_sem=ssem(events[event]),
            recv_sem=rsem(events[event]),
            device_id={"blk": who},
            device_id_type=MESH,
        )
        copy.start()
        sent[event] = copy

    return put


def gather_steps(spot, shard, view, ssem, rsem, lsem, cut):
    sent = {}
    send = sender(sent, ssem, rsem, GATHER)

    def put(event, src, slot, who, half=None):
        dst = view(slot)
        if half is not None:
            src, dst = cut(src, half), cut(dst, half)
        send(event, src, dst, who)

    right, left = spot.at(1, 0), spot.at(-1, 0)
    up, down = spot.at(0, 1), spot.at(0, -1)
    local = pltpu.make_async_copy(shard, view(spot.me), lsem)
    local.start()
    put("L", shard, spot.me, right)
    put("R", shard, spot.me, left)
    put("D0", shard, spot.me, up)
    put("U0", shard, spot.me, down)
    put("S0", shard, spot.me, spot.sibling)
    yield
    for k, event in ((1, "L"), (2, "R")):
        slot = spot.at(*ROWSLOT[k])
        sent[event].wait_recv()
        if k == 1:
            put("OA", view(slot), slot, right, 0)
        else:
            put("OB", view(slot), slot, left, 1)
        put(f"D{k}", view(slot), slot, up)
        put(f"U{k}", view(slot), slot, down)
        put(f"S{k}", view(slot), slot, spot.sibling)
        yield

    def column(k):
        a = ROWSLOT[k][0]
        slot = spot.at(a, -1)
        sent[f"D{k}"].wait_recv()
        put(f"PA{k}", view(slot), slot, up, 0)
        put(f"S{4 + k}", view(slot), slot, spot.sibling)
        slot = spot.at(a, 1)
        sent[f"U{k}"].wait_recv()
        put(f"PB{k}", view(slot), slot, down, 1)
        put(f"S{8 + k}", view(slot), slot, spot.sibling)

    column(0)
    yield
    sent["OA"].wait_recv()
    sent["OB"].wait_recv()
    slot = spot.at(2, 0)
    put("D3", view(slot), slot, up)
    put("U3", view(slot), slot, down)
    put("S3", view(slot), slot, spot.sibling)
    yield
    for k in (1, 2, 3):
        column(k)
        yield
    for k in range(4):
        slot = spot.at(ROWSLOT[k][0], 2)
        sent[f"PA{k}"].wait_recv()
        sent[f"PB{k}"].wait_recv()
        put(f"S{12 + k}", view(slot), slot, spot.sibling)
        yield
    for k in range(16):
        sent[f"S{k}"].wait_recv()
    local.wait()
    for event in GATHER:
        sent[event].wait_send()


def run_all(steps):
    steps = list(steps)
    while steps:
        alive = []
        for step in steps:
            try:
                next(step)
                alive.append(step)
            except StopIteration:
                pass
        steps = alive


def row_halves(rows):
    first = ((rows // 2) + 7) // 8 * 8

    def cut(ref, half):
        return ref.at[pl.ds(0, first)] if half == 0 else ref.at[pl.ds(first, rows - first)]

    return cut


def gather_all(spot, ins, outs, ssem, rsem, lsem, cuts=None):
    count = len(GATHER)
    steps = []
    for i, (shard, out) in enumerate(zip(ins, outs)):
        first = 0
        for rows in (cuts or {}).get(i, (shard.shape[0],)):
            piece = pl.ds(first, rows)
            at = len(steps) * count
            steps.append(
                gather_steps(
                    spot,
                    shard.at[piece],
                    lambda slot, out=out, piece=piece: out.at[slot, piece],
                    lambda e, at=at: ssem.at[at + e],
                    lambda e, at=at: rsem.at[at + e],
                    lsem.at[len(steps)],
                    row_halves(rows),
                )
            )
            first += rows
    return steps


def gather_sems(arrays):
    return [
        pltpu.SemaphoreType.DMA((arrays * len(GATHER),)),
        pltpu.SemaphoreType.DMA((arrays * len(GATHER),)),
        pltpu.SemaphoreType.DMA((arrays,)),
    ]


COLUMN = numbered(["L", "R", "OA", "OB", "S1", "S2", "S3"])


def column_steps(spot, shard, out, ssem, rsem, lsem):
    at = lax.axis_index("req")
    above, below = (at + 1) % 4, (at + 3) % 4
    half = shard.shape[0] // 2
    base = spot.core * half
    rows = pl.ds(pl.multiple_of(base, 8), half)
    parts = [pl.ds(pl.multiple_of(base + i * (half // 2), 8), half // 2) for i in range(2)]
    sent = {}

    def put(event, src, slot, part, device):
        copy = pltpu.make_async_remote_copy(
            src_ref=src,
            dst_ref=out.at[slot, part],
            send_sem=ssem.at[COLUMN[event]],
            recv_sem=rsem.at[COLUMN[event]],
            device_id=device,
            device_id_type=MESH,
        )
        copy.start()
        sent[event] = copy

    local = pltpu.make_async_copy(shard, out.at[at], lsem)
    local.start()
    put("L", shard.at[rows], at, rows, {"req": above})
    put("R", shard.at[rows], at, rows, {"req": below})
    for _ in range(2):
        yield
    sent["L"].wait_recv()
    put("OA", out.at[below, parts[0]], below, parts[0], {"req": above})
    put("S1", out.at[below, rows], below, rows, {"blk": spot.sibling})
    sent["R"].wait_recv()
    put("OB", out.at[above, parts[1]], above, parts[1], {"req": below})
    put("S2", out.at[above, rows], above, rows, {"blk": spot.sibling})
    for _ in range(3):
        yield
    sent["OA"].wait_recv()
    sent["OB"].wait_recv()
    far = (at + 2) % 4
    put("S3", out.at[far, rows], far, rows, {"blk": spot.sibling})
    yield
    local.wait()
    for event in ("S1", "S2", "S3"):
        sent[event].wait_recv()
    for event in COLUMN:
        sent[event].wait_send()


ANY = pl.BlockSpec(memory_space=pl.ANY)
HBM = pl.BlockSpec(memory_space=pltpu.HBM)
VMEM = pl.BlockSpec(memory_space=pltpu.VMEM)


def all_gather(shards, cuts, collective_id, name):
    count = len(shards)

    def kernel(*refs):
        spot = Spot()
        greet_plane(spot)
        run_all(gather_all(spot, refs[:count], refs[count : 2 * count], *refs[2 * count :], cuts))

    return pl.pallas_call(
        kernel,
        out_shape=[jax.ShapeDtypeStruct((BLK,) + s.shape, s.dtype) for s in shards],
        in_specs=[VMEM] * count,
        out_specs=[ANY] * count,
        scratch_shapes=gather_sems(count + sum(len(rows) - 1 for rows in cuts.values())),
        compiler_params=pltpu.CompilerParams(collective_id=collective_id, has_side_effects=True),
        name=name,
    )(*shards)


QKV_CUTS = (48, 48, 24)
QUERY_CUTS = (32, 32)


def iota(shape, dim):
    return lax.broadcasted_iota(jnp.int32, shape, dim)


def to_column(row):
    n = row.shape[1]
    return jnp.sum(jnp.where(iota((n, n), 0) == iota((n, n), 1), row, 0), axis=1, keepdims=True)


def to_row(column):
    n = column.shape[0]
    return jnp.sum(jnp.where(iota((n, n), 0) == iota((n, n), 1), column, 0), axis=0, keepdims=True)


def tree_marks(parent_row, leaf):
    square = (TREE, TREE)
    climb = (to_column(parent_row) == iota(square, 1)).astype(jnp.float32)
    current = (iota(square, 0) == iota(square, 1)).astype(jnp.float32)
    marks = current
    for _ in range(DEPTH - 1):
        current = jnp.dot(current, climb, preferred_element_type=jnp.float32)
        marks = jnp.maximum(marks, current)
    chosen = jnp.sum(jnp.where(iota(square, 0) == leaf, marks, 0.0), axis=0, keepdims=True)
    upto = jnp.where(iota(square, 0) <= iota(square, 1), to_column(chosen), 0.0)
    nth = (jnp.sum(upto, axis=0, keepdims=True) - 1.0).astype(jnp.int32)
    picker = (chosen > 0.5) & (nth == iota((16, TREE), 0))
    return marks, picker.astype(jnp.float32)


def page_tables(page_row, length_row, leaf_row, myself, pool_pages):
    requests = length_row.shape[1]
    npages = (length_row + (DEPTH + PAGE - 1)) // PAGE
    square = (requests, requests)
    ends = jnp.sum(
        jnp.where(iota(square, 0) <= iota(square, 1), to_column(npages), 0), axis=0, keepdims=True
    )
    offsets = ends - npages
    my_end = jnp.sum(jnp.where(iota((1, requests), 1) == myself, ends, 0), axis=1, keepdims=True)
    accepted = 1 + sum((leaf_row >= first).astype(jnp.int32) for first in LEVEL_START[1:-1])
    lines = 24
    line = iota((lines, 1), 0)
    slots = page_row.shape[1]
    located = page_row == myself * pool_pages + iota((lines, slots), 0)
    where_at = jnp.sum(jnp.where(located, iota((lines, slots), 1), 0), axis=1, keepdims=True)
    owner = jnp.sum((ends <= where_at).astype(jnp.int32), axis=1, keepdims=True)
    hot = owner == iota((lines, requests), 1)

    def of_owner(row):
        return jnp.sum(jnp.where(hot, row, 0), axis=1, keepdims=True)

    is_tree = line == pool_pages
    spare = line > pool_pages
    owner_or_me = jnp.where(is_tree, myself, jnp.minimum(owner, requests - 1))
    place = owner_or_me % 2 * (requests // 2) + owner_or_me // 2
    start = jnp.where(is_tree, 0, (where_at - of_owner(offsets)) * PAGE)
    length = jnp.where(is_tree, 0, of_owner(length_row))
    count = jnp.where(is_tree, 0, of_owner(accepted))
    spots = jnp.where(is_tree, 2 * my_end - 1, jnp.where(spare, 4 * slots + line, 2 * where_at))
    rank = jnp.sum((to_row(spots) < spots).astype(jnp.int32), axis=1, keepdims=True)
    wide = (lines, 128)

    def in_order(column):
        return jnp.sum(jnp.where(rank == iota(wide, 1), column, 0), axis=0, keepdims=True)

    def as_it_lies(column):
        return jnp.sum(jnp.where(line == iota(wide, 1), column, 0), axis=0, keepdims=True)

    columns = [place, start, length, count, owner_or_me, line]
    rows = [in_order(column) for column in columns]
    lane = iota((1, 128), 1)
    fresh = ((rows[4] != pltpu.roll(rows[4], 1, 1)) | (lane == 0)).astype(jnp.int32)
    last = jnp.max(
        jnp.where((place == iota(wide, 1)) & jnp.logical_not(spare), rank, -1),
        axis=0,
        keepdims=True,
    )
    last = jnp.where(last < 0, pool_pages + 1, last)
    rows += [fresh, fresh, in_order(is_tree.astype(jnp.int32)), last]
    return rows, [as_it_lies(column) for column in (owner_or_me, start, length, count)]


def prepare(shard, patch, tree_input, page_row, length_row, leaf_row, parent_row, pool_pages):
    def kernel(
        shard_ref, patch_ref, x_ref, page_ref, length_ref, leaf_ref, parent_ref,
        full_ref, full_patch_ref, normed_ref, steps_ref, pages_ref, marks_ref, picker_ref,
        *scratch,
    ):
        spot = Spot()
        greet_plane(spot, True)
        steps = gather_all(spot, [shard_ref], [full_ref], *scratch[:3], {0: QKV_CUTS})
        steps.append(column_steps(spot, patch_ref, full_patch_ref, *scratch[3:]))
        for _ in range(3):
            for one in steps:
                next(one)
        normed_ref[...] = rms_rows(x_ref[...])
        leaf = jnp.sum(
            jnp.where(iota(leaf_ref.shape, 1) == spot.me, leaf_ref[...], 0), axis=1, keepdims=True
        )
        marks_ref[...], picker = tree_marks(parent_ref[...], leaf)
        picker_ref[...] = picker.astype(jnp.bfloat16)
        in_order, as_they_lie = page_tables(
            page_ref[...], length_ref[...], leaf_ref[...], spot.me, pool_pages
        )
        for k, row in enumerate(in_order):
            steps_ref[pl.ds(k, 1), :] = row
        for k, row in enumerate(as_they_lie):
            pages_ref[pl.ds(k, 1), :] = row
        run_all(steps)

    return pl.pallas_call(
        kernel,
        out_shape=[
            jax.ShapeDtypeStruct((BLK,) + shard.shape, shard.dtype),
            jax.ShapeDtypeStruct((4,) + patch.shape, patch.dtype),
            jax.ShapeDtypeStruct(tree_input.shape, jnp.bfloat16),
            jax.ShapeDtypeStruct((10, 128), jnp.int32),
            jax.ShapeDtypeStruct((4, 128), jnp.int32),
            jax.ShapeDtypeStruct((TREE, TREE), jnp.float32),
            jax.ShapeDtypeStruct((16, TREE), jnp.bfloat16),
        ],
        in_specs=[VMEM] * 7,
        out_specs=[ANY, ANY] + [VMEM] * 5,
        scratch_shapes=gather_sems(len(QKV_CUTS))
        + [
            pltpu.SemaphoreType.DMA((len(COLUMN),)),
            pltpu.SemaphoreType.DMA((len(COLUMN),)),
            pltpu.SemaphoreType.DMA,
        ],
        compiler_params=pltpu.CompilerParams(collective_id=1, has_side_effects=True),
        name="prepare",
    )(shard, patch, tree_input, page_row, length_row, leaf_row, parent_row)


def window(w):
    return 128 * (5 * (w // 4) + w % 4), 32 * (w % 4)


def draft_kernel(
    tables, fresh_ref, cache_ref, layer_ref, draft_ref, patch_ref, head_ref, new_ref,
    kept, rows, draft, patch, load, save, more, wide,
):
    pages = kept.shape[0]
    weights = [
        pltpu.make_async_copy(draft_ref, draft, wide.at[0]),
        pltpu.make_async_copy(patch_ref, patch, wide.at[1]),
    ]

    def page_of(ref, p, i):
        return ref.at[0, i, pl.ds(p * PAGE, PAGE)]

    def loads(p):
        return [
            pltpu.make_async_copy(page_of(cache_ref, p, i), kept.at[p, i], load.at[2 * p + i])
            for i in range(2)
        ]

    def saves(p):
        return [
            pltpu.make_async_copy(kept.at[p, i], page_of(new_ref, p, i), save.at[2 * p + i])
            for i in range(2)
        ]

    for p in range(pages):
        for copy in loads(p):
            copy.start()
    for copy in weights:
        copy.start()
    for p in range(pages):
        for copy in loads(p):
            copy.wait()
        row0 = tables[2, p] - tables[1, p]
        count = tables[3, p]

        @pl.when((row0 < PAGE) & (row0 + count > 0))
        def _():
            fetch = pltpu.make_async_copy(fresh_ref.at[tables[0, p], pl.ds(TREE, 16)], rows, more)
            fetch.start()
            fetch.wait()
            ahead = lax.broadcasted_iota(jnp.int32, (PAGE, 8), 0) - row0
            nth = lax.broadcasted_iota(jnp.int32, (PAGE, 8), 1)
            hot = ((ahead == nth) & (nth < count)).astype(jnp.float32).astype(jnp.bfloat16)
            index = lax.broadcasted_iota(jnp.int32, (PAGE, WIDTH), 0) - row0
            hit = (index >= 0) & (index < count)
            for i in range(2):
                taken = jnp.dot(
                    hot, rows[pl.ds(8 * i, 8), :], preferred_element_type=jnp.float32
                )
                old = kept[p, i].astype(jnp.float32)
                kept[p, i] = jnp.where(hit, taken, old).astype(jnp.bfloat16)

        for copy in saves(p):
            copy.start()
    weights[0].wait()
    layer = layer_ref[...]
    grown = dot_t(rms_rows(layer), draft[...])
    branch = (grown / (1.0 + jnp.exp(-grown))).astype(jnp.bfloat16)
    drafted = (layer.astype(jnp.float32) + branch.astype(jnp.float32)).astype(jnp.bfloat16)
    weights[1].wait()
    head_ref[...] = dot_t(drafted, patch[...]).astype(jnp.bfloat16)
    for p in range(pages):
        for copy in saves(p):
            copy.wait()


def draft_and_append(tables, gathered, cache, layer, draft, patch):
    pages = cache.shape[2] // PAGE
    return pl.pallas_call(
        draft_kernel,
        out_shape=[
            jax.ShapeDtypeStruct(layer.shape, layer.dtype),
            jax.ShapeDtypeStruct(cache.shape, cache.dtype),
        ],
        in_specs=[pl.BlockSpec(memory_space=pltpu.SMEM), HBM, HBM, VMEM, HBM, HBM],
        out_specs=[VMEM, HBM],
        scratch_shapes=[
            pltpu.VMEM((pages, 2, PAGE, WIDTH), jnp.bfloat16),
            pltpu.VMEM((16, WIDTH), jnp.bfloat16),
            pltpu.VMEM(draft.shape, draft.dtype),
            pltpu.VMEM(patch.shape, patch.dtype),
            pltpu.SemaphoreType.DMA((2 * pages,)),
            pltpu.SemaphoreType.DMA((2 * pages,)),
            pltpu.SemaphoreType.DMA,
            pltpu.SemaphoreType.DMA((2,)),
        ],
        compiler_params=pltpu.CompilerParams(vmem_limit_bytes=60 * 1024 * 1024),
        name="draft_and_append",
    )(tables, gathered, cache, layer, draft, patch)


PAIR = 2 * TREE
LINES = 8 * PAIR


def attend_scratch(pages):
    return [
        pltpu.VMEM((2, pages + 1, PAGE, WIDTH), jnp.bfloat16),
        pltpu.VMEM((BLK, TREE + 16, WIDTH), jnp.bfloat16),
        pltpu.SemaphoreType.DMA((2 * pages + 1,)),
        pltpu.VMEM((8, PAIR, 256), jnp.bfloat16),
        pltpu.VMEM((8, PAIR, 256), jnp.bfloat16),
        pltpu.VMEM((TREE, PAGE), jnp.float32),
        pltpu.VMEM((LINES, 128), jnp.float32),
        pltpu.VMEM((LINES, 128), jnp.bfloat16),
        pltpu.VMEM((LINES, 128), jnp.float32),
        pltpu.VMEM((LINES, 128), jnp.float32),
        pltpu.VMEM((LINES, 128), jnp.float32),
        pltpu.VMEM((8, PAIR, 256), jnp.float32),
        pltpu.VMEM((pages + 2, TREE, WIDTH), jnp.bfloat16),
        pltpu.VMEM((pages + 2, TREE, 128), jnp.float32),
    ]


def attend_steps(tables, query_ref, cache_ref, proj_ref, marks_ref, bufs, pause):
    (kept, query, load, ones, masked, marks, scores, weights, tops, dens, scales, acc, sums, stats) = bufs
    pages = cache_ref.shape[2] // PAGE
    factor = math.log2(math.e) / math.sqrt(HD)
    lanes = lax.broadcasted_iota(jnp.int32, (TREE, 128), 1)
    columns = lax.broadcasted_iota(jnp.int32, (TREE, 256), 1)
    copies = [
        pltpu.make_async_copy(
            cache_ref.at[0, i, pl.ds(p * PAGE, PAGE)], kept.at[i, p], load.at[i * pages + p]
        )
        for i in range(2)
        for p in range(pages)
    ]
    copies.append(pltpu.make_async_copy(query_ref, query, load.at[2 * pages]))
    for copy in copies:
        copy.start()
    yield

    def inside(w, i):
        begin = window(w)[1] + HD * i
        return (columns >= begin) & (columns < begin + HD)

    for w in range(8):
        for i in range(2):
            ones[w, pl.ds(TREE * i, TREE)] = (
                inside(w, i).astype(jnp.float32).astype(jnp.bfloat16)
            )
    for i in range(2):
        kept[i, pages, pl.ds(0, TREE)] = proj_ref[:, pl.ds((1 + i) * WIDTH, WIDTH)]
        kept[i, pages, pl.ds(TREE, PAGE - TREE)] = jnp.zeros((PAGE - TREE, WIDTH), jnp.bfloat16)
    marks[...] = jnp.zeros_like(marks)
    marks[:, pl.ds(0, TREE)] = marks_ref[...]
    tops[...] = jnp.full_like(tops, LOWEST)
    dens[...] = jnp.zeros_like(dens)
    acc[...] = jnp.zeros_like(acc)
    sums[pages + 1] = jnp.zeros((TREE, WIDTH), jnp.bfloat16)
    stats[pages + 1] = jnp.where(lanes < 64, LOWEST, 0.0)
    for copy in copies:
        copy.wait()

    def step(j, carry):
        start, length, owner = tables[1, j], tables[2, j], tables[4, j]
        page, fresh, tree = tables[5, j], tables[6, j] > 0, tables[8, j] > 0
        for w in range(8):
            picked = query[owner, pl.ds(0, TREE), pl.ds(window(w)[0], 256)]
            for i in range(2):
                half = pl.ds(TREE * i, TREE)
                masked[w, half] = picked * ones[w, half]
        for w in range(8):
            scores[pl.ds(PAIR * w, PAIR), :] = dot_t(
                masked[w], kept[0, page, :, pl.ds(window(w)[0], 256)]
            )
        near = (lanes + start < length).astype(jnp.float32)
        seen = jnp.where(tree, marks[...], near)
        shown = jnp.concatenate([seen] * 4, axis=0) > 0.5
        for part in range(4):
            rows = pl.ds(2 * PAIR * part, 2 * PAIR)
            part_scores = jnp.where(shown, scores[rows, :] * factor, LOWEST)
            before = jnp.where(fresh, LOWEST, tops[rows, :])
            top = jnp.maximum(before, jnp.ceil(jnp.max(part_scores, axis=1, keepdims=True)))
            weight = jnp.where(shown, jnp.exp2(part_scores - top), 0.0)
            scale = jnp.where(fresh, 0.0, jnp.exp2(before - top))
            tops[rows, :] = top
            scales[rows, :] = scale
            dens[rows, :] = dens[rows, :] * scale + jnp.sum(weight, axis=1, keepdims=True)
            weights[rows, :] = weight.astype(jnp.bfloat16)
        carried = None
        for w in range(8):
            rows = pl.ds(PAIR * w, PAIR)
            added = jnp.dot(
                weights[rows, :],
                kept[1, page, :, pl.ds(window(w)[0], 256)],
                preferred_element_type=jnp.float32,
            )
            scale = scales[rows, :]
            total = acc[w] * jnp.concatenate([scale, scale], axis=1) + added
            acc[w] = total
            picked = jnp.where(
                inside(w, 0), total[:TREE], jnp.where(inside(w, 1), total[TREE:], 0.0)
            )
            head = picked[:, :128]
            if w % 4:
                head = head + carried
            carried = picked[:, 128:]
            sums[j, :, pl.ds(window(w)[0], 128)] = head.astype(jnp.bfloat16)
            if w % 4 == 3:
                sums[j, :, pl.ds(window(w)[0] + 128, 128)] = carried.astype(jnp.bfloat16)
        row = jnp.full((TREE, 128), LOWEST, jnp.float32)
        for head in range(H):
            rows = pl.ds(TREE * head, TREE)
            row = jnp.where(lanes == head, tops[rows, :], row)
            row = jnp.where(lanes == 64 + head, dens[rows, :], row)
        stats[j] = row
        return carry

    first = 0
    for last in pause + (pages + 1,):
        lax.fori_loop(first, last, step, 0)
        first = last
        if last <= pages:
            yield


PAIR_ORDER = (
    [(2, b) for b in range(4)]
    + [(1, 2), (1, 3), (-1, 0), (-1, 1)]
    + [(1, 0), (1, 1), (-1, 2), (-1, 3)]
    + [(0, b) for b in range(4)]
)
REDUCE = numbered(
    [f"{kind}{i}{s}" for kind, n in (("P", 16), ("T", 4), ("L", 4), ("R", 4)) for i in range(n) for s in "ns"]
    + [f"{kind}{s}" for kind in ("t0", "t1", "l", "r") for s in "ns"]
)


PAUSES = (3, 6, 9, 12, 14)
ADVANCES = (0, 6, 10, 14, 18, 22)


def split_stats(stats):
    return stats, pltpu.roll(stats, 64, 1)


def combine(parts, spread):
    stats = [split_stats(s) for _, s in parts]
    lanes = lax.broadcasted_iota(jnp.int32, stats[0][0].shape, 1)
    top = stats[0][0]
    for s, _ in stats[1:]:
        top = jnp.maximum(top, s)
    total = None
    num = None
    for (n, _), (s, d) in zip(parts, stats):
        scale = jnp.where(lanes < H, jnp.exp2(jnp.minimum(s - top, 0.0)), 0.0)
        wide = jnp.dot(scale.astype(jnp.bfloat16), spread, preferred_element_type=jnp.float32)
        d = d * scale
        n = n.astype(jnp.float32) * wide
        total = d if total is None else total + d
        num = n if num is None else num + n
    return num, top, total


def join_stats(top, total):
    lanes = lax.broadcasted_iota(jnp.int32, top.shape, 1)
    return jnp.where(lanes < H, top, pltpu.roll(jnp.where(lanes < H, total, 0.0), 64, 1))


def reduce_steps(spot, tables, sums, stats, out, spread, bufs, ssem, rsem):
    pair_n, pair_s, work_n, work_s, thru_n, thru_s, left_n, left_s, right_n, right_s = bufs[:10]
    fin_n, fin_s, two_n, two_s, out_n, out_s = bufs[10:]
    sent = {}
    send = sender(sent, ssem, rsem, REDUCE)

    def put(event, src_n, src_s, dst_n, dst_s, who):
        send(event + "n", src_n, dst_n, who)
        send(event + "s", src_s, dst_s, who)

    def took(event):
        sent[event + "n"].wait_recv()
        sent[event + "s"].wait_recv()

    right, left = spot.at(1, 0), spot.at(-1, 0)
    up, down = spot.at(0, 1), spot.at(0, -1)
    other = (1 - spot.core) * 16
    mine = spot.core * 16
    for i, (a, b) in enumerate(PAIR_ORDER):
        found = tables[9, other + spot.chip(b, a)]
        out_n[i] = sums[found]
        out_s[i] = stats[found]
        put(f"P{i}", out_n.at[i], out_s.at[i], pair_n.at[i], pair_s.at[i], spot.sibling)
    yield

    def store(dst_n, dst_s, parts):
        n, top, total = combine(parts, spread())
        dst_n[...] = n.astype(jnp.bfloat16)
        dst_s[...] = join_stats(top, total)

    place = {pair: i for i, pair in enumerate(PAIR_ORDER)}
    for i, (a, b) in enumerate(PAIR_ORDER):
        took(f"P{i}")
        found = tables[9, mine + spot.chip(a, b)]
        store(
            work_n.at[i], work_s.at[i], [(sums[found], stats[found]), (pair_n[i], pair_s[i])]
        )
        if a == 2:
            put(
                f"T{b}", work_n.at[i], work_s.at[i], thru_n.at[b], thru_s.at[b],
                right if b < 2 else left,
            )
        elif (a == 1 and b >= 2):
            put(f"L{b}", work_n.at[i], work_s.at[i], left_n.at[b], left_s.at[b], right)
        elif (a == -1 and b < 2):
            put(f"R{b}", work_n.at[i], work_s.at[i], right_n.at[b], right_s.at[b], left)
        yield
    for b in range(4):
        took(f"T{b}")
        a = 1 if b < 2 else -1
        i = place[(a, b)]
        store(
            work_n.at[i], work_s.at[i], [(work_n[i], work_s[i]), (thru_n[b], thru_s[b])]
        )
        if a == 1:
            put(f"L{b}", work_n.at[i], work_s.at[i], left_n.at[b], left_s.at[b], right)
        else:
            put(f"R{b}", work_n.at[i], work_s.at[i], right_n.at[b], right_s.at[b], left)
        yield
    cuts = (pl.ds(0, 32), pl.ds(32, 16))
    for b in (2, 1, 3, 0):
        took(f"L{b}")
        took(f"R{b}")
        i = place[(0, b)]
        store(
            fin_n.at[b],
            fin_s.at[b],
            [(work_n[i], work_s[i]), (left_n[b], left_s[b]), (right_n[b], right_s[b])],
        )
        if b == 2:
            for half, who in ((0, up), (1, down)):
                put(
                    f"t{half}",
                    fin_n.at[2, cuts[half]],
                    fin_s.at[2, cuts[half]],
                    two_n.at[0, cuts[half]],
                    two_s.at[0, cuts[half]],
                    who,
                )
        yield
    for half, b in ((0, 1), (1, 3)):
        took(f"t{half}")
        rows = cuts[half]
        store(
            fin_n.at[b, rows],
            fin_s.at[b, rows],
            [(fin_n[b, rows], fin_s[b, rows]), (two_n[0, rows], two_s[0, rows])],
        )
        if b == 1:
            put("l", fin_n.at[1], fin_s.at[1], two_n.at[1], two_s.at[1], up)
        else:
            put("r", fin_n.at[3], fin_s.at[3], two_n.at[2], two_s.at[2], down)
        yield
    took("l")
    took("r")
    n, top, total = combine(
        [(fin_n[0], fin_s[0]), (two_n[1], two_s[1]), (two_n[2], two_s[2])], spread()
    )
    lanes = lax.broadcasted_iota(jnp.int32, total.shape, 1)
    inverse = jnp.where(lanes < H, 1.0 / jnp.where(lanes < H, total, 1.0), 0.0)
    wide = jnp.dot(
        inverse,
        spread().astype(jnp.float32),
        preferred_element_type=jnp.float32,
        precision=lax.Precision.HIGHEST,
    )
    out[...] = (n * wide).astype(jnp.bfloat16)
    for event in REDUCE:
        sent[event].wait_send()


def attend_and_reduce(tables, gathered, cache, projected, marks, spread, shards, collective_id):
    count = len(shards)
    pages = cache.shape[2] // PAGE

    def block(n):
        return [
            pltpu.VMEM((n, TREE, WIDTH), jnp.bfloat16),
            pltpu.VMEM((n, TREE, 128), jnp.float32),
        ]

    parts = [
        [pltpu.SemaphoreType.DMA((len(REDUCE),))] * 2,
        gather_sems(count),
        attend_scratch(pages),
        block(16) + block(16) + block(4) + block(4) + block(4) + block(4) + block(3) + block(16),
    ]

    def kernel(tables_ref, query_ref, cache_ref, proj_ref, marks_ref, spread_ref, *refs):
        ins = refs[:count]
        out = refs[count]
        outs = refs[count + 1 : 2 * count + 1]
        left = list(refs[2 * count + 1 :])
        scratch = []
        for part in parts:
            scratch.append(left[: len(part)])
            left = left[len(part) :]
        (ssem, rsem), gather_scratch, attend_bufs, reduce_bufs = scratch
        spot = Spot()
        work = attend_steps(
            tables_ref, query_ref, cache_ref, proj_ref, marks_ref, attend_bufs, PAUSES
        )
        next(work)
        greet_plane(spot)
        gathers = gather_all(spot, ins, outs, *gather_scratch)

        def advance():
            for one in gathers:
                next(one, None)

        advance()
        for _ in work:
            advance()
        for i, _ in enumerate(
            reduce_steps(
                spot,
                tables_ref,
                attend_bufs[-2],
                attend_bufs[-1],
                out,
                lambda: spread_ref[...],
                reduce_bufs,
                lambda e: ssem.at[e],
                lambda e: rsem.at[e],
            )
        ):
            if i in ADVANCES:
                advance()
        run_all(gathers)

    return pl.pallas_call(
        kernel,
        out_shape=[jax.ShapeDtypeStruct((TREE, WIDTH), jnp.bfloat16)]
        + [jax.ShapeDtypeStruct((BLK,) + s.shape, s.dtype) for s in shards],
        in_specs=[pl.BlockSpec(memory_space=pltpu.SMEM), ANY, ANY, VMEM, VMEM, VMEM] + [VMEM] * count,
        out_specs=[VMEM] + [ANY] * count,
        scratch_shapes=[ref for part in parts for ref in part],
        compiler_params=pltpu.CompilerParams(
            collective_id=collective_id,
            has_side_effects=True,
            vmem_limit_bytes=52 * 1024 * 1024,
        ),
        name="attend_and_reduce",
    )(tables, gathered, cache, projected, marks, spread, *shards)


RETURN = numbered(["TA", "TB", "L", "R", "OA", "OB"])


def column_kernel(exchange):
    def kernel(block, out, thru, ssem, rsem, lsem):
        at = lax.axis_index("req")
        above, far, below = (at + 1) % 4, (at + 2) % 4, (at + 3) % 4
        barrier = pltpu.get_barrier_semaphore()
        for who in (above, below):
            pl.semaphore_signal(barrier, inc=1, device_id={"req": who}, device_id_type=MESH)
        pl.semaphore_wait(barrier, 2)
        sent = {}
        upper, lower = pl.ds(0, 32), pl.ds(32, TREE - 32)

        def put(event, src, dst, who):
            copy = pltpu.make_async_remote_copy(
                src_ref=src,
                dst_ref=dst,
                send_sem=ssem.at[RETURN[event]],
                recv_sem=rsem.at[RETURN[event]],
                device_id={"req": who},
                device_id_type=MESH,
            )
            copy.start()
            sent[event] = copy

        if exchange:
            put("TA", block.at[far, upper], thru.at[upper], above)
            put("TB", block.at[far, lower], thru.at[lower], below)
        put("L", block.at[above] if exchange else block, out.at[at], above)
        put("R", block.at[below] if exchange else block, out.at[at], below)
        local = pltpu.make_async_copy(block.at[at] if exchange else block, out.at[at], lsem)
        local.start()
        sent["TA" if exchange else "L"].wait_recv()
        put("OA", thru.at[upper] if exchange else out.at[below, upper], out.at[below, upper], above)
        sent["TB" if exchange else "R"].wait_recv()
        put("OB", thru.at[lower] if exchange else out.at[above, lower], out.at[above, lower], below)
        local.wait()
        for event in ("L", "R", "OA", "OB") if exchange else ("OA", "OB"):
            sent[event].wait_recv()
        for copy in sent.values():
            copy.wait_send()

    return kernel


def over_column(block, exchange, collective_id, name):
    shape = block.shape if exchange else (4,) + block.shape
    return pl.pallas_call(
        column_kernel(exchange),
        out_shape=jax.ShapeDtypeStruct(shape, block.dtype),
        in_specs=[VMEM],
        out_specs=VMEM,
        scratch_shapes=[
            pltpu.VMEM(block.shape[-2:], block.dtype),
            pltpu.SemaphoreType.DMA((len(RETURN),)),
            pltpu.SemaphoreType.DMA((len(RETURN),)),
            pltpu.SemaphoreType.DMA,
        ],
        compiler_params=pltpu.CompilerParams(
            collective_id=collective_id, has_side_effects=True
        ),
        name=name,
    )(block)


def on_device(
    tree_input,
    cache,
    page_table,
    lengths,
    parents,
    accept_leaf,
    w_qkv,
    w_out,
    w_up,
    w_down,
    w_draft,
    w_patch,
):
    width = WIDTH
    pool_pages = cache.shape[2] // PAGE
    draft_mine = lax.dynamic_index_in_dim(
        w_draft.transpose(0, 2, 1), lax.axis_index("req"), 0, keepdims=False
    )
    qkv, patch, normed, tables, pages, marks, picker = prepare(
        w_qkv.T, w_patch.T, tree_input, page_table, lengths, accept_leaf, parents, pool_pages
    )
    projected = dot_t(normed, qkv.reshape(3 * width, width)).astype(jnp.bfloat16)
    send_rows = jnp.dot(
        picker[:8], projected[:, width:], preferred_element_type=jnp.float32
    ).astype(jnp.bfloat16)
    pack = jnp.concatenate([projected[:, :width], send_rows[:, :width], send_rows[:, width:]])
    gathered, *full_early = all_gather(
        [pack, w_out.T, ],
        {0: QUERY_CUTS},
        2,
        "gather_query",
    )
    spread = (
        jnp.arange(128, dtype=jnp.int32)[:, None]
        == jnp.arange(width, dtype=jnp.int32)[None, :] // HD
    ).astype(jnp.bfloat16)
    attended, *full_late = attend_and_reduce(
        tables,
        gathered,
        cache,
        projected,
        marks,
        spread,
        [w_up.T, w_down, draft_mine],
        3,
    )
    full_out, full_up, full_down, full_draft, patch = (
        w.reshape(width, width) for w in (*full_early, *full_late, patch)
    )
    proj = dot_t(attended, full_out).astype(jnp.bfloat16)
    mid = (tree_input.astype(jnp.float32) + proj.astype(jnp.float32)).astype(jnp.bfloat16)
    hidden = jax.nn.gelu(dot_t(rms_rows(mid), full_up)).astype(jnp.bfloat16)
    feedforward = jnp.dot(hidden, full_down, preferred_element_type=jnp.float32)
    layer_out = (mid.astype(jnp.float32) + feedforward).astype(jnp.bfloat16)
    rows = over_column(layer_out, False, 4, "gather_rows").reshape(4 * TREE, width)
    head, cache_new = draft_and_append(pages, gathered, cache, rows, full_draft, patch)
    drafts = over_column(head.reshape(4, TREE, width), True, 5, "return_rows")
    return (layer_out, drafts, cache_new)


def solution(mesh):
    in_specs = (
        P(("req", "blk"), None),
        P("req", None, "blk", None),
        P("req", None),
        P("req", None),
        P(("req", "blk"), None),
        P("req", None),
        P(None, "blk"),
        P(None, "blk"),
        P(None, "blk"),
        P("blk", None),
        P(None, None, "blk"),
        P(None, "req"),
    )
    out_specs = (
        P(("req", "blk"), None),
        P(None, ("req", "blk"), None),
        P("req", None, "blk", None),
    )
    return jax.shard_map(
        on_device, mesh=mesh, in_specs=in_specs, out_specs=out_specs, check_vma=False
    )
```

```python
import math

import jax
import jax.numpy as jnp
from jax import lax
from jax.experimental import pallas as pl
from jax.experimental.pallas import tpu as pltpu
from jax.sharding import PartitionSpec as P

H = 16
HD = 80
TREE = 48
DEPTH = 5
PAGE = 128
BLK = 32
WIDTH = H * HD

EPS = 1e-06
LOWEST = -8388608.0
LEVEL_START = (0, 1, 5, 15, 30, 48)
MESH = pl.DeviceIdType.MESH
ROWSLOT = ((0, 0), (-1, 0), (1, 0), (2, 0))


def rms_rows(values):
    wide = values.astype(jnp.float32)
    return (wide * lax.rsqrt(jnp.mean(wide * wide, axis=-1, keepdims=True) + EPS)).astype(
        jnp.bfloat16
    )


def dot_t(left, right):
    return lax.dot_general(
        left, right, (((1,), (1,)), ((), ())), preferred_element_type=jnp.float32
    )


class Spot:
    def __init__(self):
        self.me = lax.axis_index("blk")
        self.core = self.me % 2
        x = (self.me // 2) % 4
        y = self.me // 8
        self.one = x + self.core * (y - x)
        self.two = y + self.core * (x - y)
        self.sibling = self.me + 1 - 2 * self.core

    def at(self, a, b):
        return self.core + 2 * self.chip(a, b)

    def chip(self, a, b):
        one = (self.one + a + 4) % 4
        two = (self.two + b + 4) % 4
        return (1 + 3 * self.core) * one + (4 - 3 * self.core) * two


def greet_plane(spot, column=False):
    barrier = pltpu.get_barrier_semaphore()
    for who in (spot.at(1, 0), spot.at(-1, 0), spot.at(0, 1), spot.at(0, -1), spot.sibling):
        pl.semaphore_signal(barrier, inc=1, device_id={"blk": who}, device_id_type=MESH)
    if column:
        at = lax.axis_index("req")
        for d in (1, 3):
            pl.semaphore_signal(
                barrier, inc=1, device_id={"req": (at + d) % 4}, device_id_type=MESH
            )
    pl.semaphore_wait(barrier, 7 if column else 5)


def numbered(names):
    return {name: i for i, name in enumerate(names)}


GATHER = numbered(
    ["L", "R", "OA", "OB"]
    + [f"{kind}{k}" for k in range(4) for kind in ("D", "U", "PA", "PB")]
    + [f"S{k}" for k in range(16)]
)


def sender(sent, ssem, rsem, events):
    def put(event, src, dst, who):
        copy = pltpu.make_async_remote_copy(
            src_ref=src,
            dst_ref=dst,
            send_sem=ssem(events[event]),
            recv_sem=rsem(events[event]),
            device_id={"blk": who},
            device_id_type=MESH,
        )
        copy.start()
        sent[event] = copy

    return put


def gather_steps(spot, shard, view, ssem, rsem, lsem, cut, ready=None):
    sent = {}
    send = sender(sent, ssem, rsem, GATHER)

    def put(event, src, slot, who, half=None):
        dst = view(slot)
        if half is not None:
            src, dst = cut(src, half), cut(dst, half)
        send(event, src, dst, who)

    left_over = list(range(16))

    def done(*slots):
        if ready is not None:
            for slot in slots:
                ready(slot)

    def from_sibling(*events):
        for k in events:
            left_over.remove(k)
            sent[f"S{k}"].wait_recv()
            a, b = ROWSLOT[k % 4][0], (0, -1, 1, 2)[k // 4]
            done(1 - spot.core + 2 * spot.chip(b, a))

    def early(*events):
        if ready is not None:
            from_sibling(*events)

    right, left = spot.at(1, 0), spot.at(-1, 0)
    up, down = spot.at(0, 1), spot.at(0, -1)
    local = pltpu.make_async_copy(shard, view(spot.me), lsem)
    local.start()
    put("L", shard, spot.me, right)
    put("R", shard, spot.me, left)
    put("D0", shard, spot.me, up)
    put("U0", shard, spot.me, down)
    put("S0", shard, spot.me, spot.sibling)
    yield
    for k, event in ((1, "L"), (2, "R")):
        slot = spot.at(*ROWSLOT[k])
        sent[event].wait_recv()
        if k == 1:
            put("OA", view(slot), slot, right, 0)
        else:
            put("OB", view(slot), slot, left, 1)
        put(f"D{k}", view(slot), slot, up)
        put(f"U{k}", view(slot), slot, down)
        put(f"S{k}", view(slot), slot, spot.sibling)
        done(slot)
        early(k - 1)
        yield

    def column(k):
        a = ROWSLOT[k][0]
        slot = spot.at(a, -1)
        sent[f"D{k}"].wait_recv()
        put(f"PA{k}", view(slot), slot, up, 0)
        put(f"S{4 + k}", view(slot), slot, spot.sibling)
        slot = spot.at(a, 1)
        sent[f"U{k}"].wait_recv()
        put(f"PB{k}", view(slot), slot, down, 1)
        put(f"S{8 + k}", view(slot), slot, spot.sibling)
        done(spot.at(a, -1), slot)

    column(0)
    early(2)
    yield
    sent["OA"].wait_recv()
    sent["OB"].wait_recv()
    slot = spot.at(2, 0)
    put("D3", view(slot), slot, up)
    put("U3", view(slot), slot, down)
    put("S3", view(slot), slot, spot.sibling)
    done(slot)
    early(4, 8)
    yield
    for k in (1, 2, 3):
        column(k)
        early(*((3,), (5, 9), (6, 10))[k - 1])
        yield
    for k in range(4):
        slot = spot.at(ROWSLOT[k][0], 2)
        sent[f"PA{k}"].wait_recv()
        sent[f"PB{k}"].wait_recv()
        put(f"S{12 + k}", view(slot), slot, spot.sibling)
        done(slot)
        early(*((7, 11) if k == 0 else (11 + k,)))
        yield
    from_sibling(*list(left_over))
    local.wait()
    for event in GATHER:
        sent[event].wait_send()


def run_all(steps):
    steps = list(steps)
    while steps:
        alive = []
        for step in steps:
            try:
                next(step)
                alive.append(step)
            except StopIteration:
                pass
        steps = alive


def row_halves(rows, tile):
    first = ((rows // 2) + tile - 1) // tile * tile

    def cut(ref, half):
        return ref.at[pl.ds(0, first)] if half == 0 else ref.at[pl.ds(first, rows - first)]

    return cut


def gather_all(spot, ins, outs, ssem, rsem, lsem, cuts=None, ready=None):
    count = len(GATHER)
    steps = []
    for i, (shard, out) in enumerate(zip(ins, outs)):
        first = 0
        for rows in (cuts or {}).get(i, (shard.shape[0],)):
            piece = pl.ds(first, rows)
            at = len(steps) * count
            steps.append(
                gather_steps(
                    spot,
                    shard.at[piece],
                    lambda slot, out=out, piece=piece: out.at[slot, piece],
                    lambda e, at=at: ssem.at[at + e],
                    lambda e, at=at: rsem.at[at + e],
                    lsem.at[len(steps)],
                    row_halves(rows, 16 if ready else 8),
                    (lambda slot: None) if ready else None,
                )
                if ready is None or first + rows < shard.shape[0]
                else gather_steps(
                    spot,
                    shard.at[piece],
                    lambda slot, out=out, piece=piece: out.at[slot, piece],
                    lambda e, at=at: ssem.at[at + e],
                    lambda e, at=at: rsem.at[at + e],
                    lsem.at[len(steps)],
                    row_halves(rows, 16),
                    ready,
                )
            )
            first += rows
    return steps


def gather_sems(arrays):
    return [
        pltpu.SemaphoreType.DMA((arrays * len(GATHER),)),
        pltpu.SemaphoreType.DMA((arrays * len(GATHER),)),
        pltpu.SemaphoreType.DMA((arrays,)),
    ]


COLUMN = numbered(["L", "R", "OA", "OB", "S1", "S2", "S3"])


def column_steps(spot, shard, out, ssem, rsem, lsem):
    at = lax.axis_index("req")
    above, below = (at + 1) % 4, (at + 3) % 4
    half = shard.shape[0] // 2
    base = spot.core * half
    rows = pl.ds(pl.multiple_of(base, 8), half)
    parts = [pl.ds(pl.multiple_of(base + i * (half // 2), 8), half // 2) for i in range(2)]
    sent = {}

    def put(event, src, slot, part, device):
        copy = pltpu.make_async_remote_copy(
            src_ref=src,
            dst_ref=out.at[slot, part],
            send_sem=ssem.at[COLUMN[event]],
            recv_sem=rsem.at[COLUMN[event]],
            device_id=device,
            device_id_type=MESH,
        )
        copy.start()
        sent[event] = copy

    local = pltpu.make_async_copy(shard, out.at[at], lsem)
    local.start()
    put("L", shard.at[rows], at, rows, {"req": above})
    put("R", shard.at[rows], at, rows, {"req": below})
    for _ in range(2):
        yield
    sent["L"].wait_recv()
    put("OA", out.at[below, parts[0]], below, parts[0], {"req": above})
    put("S1", out.at[below, rows], below, rows, {"blk": spot.sibling})
    sent["R"].wait_recv()
    put("OB", out.at[above, parts[1]], above, parts[1], {"req": below})
    put("S2", out.at[above, rows], above, rows, {"blk": spot.sibling})
    for _ in range(3):
        yield
    sent["OA"].wait_recv()
    sent["OB"].wait_recv()
    far = (at + 2) % 4
    put("S3", out.at[far, rows], far, rows, {"blk": spot.sibling})
    yield
    local.wait()
    for event in ("S1", "S2", "S3"):
        sent[event].wait_recv()
    for event in COLUMN:
        sent[event].wait_send()


ANY = pl.BlockSpec(memory_space=pl.ANY)
HBM = pl.BlockSpec(memory_space=pltpu.HBM)
VMEM = pl.BlockSpec(memory_space=pltpu.VMEM)


def all_gather(shards, cuts, collective_id, name):
    count = len(shards)

    def kernel(*refs):
        spot = Spot()
        greet_plane(spot)
        run_all(gather_all(spot, refs[:count], refs[count : 2 * count], *refs[2 * count :], cuts))

    return pl.pallas_call(
        kernel,
        out_shape=[jax.ShapeDtypeStruct((BLK,) + s.shape, s.dtype) for s in shards],
        in_specs=[VMEM] * count,
        out_specs=[ANY] * count,
        scratch_shapes=gather_sems(count + sum(len(rows) - 1 for rows in cuts.values())),
        compiler_params=pltpu.CompilerParams(collective_id=collective_id, has_side_effects=True),
        name=name,
    )(*shards)


QKV_CUTS = (48, 48, 24)
QUERY_CUTS = (32, 32)


def iota(shape, dim):
    return lax.broadcasted_iota(jnp.int32, shape, dim)


def to_column(row):
    n = row.shape[1]
    return jnp.sum(jnp.where(iota((n, n), 0) == iota((n, n), 1), row, 0), axis=1, keepdims=True)


def to_row(column):
    n = column.shape[0]
    return jnp.sum(jnp.where(iota((n, n), 0) == iota((n, n), 1), column, 0), axis=0, keepdims=True)


def tree_marks(parent_row, leaf):
    square = (TREE, TREE)
    climb = (to_column(parent_row) == iota(square, 1)).astype(jnp.float32)
    current = (iota(square, 0) == iota(square, 1)).astype(jnp.float32)
    marks = current
    for _ in range(DEPTH - 1):
        current = jnp.dot(current, climb, preferred_element_type=jnp.float32)
        marks = jnp.maximum(marks, current)
    chosen = jnp.sum(jnp.where(iota(square, 0) == leaf, marks, 0.0), axis=0, keepdims=True)
    upto = jnp.where(iota(square, 0) <= iota(square, 1), to_column(chosen), 0.0)
    nth = (jnp.sum(upto, axis=0, keepdims=True) - 1.0).astype(jnp.int32)
    picker = (chosen > 0.5) & (nth == iota((16, TREE), 0))
    return marks, picker.astype(jnp.float32)


def page_tables(page_row, length_row, leaf_row, myself, pool_pages):
    requests = length_row.shape[1]
    npages = (length_row + (DEPTH + PAGE - 1)) // PAGE
    square = (requests, requests)
    ends = jnp.sum(
        jnp.where(iota(square, 0) <= iota(square, 1), to_column(npages), 0), axis=0, keepdims=True
    )
    offsets = ends - npages
    my_end = jnp.sum(jnp.where(iota((1, requests), 1) == myself, ends, 0), axis=1, keepdims=True)
    accepted = 1 + sum((leaf_row >= first).astype(jnp.int32) for first in LEVEL_START[1:-1])
    lines = 24
    line = iota((lines, 1), 0)
    slots = page_row.shape[1]
    located = page_row == myself * pool_pages + iota((lines, slots), 0)
    where_at = jnp.sum(jnp.where(located, iota((lines, slots), 1), 0), axis=1, keepdims=True)
    owner = jnp.sum((ends <= where_at).astype(jnp.int32), axis=1, keepdims=True)
    hot = owner == iota((lines, requests), 1)

    def of_owner(row):
        return jnp.sum(jnp.where(hot, row, 0), axis=1, keepdims=True)

    is_tree = line == pool_pages
    spare = line > pool_pages
    owner_or_me = jnp.where(is_tree, myself, jnp.minimum(owner, requests - 1))
    place = owner_or_me % 2 * (requests // 2) + owner_or_me // 2
    start = jnp.where(is_tree, 0, (where_at - of_owner(offsets)) * PAGE)
    length = jnp.where(is_tree, 0, of_owner(length_row))
    count = jnp.where(is_tree, 0, of_owner(accepted))
    spots = jnp.where(is_tree, 2 * my_end - 1, jnp.where(spare, 4 * slots + line, 2 * where_at))
    rank = jnp.sum((to_row(spots) < spots).astype(jnp.int32), axis=1, keepdims=True)
    wide = (lines, 128)

    def in_order(column):
        return jnp.sum(jnp.where(rank == iota(wide, 1), column, 0), axis=0, keepdims=True)

    def as_it_lies(column):
        return jnp.sum(jnp.where(line == iota(wide, 1), column, 0), axis=0, keepdims=True)

    columns = [place, start, length, count, owner_or_me, line]
    rows = [in_order(column) for column in columns]
    lane = iota((1, 128), 1)
    fresh = ((rows[4] != pltpu.roll(rows[4], 1, 1)) | (lane == 0)).astype(jnp.int32)
    last = jnp.max(
        jnp.where((place == iota(wide, 1)) & jnp.logical_not(spare), rank, -1),
        axis=0,
        keepdims=True,
    )
    last = jnp.where(last < 0, pool_pages + 1, last)
    rows += [fresh, fresh, in_order(is_tree.astype(jnp.int32)), last]
    return rows, [as_it_lies(column) for column in (owner_or_me, start, length, count)]


def prepare(shard, patch, tree_input, page_row, length_row, leaf_row, parent_row, pool_pages):
    def kernel(
        shard_ref, patch_ref, x_ref, page_ref, length_ref, leaf_ref, parent_ref,
        full_patch_ref, projected_ref, pack_ref, steps_ref, pages_ref, marks_ref,
        full_ref, normed, parts, joined, *scratch,
    ):
        spot = Spot()
        columns = shard_ref.shape[0]
        greet_plane(spot, True)

        def project(slot):
            parts[slot, :, pl.ds(0, columns)] = dot_t(normed[...], full_ref[slot])

        steps = gather_all(
            spot, [shard_ref], [full_ref], *scratch[:3], {0: QKV_CUTS}, project
        )
        steps.append(column_steps(spot, patch_ref, full_patch_ref, *scratch[3:]))
        for one in steps:
            next(one)
        normed[...] = rms_rows(x_ref[...])
        parts[spot.me, :, pl.ds(0, columns)] = dot_t(normed[...], shard_ref[...])
        leaf = jnp.sum(
            jnp.where(iota(leaf_ref.shape, 1) == spot.me, leaf_ref[...], 0), axis=1, keepdims=True
        )
        marks_ref[...], picker = tree_marks(parent_ref[...], leaf)
        in_order, as_they_lie = page_tables(
            page_ref[...], length_ref[...], leaf_ref[...], spot.me, pool_pages
        )
        for k, row in enumerate(in_order):
            steps_ref[pl.ds(k, 1), :] = row
        for k, row in enumerate(as_they_lie):
            pages_ref[pl.ds(k, 1), :] = row
        run_all(steps)
        for slot in range(BLK):
            joined[:, pl.ds(columns * slot, columns)] = parts[slot, :, pl.ds(0, columns)]
        projected_ref[...] = joined[...].astype(jnp.bfloat16)
        pack_ref[pl.ds(0, TREE), :] = projected_ref[:, pl.ds(0, WIDTH)]
        picked = jnp.dot(
            picker.astype(jnp.bfloat16),
            projected_ref[:, pl.ds(WIDTH, 2 * WIDTH)],
            preferred_element_type=jnp.float32,
        )
        pack_ref[pl.ds(TREE, 16), :] = jnp.concatenate(
            [picked[:8, :WIDTH], picked[:8, WIDTH:]], axis=0
        ).astype(jnp.bfloat16)

    return pl.pallas_call(
        kernel,
        out_shape=[
            jax.ShapeDtypeStruct((4,) + patch.shape, patch.dtype),
            jax.ShapeDtypeStruct((TREE, 3 * WIDTH), jnp.bfloat16),
            jax.ShapeDtypeStruct((TREE + 16, WIDTH), jnp.bfloat16),
            jax.ShapeDtypeStruct((10, 128), jnp.int32),
            jax.ShapeDtypeStruct((4, 128), jnp.int32),
            jax.ShapeDtypeStruct((TREE, TREE), jnp.float32),
        ],
        in_specs=[VMEM] * 7,
        out_specs=[ANY] + [VMEM] * 5,
        scratch_shapes=[
            pltpu.VMEM((BLK,) + shard.shape, shard.dtype),
            pltpu.VMEM(tree_input.shape, jnp.bfloat16),
            pltpu.VMEM((BLK, TREE, 128), jnp.float32),
            pltpu.VMEM((TREE, 3 * WIDTH), jnp.float32),
        ]
        + gather_sems(len(QKV_CUTS))
        + [
            pltpu.SemaphoreType.DMA((len(COLUMN),)),
            pltpu.SemaphoreType.DMA((len(COLUMN),)),
            pltpu.SemaphoreType.DMA,
        ],
        compiler_params=pltpu.CompilerParams(
            collective_id=1, has_side_effects=True
        ),
        name="prepare",
    )(shard, patch, tree_input, page_row, length_row, leaf_row, parent_row)


def window(w):
    return 128 * (5 * (w // 4) + w % 4), 32 * (w % 4)


def draft_kernel(
    tables, fresh_ref, cache_ref, layer_ref, draft_ref, patch_ref, head_ref, new_ref,
    kept, rows, draft, patch, load, save, more, wide,
):
    pages = kept.shape[0]
    weights = [
        pltpu.make_async_copy(draft_ref, draft, wide.at[0]),
        pltpu.make_async_copy(patch_ref, patch, wide.at[1]),
    ]

    def page_of(ref, p, i):
        return ref.at[0, i, pl.ds(p * PAGE, PAGE)]

    def loads(p):
        return [
            pltpu.make_async_copy(page_of(cache_ref, p, i), kept.at[p, i], load.at[2 * p + i])
            for i in range(2)
        ]

    def saves(p):
        return [
            pltpu.make_async_copy(kept.at[p, i], page_of(new_ref, p, i), save.at[2 * p + i])
            for i in range(2)
        ]

    for p in range(pages):
        for copy in loads(p):
            copy.start()
    for copy in weights:
        copy.start()
    for p in range(pages):
        for copy in loads(p):
            copy.wait()
        row0 = tables[2, p] - tables[1, p]
        count = tables[3, p]

        @pl.when((row0 < PAGE) & (row0 + count > 0))
        def _():
            fetch = pltpu.make_async_copy(fresh_ref.at[tables[0, p], pl.ds(TREE, 16)], rows, more)
            fetch.start()
            fetch.wait()
            ahead = lax.broadcasted_iota(jnp.int32, (PAGE, 8), 0) - row0
            nth = lax.broadcasted_iota(jnp.int32, (PAGE, 8), 1)
            hot = ((ahead == nth) & (nth < count)).astype(jnp.float32).astype(jnp.bfloat16)
            index = lax.broadcasted_iota(jnp.int32, (PAGE, WIDTH), 0) - row0
            hit = (index >= 0) & (index < count)
            for i in range(2):
                taken = jnp.dot(
                    hot, rows[pl.ds(8 * i, 8), :], preferred_element_type=jnp.float32
                )
                old = kept[p, i].astype(jnp.float32)
                kept[p, i] = jnp.where(hit, taken, old).astype(jnp.bfloat16)

        for copy in saves(p):
            copy.start()
    weights[0].wait()
    layer = layer_ref[...]
    grown = dot_t(rms_rows(layer), draft[...])
    branch = (grown / (1.0 + jnp.exp(-grown))).astype(jnp.bfloat16)
    drafted = (layer.astype(jnp.float32) + branch.astype(jnp.float32)).astype(jnp.bfloat16)
    weights[1].wait()
    head_ref[...] = dot_t(drafted, patch[...]).astype(jnp.bfloat16)
    for p in range(pages):
        for copy in saves(p):
            copy.wait()


def draft_and_append(tables, gathered, cache, layer, draft, patch):
    pages = cache.shape[2] // PAGE
    return pl.pallas_call(
        draft_kernel,
        out_shape=[
            jax.ShapeDtypeStruct(layer.shape, layer.dtype),
            jax.ShapeDtypeStruct(cache.shape, cache.dtype),
        ],
        in_specs=[pl.BlockSpec(memory_space=pltpu.SMEM), HBM, HBM, VMEM, HBM, HBM],
        out_specs=[VMEM, HBM],
        scratch_shapes=[
            pltpu.VMEM((pages, 2, PAGE, WIDTH), jnp.bfloat16),
            pltpu.VMEM((16, WIDTH), jnp.bfloat16),
            pltpu.VMEM(draft.shape, draft.dtype),
            pltpu.VMEM(patch.shape, patch.dtype),
            pltpu.SemaphoreType.DMA((2 * pages,)),
            pltpu.SemaphoreType.DMA((2 * pages,)),
            pltpu.SemaphoreType.DMA,
            pltpu.SemaphoreType.DMA((2,)),
        ],
        compiler_params=pltpu.CompilerParams(vmem_limit_bytes=60 * 1024 * 1024),
        name="draft_and_append",
    )(tables, gathered, cache, layer, draft, patch)


PAIR = 2 * TREE
LINES = 8 * PAIR


def attend_scratch(pages):
    return [
        pltpu.VMEM((2, pages + 1, PAGE, WIDTH), jnp.bfloat16),
        pltpu.VMEM((BLK, TREE + 16, WIDTH), jnp.bfloat16),
        pltpu.SemaphoreType.DMA((2 * pages + 1,)),
        pltpu.VMEM((8, PAIR, 256), jnp.bfloat16),
        pltpu.VMEM((8, PAIR, 256), jnp.bfloat16),
        pltpu.VMEM((TREE, PAGE), jnp.float32),
        pltpu.VMEM((LINES, 128), jnp.float32),
        pltpu.VMEM((LINES, 128), jnp.bfloat16),
        pltpu.VMEM((LINES, 128), jnp.float32),
        pltpu.VMEM((LINES, 128), jnp.float32),
        pltpu.VMEM((LINES, 128), jnp.float32),
        pltpu.VMEM((8, PAIR, 256), jnp.float32),
        pltpu.VMEM((pages + 2, TREE, WIDTH), jnp.bfloat16),
        pltpu.VMEM((pages + 2, TREE, 128), jnp.float32),
    ]


def attend_steps(tables, query_ref, cache_ref, proj_ref, marks_ref, bufs, pause):
    (kept, query, load, ones, masked, marks, scores, weights, tops, dens, scales, acc, sums, stats) = bufs
    pages = cache_ref.shape[2] // PAGE
    factor = math.log2(math.e) / math.sqrt(HD)
    lanes = lax.broadcasted_iota(jnp.int32, (TREE, 128), 1)
    columns = lax.broadcasted_iota(jnp.int32, (TREE, 256), 1)
    copies = [
        pltpu.make_async_copy(
            cache_ref.at[0, i, pl.ds(p * PAGE, PAGE)], kept.at[i, p], load.at[i * pages + p]
        )
        for i in range(2)
        for p in range(pages)
    ]
    copies.append(pltpu.make_async_copy(query_ref, query, load.at[2 * pages]))
    for copy in copies:
        copy.start()
    yield

    def inside(w, i):
        begin = window(w)[1] + HD * i
        return (columns >= begin) & (columns < begin + HD)

    for w in range(8):
        for i in range(2):
            ones[w, pl.ds(TREE * i, TREE)] = (
                inside(w, i).astype(jnp.float32).astype(jnp.bfloat16)
            )
    for i in range(2):
        kept[i, pages, pl.ds(0, TREE)] = proj_ref[:, pl.ds((1 + i) * WIDTH, WIDTH)]
        kept[i, pages, pl.ds(TREE, PAGE - TREE)] = jnp.zeros((PAGE - TREE, WIDTH), jnp.bfloat16)
    marks[...] = jnp.zeros_like(marks)
    marks[:, pl.ds(0, TREE)] = marks_ref[...]
    tops[...] = jnp.full_like(tops, LOWEST)
    dens[...] = jnp.zeros_like(dens)
    acc[...] = jnp.zeros_like(acc)
    sums[pages + 1] = jnp.zeros((TREE, WIDTH), jnp.bfloat16)
    stats[pages + 1] = jnp.where(lanes < 64, LOWEST, 0.0)
    for copy in copies:
        copy.wait()

    def step(j, carry):
        start, length, owner = tables[1, j], tables[2, j], tables[4, j]
        page, fresh, tree = tables[5, j], tables[6, j] > 0, tables[8, j] > 0
        for w in range(8):
            picked = query[owner, pl.ds(0, TREE), pl.ds(window(w)[0], 256)]
            for i in range(2):
                half = pl.ds(TREE * i, TREE)
                masked[w, half] = picked * ones[w, half]
        for w in range(8):
            scores[pl.ds(PAIR * w, PAIR), :] = dot_t(
                masked[w], kept[0, page, :, pl.ds(window(w)[0], 256)]
            )
        near = (lanes + start < length).astype(jnp.float32)
        seen = jnp.where(tree, marks[...], near)
        shown = jnp.concatenate([seen] * 4, axis=0) > 0.5
        for part in range(4):
            rows = pl.ds(2 * PAIR * part, 2 * PAIR)
            part_scores = jnp.where(shown, scores[rows, :] * factor, LOWEST)
            before = jnp.where(fresh, LOWEST, tops[rows, :])
            top = jnp.maximum(before, jnp.ceil(jnp.max(part_scores, axis=1, keepdims=True)))
            weight = jnp.where(shown, jnp.exp2(part_scores - top), 0.0)
            scale = jnp.where(fresh, 0.0, jnp.exp2(before - top))
            tops[rows, :] = top
            scales[rows, :] = scale
            dens[rows, :] = dens[rows, :] * scale + jnp.sum(weight, axis=1, keepdims=True)
            weights[rows, :] = weight.astype(jnp.bfloat16)
        carried = None
        for w in range(8):
            rows = pl.ds(PAIR * w, PAIR)
            added = jnp.dot(
                weights[rows, :],
                kept[1, page, :, pl.ds(window(w)[0], 256)],
                preferred_element_type=jnp.float32,
            )
            scale = scales[rows, :]
            total = acc[w] * jnp.concatenate([scale, scale], axis=1) + added
            acc[w] = total
            picked = jnp.where(
                inside(w, 0), total[:TREE], jnp.where(inside(w, 1), total[TREE:], 0.0)
            )
            head = picked[:, :128]
            if w % 4:
                head = head + carried
            carried = picked[:, 128:]
            sums[j, :, pl.ds(window(w)[0], 128)] = head.astype(jnp.bfloat16)
            if w % 4 == 3:
                sums[j, :, pl.ds(window(w)[0] + 128, 128)] = carried.astype(jnp.bfloat16)
        row = jnp.full((TREE, 128), LOWEST, jnp.float32)
        for head in range(H):
            rows = pl.ds(TREE * head, TREE)
            row = jnp.where(lanes == head, tops[rows, :], row)
            row = jnp.where(lanes == 64 + head, dens[rows, :], row)
        stats[j] = row
        return carry

    first = 0
    for last in pause + (pages + 1,):
        lax.fori_loop(first, last, step, 0)
        first = last
        if last <= pages:
            yield


PAIR_ORDER = (
    [(2, b) for b in range(4)]
    + [(1, 2), (1, 3), (-1, 0), (-1, 1)]
    + [(1, 0), (1, 1), (-1, 2), (-1, 3)]
    + [(0, b) for b in range(4)]
)
REDUCE = numbered(
    [f"{kind}{i}{s}" for kind, n in (("P", 16), ("T", 4), ("L", 4), ("R", 4)) for i in range(n) for s in "ns"]
    + [f"{kind}{s}" for kind in ("t0", "t1", "l", "r") for s in "ns"]
)


PAUSES = (3, 6, 9, 12, 14)
ADVANCES = (0, 6, 10, 14, 18, 22)


def split_stats(stats):
    return stats, pltpu.roll(stats, 64, 1)


def combine(parts, spread):
    stats = [split_stats(s) for _, s in parts]
    lanes = lax.broadcasted_iota(jnp.int32, stats[0][0].shape, 1)
    top = stats[0][0]
    for s, _ in stats[1:]:
        top = jnp.maximum(top, s)
    total = None
    num = None
    for (n, _), (s, d) in zip(parts, stats):
        scale = jnp.where(lanes < H, jnp.exp2(jnp.minimum(s - top, 0.0)), 0.0)
        wide = jnp.dot(scale.astype(jnp.bfloat16), spread, preferred_element_type=jnp.float32)
        d = d * scale
        n = n.astype(jnp.float32) * wide
        total = d if total is None else total + d
        num = n if num is None else num + n
    return num, top, total


def join_stats(top, total):
    lanes = lax.broadcasted_iota(jnp.int32, top.shape, 1)
    return jnp.where(lanes < H, top, pltpu.roll(jnp.where(lanes < H, total, 0.0), 64, 1))


def reduce_steps(spot, tables, sums, stats, out, spread, bufs, ssem, rsem):
    pair_n, pair_s, work_n, work_s, thru_n, thru_s, left_n, left_s, right_n, right_s = bufs[:10]
    fin_n, fin_s, two_n, two_s, out_n, out_s = bufs[10:]
    sent = {}
    send = sender(sent, ssem, rsem, REDUCE)

    def put(event, src_n, src_s, dst_n, dst_s, who):
        send(event + "n", src_n, dst_n, who)
        send(event + "s", src_s, dst_s, who)

    def took(event):
        sent[event + "n"].wait_recv()
        sent[event + "s"].wait_recv()

    right, left = spot.at(1, 0), spot.at(-1, 0)
    up, down = spot.at(0, 1), spot.at(0, -1)
    other = (1 - spot.core) * 16
    mine = spot.core * 16
    for i, (a, b) in enumerate(PAIR_ORDER):
        found = tables[9, other + spot.chip(b, a)]
        out_n[i] = sums[found]
        out_s[i] = stats[found]
        put(f"P{i}", out_n.at[i], out_s.at[i], pair_n.at[i], pair_s.at[i], spot.sibling)
    yield

    def store(dst_n, dst_s, parts):
        n, top, total = combine(parts, spread())
        dst_n[...] = n.astype(jnp.bfloat16)
        dst_s[...] = join_stats(top, total)

    place = {pair: i for i, pair in enumerate(PAIR_ORDER)}
    for i, (a, b) in enumerate(PAIR_ORDER):
        took(f"P{i}")
        found = tables[9, mine + spot.chip(a, b)]
        store(
            work_n.at[i], work_s.at[i], [(sums[found], stats[found]), (pair_n[i], pair_s[i])]
        )
        if a == 2:
            put(
                f"T{b}", work_n.at[i], work_s.at[i], thru_n.at[b], thru_s.at[b],
                right if b < 2 else left,
            )
        elif (a == 1 and b >= 2):
            put(f"L{b}", work_n.at[i], work_s.at[i], left_n.at[b], left_s.at[b], right)
        elif (a == -1 and b < 2):
            put(f"R{b}", work_n.at[i], work_s.at[i], right_n.at[b], right_s.at[b], left)
        yield
    for b in range(4):
        took(f"T{b}")
        a = 1 if b < 2 else -1
        i = place[(a, b)]
        store(
            work_n.at[i], work_s.at[i], [(work_n[i], work_s[i]), (thru_n[b], thru_s[b])]
        )
        if a == 1:
            put(f"L{b}", work_n.at[i], work_s.at[i], left_n.at[b], left_s.at[b], right)
        else:
            put(f"R{b}", work_n.at[i], work_s.at[i], right_n.at[b], right_s.at[b], left)
        yield
    cuts = (pl.ds(0, 32), pl.ds(32, 16))
    for b in (2, 1, 3, 0):
        took(f"L{b}")
        took(f"R{b}")
        i = place[(0, b)]
        store(
            fin_n.at[b],
            fin_s.at[b],
            [(work_n[i], work_s[i]), (left_n[b], left_s[b]), (right_n[b], right_s[b])],
        )
        if b == 2:
            for half, who in ((0, up), (1, down)):
                put(
                    f"t{half}",
                    fin_n.at[2, cuts[half]],
                    fin_s.at[2, cuts[half]],
                    two_n.at[0, cuts[half]],
                    two_s.at[0, cuts[half]],
                    who,
                )
        yield
    for half, b in ((0, 1), (1, 3)):
        took(f"t{half}")
        rows = cuts[half]
        store(
            fin_n.at[b, rows],
            fin_s.at[b, rows],
            [(fin_n[b, rows], fin_s[b, rows]), (two_n[0, rows], two_s[0, rows])],
        )
        if b == 1:
            put("l", fin_n.at[1], fin_s.at[1], two_n.at[1], two_s.at[1], up)
        else:
            put("r", fin_n.at[3], fin_s.at[3], two_n.at[2], two_s.at[2], down)
        yield
    took("l")
    took("r")
    n, top, total = combine(
        [(fin_n[0], fin_s[0]), (two_n[1], two_s[1]), (two_n[2], two_s[2])], spread()
    )
    lanes = lax.broadcasted_iota(jnp.int32, total.shape, 1)
    inverse = jnp.where(lanes < H, 1.0 / jnp.where(lanes < H, total, 1.0), 0.0)
    wide = jnp.dot(
        inverse,
        spread().astype(jnp.float32),
        preferred_element_type=jnp.float32,
        precision=lax.Precision.HIGHEST,
    )
    out[...] = (n * wide).astype(jnp.bfloat16)
    for event in REDUCE:
        sent[event].wait_send()


def attend_and_reduce(tables, gathered, cache, projected, marks, spread, shards, collective_id):
    count = len(shards)
    pages = cache.shape[2] // PAGE

    def block(n):
        return [
            pltpu.VMEM((n, TREE, WIDTH), jnp.bfloat16),
            pltpu.VMEM((n, TREE, 128), jnp.float32),
        ]

    parts = [
        [pltpu.SemaphoreType.DMA((len(REDUCE),))] * 2,
        gather_sems(count),
        attend_scratch(pages),
        block(16) + block(16) + block(4) + block(4) + block(4) + block(4) + block(3) + block(16),
    ]

    def kernel(tables_ref, query_ref, cache_ref, proj_ref, marks_ref, spread_ref, *refs):
        ins = refs[:count]
        out = refs[count]
        outs = refs[count + 1 : 2 * count + 1]
        left = list(refs[2 * count + 1 :])
        scratch = []
        for part in parts:
            scratch.append(left[: len(part)])
            left = left[len(part) :]
        (ssem, rsem), gather_scratch, attend_bufs, reduce_bufs = scratch
        spot = Spot()
        work = attend_steps(
            tables_ref, query_ref, cache_ref, proj_ref, marks_ref, attend_bufs, PAUSES
        )
        next(work)
        greet_plane(spot)
        gathers = gather_all(spot, ins, outs, *gather_scratch)

        def advance():
            for one in gathers:
                next(one, None)

        advance()
        for _ in work:
            advance()
        for i, _ in enumerate(
            reduce_steps(
                spot,
                tables_ref,
                attend_bufs[-2],
                attend_bufs[-1],
                out,
                lambda: spread_ref[...],
                reduce_bufs,
                lambda e: ssem.at[e],
                lambda e: rsem.at[e],
            )
        ):
            if i in ADVANCES:
                advance()
        run_all(gathers)

    return pl.pallas_call(
        kernel,
        out_shape=[jax.ShapeDtypeStruct((TREE, WIDTH), jnp.bfloat16)]
        + [jax.ShapeDtypeStruct((BLK,) + s.shape, s.dtype) for s in shards],
        in_specs=[pl.BlockSpec(memory_space=pltpu.SMEM), ANY, ANY, VMEM, VMEM, VMEM] + [VMEM] * count,
        out_specs=[VMEM] + [ANY] * count,
        scratch_shapes=[ref for part in parts for ref in part],
        compiler_params=pltpu.CompilerParams(
            collective_id=collective_id,
            has_side_effects=True,
        ),
        name="attend_and_reduce",
    )(tables, gathered, cache, projected, marks, spread, *shards)


RETURN = numbered(["TA", "TB", "L", "R", "OA", "OB"])


def column_kernel(exchange):
    def kernel(block, out, thru, ssem, rsem, lsem):
        at = lax.axis_index("req")
        above, far, below = (at + 1) % 4, (at + 2) % 4, (at + 3) % 4
        barrier = pltpu.get_barrier_semaphore()
        for who in (above, below):
            pl.semaphore_signal(barrier, inc=1, device_id={"req": who}, device_id_type=MESH)
        pl.semaphore_wait(barrier, 2)
        sent = {}
        upper, lower = pl.ds(0, 32), pl.ds(32, TREE - 32)

        def put(event, src, dst, who):
            copy = pltpu.make_async_remote_copy(
                src_ref=src,
                dst_ref=dst,
                send_sem=ssem.at[RETURN[event]],
                recv_sem=rsem.at[RETURN[event]],
                device_id={"req": who},
                device_id_type=MESH,
            )
            copy.start()
            sent[event] = copy

        if exchange:
            put("TA", block.at[far, upper], thru.at[upper], above)
            put("TB", block.at[far, lower], thru.at[lower], below)
        put("L", block.at[above] if exchange else block, out.at[at], above)
        put("R", block.at[below] if exchange else block, out.at[at], below)
        local = pltpu.make_async_copy(block.at[at] if exchange else block, out.at[at], lsem)
        local.start()
        sent["TA" if exchange else "L"].wait_recv()
        put("OA", thru.at[upper] if exchange else out.at[below, upper], out.at[below, upper], above)
        sent["TB" if exchange else "R"].wait_recv()
        put("OB", thru.at[lower] if exchange else out.at[above, lower], out.at[above, lower], below)
        local.wait()
        for event in ("L", "R", "OA", "OB") if exchange else ("OA", "OB"):
            sent[event].wait_recv()
        for copy in sent.values():
            copy.wait_send()

    return kernel


def over_column(block, exchange, collective_id, name):
    shape = block.shape if exchange else (4,) + block.shape
    return pl.pallas_call(
        column_kernel(exchange),
        out_shape=jax.ShapeDtypeStruct(shape, block.dtype),
        in_specs=[VMEM],
        out_specs=VMEM,
        scratch_shapes=[
            pltpu.VMEM(block.shape[-2:], block.dtype),
            pltpu.SemaphoreType.DMA((len(RETURN),)),
            pltpu.SemaphoreType.DMA((len(RETURN),)),
            pltpu.SemaphoreType.DMA,
        ],
        compiler_params=pltpu.CompilerParams(
            collective_id=collective_id, has_side_effects=True
        ),
        name=name,
    )(block)


def on_device(
    tree_input,
    cache,
    page_table,
    lengths,
    parents,
    accept_leaf,
    w_qkv,
    w_out,
    w_up,
    w_down,
    w_draft,
    w_patch,
):
    width = WIDTH
    pool_pages = cache.shape[2] // PAGE
    draft_mine = lax.dynamic_index_in_dim(
        w_draft.transpose(0, 2, 1), lax.axis_index("req"), 0, keepdims=False
    )
    patch, projected, pack, tables, pages, marks = prepare(
        w_qkv.T, w_patch.T, tree_input, page_table, lengths, accept_leaf, parents, pool_pages
    )
    gathered, *full_early = all_gather(
        [pack, w_out.T, ],
        {0: QUERY_CUTS},
        2,
        "gather_query",
    )
    spread = (
        jnp.arange(128, dtype=jnp.int32)[:, None]
        == jnp.arange(width, dtype=jnp.int32)[None, :] // HD
    ).astype(jnp.bfloat16)
    attended, *full_late = attend_and_reduce(
        tables,
        gathered,
        cache,
        projected,
        marks,
        spread,
        [w_up.T, w_down, draft_mine],
        3,
    )
    full_out, full_up, full_down, full_draft, patch = (
        w.reshape(width, width) for w in (*full_early, *full_late, patch)
    )
    proj = dot_t(attended, full_out).astype(jnp.bfloat16)
    mid = (tree_input.astype(jnp.float32) + proj.astype(jnp.float32)).astype(jnp.bfloat16)
    hidden = jax.nn.gelu(dot_t(rms_rows(mid), full_up)).astype(jnp.bfloat16)
    feedforward = jnp.dot(hidden, full_down, preferred_element_type=jnp.float32)
    layer_out = (mid.astype(jnp.float32) + feedforward).astype(jnp.bfloat16)
    rows = over_column(layer_out, False, 4, "gather_rows").reshape(4 * TREE, width)
    head, cache_new = draft_and_append(pages, gathered, cache, rows, full_draft, patch)
    drafts = over_column(head.reshape(4, TREE, width), True, 5, "return_rows")
    return (layer_out, drafts, cache_new)


def solution(mesh):
    in_specs = (
        P(("req", "blk"), None),
        P("req", None, "blk", None),
        P("req", None),
        P("req", None),
        P(("req", "blk"), None),
        P("req", None),
        P(None, "blk"),
        P(None, "blk"),
        P(None, "blk"),
        P("blk", None),
        P(None, None, "blk"),
        P(None, "req"),
    )
    out_specs = (
        P(("req", "blk"), None),
        P(None, ("req", "blk"), None),
        P("req", None, "blk", None),
    )
    return jax.shard_map(
        on_device, mesh=mesh, in_specs=in_specs, out_specs=out_specs, check_vma=False
    )
```

```python
import math

import jax
import jax.numpy as jnp
from jax import lax
from jax.experimental import pallas as pl
from jax.experimental.pallas import tpu as pltpu
from jax.sharding import PartitionSpec as P

H = 16
HD = 80
TREE = 48
DEPTH = 5
PAGE = 128
BLK = 32
WIDTH = H * HD

EPS = 1e-06
LOWEST = -8388608.0
LEVEL_START = (0, 1, 5, 15, 30, 48)
MESH = pl.DeviceIdType.MESH
ROWSLOT = ((0, 0), (-1, 0), (1, 0), (2, 0))


def rms_rows(values):
    wide = values.astype(jnp.float32)
    return (wide * lax.rsqrt(jnp.mean(wide * wide, axis=-1, keepdims=True) + EPS)).astype(
        jnp.bfloat16
    )


def dot_t(left, right):
    return lax.dot_general(
        left, right, (((1,), (1,)), ((), ())), preferred_element_type=jnp.float32
    )


class Spot:
    def __init__(self):
        self.me = lax.axis_index("blk")
        self.core = self.me % 2
        x = (self.me // 2) % 4
        y = self.me // 8
        self.one = x + self.core * (y - x)
        self.two = y + self.core * (x - y)
        self.sibling = self.me + 1 - 2 * self.core

    def at(self, a, b):
        return self.core + 2 * self.chip(a, b)

    def chip(self, a, b):
        one = (self.one + a + 4) % 4
        two = (self.two + b + 4) % 4
        return (1 + 3 * self.core) * one + (4 - 3 * self.core) * two


def greet_plane(spot, column=False):
    barrier = pltpu.get_barrier_semaphore()
    for who in (spot.at(1, 0), spot.at(-1, 0), spot.at(0, 1), spot.at(0, -1), spot.sibling):
        pl.semaphore_signal(barrier, inc=1, device_id={"blk": who}, device_id_type=MESH)
    if column:
        at = lax.axis_index("req")
        for d in (1, 3):
            pl.semaphore_signal(
                barrier, inc=1, device_id={"req": (at + d) % 4}, device_id_type=MESH
            )
    pl.semaphore_wait(barrier, 7 if column else 5)


def numbered(names):
    return {name: i for i, name in enumerate(names)}


GATHER = numbered(
    ["L", "R", "OA", "OB"]
    + [f"{kind}{k}" for k in range(4) for kind in ("D", "U", "PA", "PB")]
    + [f"S{k}" for k in range(16)]
)


def sender(sent, ssem, rsem, events):
    def put(event, src, dst, who):
        copy = pltpu.make_async_remote_copy(
            src_ref=src,
            dst_ref=dst,
            send_sem=ssem(events[event]),
            recv_sem=rsem(events[event]),
            device_id={"blk": who},
            device_id_type=MESH,
        )
        copy.start()
        sent[event] = copy

    return put


def gather_steps(spot, shard, view, ssem, rsem, lsem, cut, ready=None):
    sent = {}
    send = sender(sent, ssem, rsem, GATHER)

    def put(event, src, slot, who, half=None):
        dst = view(slot)
        if half is not None:
            src, dst = cut(src, half), cut(dst, half)
        send(event, src, dst, who)

    left_over = list(range(16))

    def done(*slots):
        if ready is not None:
            for slot in slots:
                ready(slot)

    def from_sibling(*events):
        for k in events:
            left_over.remove(k)
            sent[f"S{k}"].wait_recv()
            a, b = ROWSLOT[k % 4][0], (0, -1, 1, 2)[k // 4]
            done(1 - spot.core + 2 * spot.chip(b, a))

    def early(*events):
        if ready is not None:
            from_sibling(*events)

    right, left = spot.at(1, 0), spot.at(-1, 0)
    up, down = spot.at(0, 1), spot.at(0, -1)
    local = pltpu.make_async_copy(shard, view(spot.me), lsem)
    local.start()
    put("L", shard, spot.me, right)
    put("R", shard, spot.me, left)
    put("D0", shard, spot.me, up)
    put("U0", shard, spot.me, down)
    put("S0", shard, spot.me, spot.sibling)
    yield
    for k, event in ((1, "L"), (2, "R")):
        slot = spot.at(*ROWSLOT[k])
        sent[event].wait_recv()
        if k == 1:
            put("OA", view(slot), slot, right, 0)
        else:
            put("OB", view(slot), slot, left, 1)
        put(f"D{k}", view(slot), slot, up)
        put(f"U{k}", view(slot), slot, down)
        put(f"S{k}", view(slot), slot, spot.sibling)
        done(slot)
        early(k - 1)
        yield

    def column(k):
        a = ROWSLOT[k][0]
        slot = spot.at(a, -1)
        sent[f"D{k}"].wait_recv()
        put(f"PA{k}", view(slot), slot, up, 0)
        put(f"S{4 + k}", view(slot), slot, spot.sibling)
        slot = spot.at(a, 1)
        sent[f"U{k}"].wait_recv()
        put(f"PB{k}", view(slot), slot, down, 1)
        put(f"S{8 + k}", view(slot), slot, spot.sibling)
        done(spot.at(a, -1), slot)

    column(0)
    early(2)
    yield
    sent["OA"].wait_recv()
    sent["OB"].wait_recv()
    slot = spot.at(2, 0)
    put("D3", view(slot), slot, up)
    put("U3", view(slot), slot, down)
    put("S3", view(slot), slot, spot.sibling)
    done(slot)
    early(4, 8)
    yield
    for k in (1, 2, 3):
        column(k)
        early(*((3,), (5, 9), (6, 10))[k - 1])
        yield
    for k in range(4):
        slot = spot.at(ROWSLOT[k][0], 2)
        sent[f"PA{k}"].wait_recv()
        sent[f"PB{k}"].wait_recv()
        put(f"S{12 + k}", view(slot), slot, spot.sibling)
        done(slot)
        early(*((7, 11) if k == 0 else (11 + k,)))
        yield
    from_sibling(*list(left_over))
    local.wait()
    for event in GATHER:
        sent[event].wait_send()


def run_all(steps):
    steps = list(steps)
    while steps:
        alive = []
        for step in steps:
            try:
                next(step)
                alive.append(step)
            except StopIteration:
                pass
        steps = alive


def row_halves(rows, tile):
    first = ((rows // 2) + tile - 1) // tile * tile

    def cut(ref, half):
        return ref.at[pl.ds(0, first)] if half == 0 else ref.at[pl.ds(first, rows - first)]

    return cut


def gather_all(spot, ins, outs, ssem, rsem, lsem, cuts=None, ready=None):
    count = len(GATHER)
    steps = []
    for i, (shard, out) in enumerate(zip(ins, outs)):
        first = 0
        for rows in (cuts or {}).get(i, (shard.shape[0],)):
            piece = pl.ds(first, rows)
            at = len(steps) * count
            steps.append(
                gather_steps(
                    spot,
                    shard.at[piece],
                    lambda slot, out=out, piece=piece: out.at[slot, piece],
                    lambda e, at=at: ssem.at[at + e],
                    lambda e, at=at: rsem.at[at + e],
                    lsem.at[len(steps)],
                    row_halves(rows, 16 if ready else 8),
                    (lambda slot: None) if ready else None,
                )
                if ready is None or first + rows < shard.shape[0]
                else gather_steps(
                    spot,
                    shard.at[piece],
                    lambda slot, out=out, piece=piece: out.at[slot, piece],
                    lambda e, at=at: ssem.at[at + e],
                    lambda e, at=at: rsem.at[at + e],
                    lsem.at[len(steps)],
                    row_halves(rows, 16),
                    ready,
                )
            )
            first += rows
    return steps


def gather_sems(arrays):
    return [
        pltpu.SemaphoreType.DMA((arrays * len(GATHER),)),
        pltpu.SemaphoreType.DMA((arrays * len(GATHER),)),
        pltpu.SemaphoreType.DMA((arrays,)),
    ]


COLUMN = numbered(["L", "R", "OA", "OB", "S1", "S2", "S3"])


def column_steps(spot, shard, out, ssem, rsem, lsem):
    at = lax.axis_index("req")
    above, below = (at + 1) % 4, (at + 3) % 4
    half = shard.shape[0] // 2
    base = spot.core * half
    rows = pl.ds(pl.multiple_of(base, 8), half)
    parts = [pl.ds(pl.multiple_of(base + i * (half // 2), 8), half // 2) for i in range(2)]
    sent = {}

    def put(event, src, slot, part, device):
        copy = pltpu.make_async_remote_copy(
            src_ref=src,
            dst_ref=out.at[slot, part],
            send_sem=ssem.at[COLUMN[event]],
            recv_sem=rsem.at[COLUMN[event]],
            device_id=device,
            device_id_type=MESH,
        )
        copy.start()
        sent[event] = copy

    local = pltpu.make_async_copy(shard, out.at[at], lsem)
    local.start()
    put("L", shard.at[rows], at, rows, {"req": above})
    put("R", shard.at[rows], at, rows, {"req": below})
    for _ in range(2):
        yield
    sent["L"].wait_recv()
    put("OA", out.at[below, parts[0]], below, parts[0], {"req": above})
    put("S1", out.at[below, rows], below, rows, {"blk": spot.sibling})
    sent["R"].wait_recv()
    put("OB", out.at[above, parts[1]], above, parts[1], {"req": below})
    put("S2", out.at[above, rows], above, rows, {"blk": spot.sibling})
    for _ in range(3):
        yield
    sent["OA"].wait_recv()
    sent["OB"].wait_recv()
    far = (at + 2) % 4
    put("S3", out.at[far, rows], far, rows, {"blk": spot.sibling})
    yield
    local.wait()
    for event in ("S1", "S2", "S3"):
        sent[event].wait_recv()
    for event in COLUMN:
        sent[event].wait_send()


ANY = pl.BlockSpec(memory_space=pl.ANY)
HBM = pl.BlockSpec(memory_space=pltpu.HBM)
VMEM = pl.BlockSpec(memory_space=pltpu.VMEM)


def all_gather(shards, cuts, collective_id, name):
    count = len(shards)

    def kernel(*refs):
        spot = Spot()
        greet_plane(spot)
        run_all(gather_all(spot, refs[:count], refs[count : 2 * count], *refs[2 * count :], cuts))

    return pl.pallas_call(
        kernel,
        out_shape=[jax.ShapeDtypeStruct((BLK,) + s.shape, s.dtype) for s in shards],
        in_specs=[VMEM] * count,
        out_specs=[ANY] * count,
        scratch_shapes=gather_sems(count + sum(len(rows) - 1 for rows in cuts.values())),
        compiler_params=pltpu.CompilerParams(collective_id=collective_id, has_side_effects=True),
        name=name,
    )(*shards)


QKV_CUTS = (48, 48, 24)
QUERY_CUTS = (32, 32)


def iota(shape, dim):
    return lax.broadcasted_iota(jnp.int32, shape, dim)


def to_column(row):
    n = row.shape[1]
    return jnp.sum(jnp.where(iota((n, n), 0) == iota((n, n), 1), row, 0), axis=1, keepdims=True)


def to_row(column):
    n = column.shape[0]
    return jnp.sum(jnp.where(iota((n, n), 0) == iota((n, n), 1), column, 0), axis=0, keepdims=True)


def tree_marks(parent_row, leaf):
    square = (TREE, TREE)
    climb = (to_column(parent_row) == iota(square, 1)).astype(jnp.float32)
    current = (iota(square, 0) == iota(square, 1)).astype(jnp.float32)
    marks = current
    for _ in range(DEPTH - 1):
        current = jnp.dot(current, climb, preferred_element_type=jnp.float32)
        marks = jnp.maximum(marks, current)
    chosen = jnp.sum(jnp.where(iota(square, 0) == leaf, marks, 0.0), axis=0, keepdims=True)
    upto = jnp.where(iota(square, 0) <= iota(square, 1), to_column(chosen), 0.0)
    nth = (jnp.sum(upto, axis=0, keepdims=True) - 1.0).astype(jnp.int32)
    picker = (chosen > 0.5) & (nth == iota((16, TREE), 0))
    return marks, picker.astype(jnp.float32)


def page_tables(page_row, length_row, leaf_row, myself, pool_pages):
    requests = length_row.shape[1]
    npages = (length_row + (DEPTH + PAGE - 1)) // PAGE
    square = (requests, requests)
    ends = jnp.sum(
        jnp.where(iota(square, 0) <= iota(square, 1), to_column(npages), 0), axis=0, keepdims=True
    )
    offsets = ends - npages
    my_end = jnp.sum(jnp.where(iota((1, requests), 1) == myself, ends, 0), axis=1, keepdims=True)
    accepted = 1 + sum((leaf_row >= first).astype(jnp.int32) for first in LEVEL_START[1:-1])
    lines = 24
    line = iota((lines, 1), 0)
    slots = page_row.shape[1]
    located = page_row == myself * pool_pages + iota((lines, slots), 0)
    where_at = jnp.sum(jnp.where(located, iota((lines, slots), 1), 0), axis=1, keepdims=True)
    owner = jnp.sum((ends <= where_at).astype(jnp.int32), axis=1, keepdims=True)
    hot = owner == iota((lines, requests), 1)

    def of_owner(row):
        return jnp.sum(jnp.where(hot, row, 0), axis=1, keepdims=True)

    is_tree = line == pool_pages
    spare = line > pool_pages
    owner_or_me = jnp.where(is_tree, myself, jnp.minimum(owner, requests - 1))
    place = owner_or_me % 2 * (requests // 2) + owner_or_me // 2
    start = jnp.where(is_tree, 0, (where_at - of_owner(offsets)) * PAGE)
    length = jnp.where(is_tree, 0, of_owner(length_row))
    count = jnp.where(is_tree, 0, of_owner(accepted))
    spots = jnp.where(is_tree, 2 * my_end - 1, jnp.where(spare, 4 * slots + line, 2 * where_at))
    rank = jnp.sum((to_row(spots) < spots).astype(jnp.int32), axis=1, keepdims=True)
    wide = (lines, 128)

    def in_order(column):
        return jnp.sum(jnp.where(rank == iota(wide, 1), column, 0), axis=0, keepdims=True)

    def as_it_lies(column):
        return jnp.sum(jnp.where(line == iota(wide, 1), column, 0), axis=0, keepdims=True)

    columns = [place, start, length, count, owner_or_me, line]
    rows = [in_order(column) for column in columns]
    lane = iota((1, 128), 1)
    fresh = ((rows[4] != pltpu.roll(rows[4], 1, 1)) | (lane == 0)).astype(jnp.int32)
    last = jnp.max(
        jnp.where((place == iota(wide, 1)) & jnp.logical_not(spare), rank, -1),
        axis=0,
        keepdims=True,
    )
    last = jnp.where(last < 0, pool_pages + 1, last)
    rows += [fresh, fresh, in_order(is_tree.astype(jnp.int32)), last]
    return rows, [as_it_lies(column) for column in (owner_or_me, start, length, count)]


def prepare(shard, patch, tree_input, page_row, length_row, leaf_row, parent_row, pool_pages):
    def kernel(
        shard_ref, patch_ref, x_ref, page_ref, length_ref, leaf_ref, parent_ref,
        full_patch_ref, projected_ref, pack_ref, steps_ref, pages_ref, marks_ref,
        full_ref, normed, parts, joined, *scratch,
    ):
        spot = Spot()
        columns = shard_ref.shape[0]
        greet_plane(spot, True)

        def project(slot):
            parts[slot, :, pl.ds(0, columns)] = dot_t(normed[...], full_ref[slot])

        steps = gather_all(
            spot, [shard_ref], [full_ref], *scratch[:3], {0: QKV_CUTS}, project
        )
        steps.append(column_steps(spot, patch_ref, full_patch_ref, *scratch[3:]))
        for one in steps:
            next(one)
        normed[...] = rms_rows(x_ref[...])
        parts[spot.me, :, pl.ds(0, columns)] = dot_t(normed[...], shard_ref[...])
        leaf = jnp.sum(
            jnp.where(iota(leaf_ref.shape, 1) == spot.me, leaf_ref[...], 0), axis=1, keepdims=True
        )
        marks_ref[...], picker = tree_marks(parent_ref[...], leaf)
        in_order, as_they_lie = page_tables(
            page_ref[...], length_ref[...], leaf_ref[...], spot.me, pool_pages
        )
        for k, row in enumerate(in_order):
            steps_ref[pl.ds(k, 1), :] = row
        for k, row in enumerate(as_they_lie):
            pages_ref[pl.ds(k, 1), :] = row
        run_all(steps)
        for slot in range(BLK):
            joined[:, pl.ds(columns * slot, columns)] = parts[slot, :, pl.ds(0, columns)]
        projected_ref[...] = joined[...].astype(jnp.bfloat16)
        pack_ref[pl.ds(0, TREE), :] = projected_ref[:, pl.ds(0, WIDTH)]
        picked = jnp.dot(
            picker.astype(jnp.bfloat16),
            projected_ref[:, pl.ds(WIDTH, 2 * WIDTH)],
            preferred_element_type=jnp.float32,
        )
        pack_ref[pl.ds(TREE, 16), :] = jnp.concatenate(
            [picked[:8, :WIDTH], picked[:8, WIDTH:]], axis=0
        ).astype(jnp.bfloat16)

    return pl.pallas_call(
        kernel,
        out_shape=[
            jax.ShapeDtypeStruct((4,) + patch.shape, patch.dtype),
            jax.ShapeDtypeStruct((TREE, 3 * WIDTH), jnp.bfloat16),
            jax.ShapeDtypeStruct((TREE + 16, WIDTH), jnp.bfloat16),
            jax.ShapeDtypeStruct((10, 128), jnp.int32),
            jax.ShapeDtypeStruct((4, 128), jnp.int32),
            jax.ShapeDtypeStruct((TREE, TREE), jnp.float32),
        ],
        in_specs=[VMEM] * 7,
        out_specs=[ANY] + [VMEM] * 5,
        scratch_shapes=[
            pltpu.VMEM((BLK,) + shard.shape, shard.dtype),
            pltpu.VMEM(tree_input.shape, jnp.bfloat16),
            pltpu.VMEM((BLK, TREE, 128), jnp.float32),
            pltpu.VMEM((TREE, 3 * WIDTH), jnp.float32),
        ]
        + gather_sems(len(QKV_CUTS))
        + [
            pltpu.SemaphoreType.DMA((len(COLUMN),)),
            pltpu.SemaphoreType.DMA((len(COLUMN),)),
            pltpu.SemaphoreType.DMA,
        ],
        compiler_params=pltpu.CompilerParams(
            collective_id=1, has_side_effects=True
        ),
        name="prepare",
    )(shard, patch, tree_input, page_row, length_row, leaf_row, parent_row)


def window(w):
    return 128 * (5 * (w // 4) + w % 4), 32 * (w % 4)


def draft_kernel(
    tables, fresh_ref, cache_ref, layer_ref, draft_ref, patch_ref, head_ref, new_ref,
    kept, rows, draft, patch, load, save, more, wide,
):
    pages = kept.shape[0]
    weights = [
        pltpu.make_async_copy(draft_ref, draft, wide.at[0]),
        pltpu.make_async_copy(patch_ref, patch, wide.at[1]),
    ]

    def page_of(ref, p, i):
        return ref.at[0, i, pl.ds(p * PAGE, PAGE)]

    def loads(p):
        return [
            pltpu.make_async_copy(page_of(cache_ref, p, i), kept.at[p, i], load.at[2 * p + i])
            for i in range(2)
        ]

    def saves(p):
        return [
            pltpu.make_async_copy(kept.at[p, i], page_of(new_ref, p, i), save.at[2 * p + i])
            for i in range(2)
        ]

    for p in range(pages):
        for copy in loads(p):
            copy.start()
    for copy in weights:
        copy.start()
    for p in range(pages):
        for copy in loads(p):
            copy.wait()
        row0 = tables[2, p] - tables[1, p]
        count = tables[3, p]

        @pl.when((row0 < PAGE) & (row0 + count > 0))
        def _():
            fetch = pltpu.make_async_copy(fresh_ref.at[tables[0, p], pl.ds(TREE, 16)], rows, more)
            fetch.start()
            fetch.wait()
            ahead = lax.broadcasted_iota(jnp.int32, (PAGE, 8), 0) - row0
            nth = lax.broadcasted_iota(jnp.int32, (PAGE, 8), 1)
            hot = ((ahead == nth) & (nth < count)).astype(jnp.float32).astype(jnp.bfloat16)
            index = lax.broadcasted_iota(jnp.int32, (PAGE, WIDTH), 0) - row0
            hit = (index >= 0) & (index < count)
            for i in range(2):
                taken = jnp.dot(
                    hot, rows[pl.ds(8 * i, 8), :], preferred_element_type=jnp.float32
                )
                old = kept[p, i].astype(jnp.float32)
                kept[p, i] = jnp.where(hit, taken, old).astype(jnp.bfloat16)

        for copy in saves(p):
            copy.start()
    weights[0].wait()
    layer = layer_ref[...]
    grown = dot_t(rms_rows(layer), draft[...])
    branch = (grown / (1.0 + jnp.exp(-grown))).astype(jnp.bfloat16)
    drafted = (layer.astype(jnp.float32) + branch.astype(jnp.float32)).astype(jnp.bfloat16)
    weights[1].wait()
    head_ref[...] = dot_t(drafted, patch[...]).astype(jnp.bfloat16)
    for p in range(pages):
        for copy in saves(p):
            copy.wait()


def draft_and_append(tables, gathered, cache, layer, draft, patch):
    pages = cache.shape[2] // PAGE
    return pl.pallas_call(
        draft_kernel,
        out_shape=[
            jax.ShapeDtypeStruct(layer.shape, layer.dtype),
            jax.ShapeDtypeStruct(cache.shape, cache.dtype),
        ],
        in_specs=[pl.BlockSpec(memory_space=pltpu.SMEM), HBM, HBM, VMEM, HBM, HBM],
        out_specs=[VMEM, HBM],
        scratch_shapes=[
            pltpu.VMEM((pages, 2, PAGE, WIDTH), jnp.bfloat16),
            pltpu.VMEM((16, WIDTH), jnp.bfloat16),
            pltpu.VMEM(draft.shape, draft.dtype),
            pltpu.VMEM(patch.shape, patch.dtype),
            pltpu.SemaphoreType.DMA((2 * pages,)),
            pltpu.SemaphoreType.DMA((2 * pages,)),
            pltpu.SemaphoreType.DMA,
            pltpu.SemaphoreType.DMA((2,)),
        ],
        compiler_params=pltpu.CompilerParams(vmem_limit_bytes=60 * 1024 * 1024),
        name="draft_and_append",
    )(tables, gathered, cache, layer, draft, patch)


PAIR = 2 * TREE
LINES = 8 * PAIR


def attend_scratch(pages):
    return [
        pltpu.VMEM((2, pages + 1, PAGE, WIDTH), jnp.bfloat16),
        pltpu.VMEM((BLK, TREE + 16, WIDTH), jnp.bfloat16),
        pltpu.SemaphoreType.DMA((2 * pages + 1,)),
        pltpu.VMEM((8, PAIR, 256), jnp.bfloat16),
        pltpu.VMEM((8, PAIR, 256), jnp.bfloat16),
        pltpu.VMEM((TREE, PAGE), jnp.float32),
        pltpu.VMEM((LINES, 128), jnp.float32),
        pltpu.VMEM((LINES, 128), jnp.bfloat16),
        pltpu.VMEM((LINES, 128), jnp.float32),
        pltpu.VMEM((LINES, 128), jnp.float32),
        pltpu.VMEM((LINES, 128), jnp.float32),
        pltpu.VMEM((8, PAIR, 256), jnp.float32),
        pltpu.VMEM((pages + 2, TREE, WIDTH), jnp.bfloat16),
        pltpu.VMEM((pages + 2, TREE, 128), jnp.float32),
    ]


def attend_steps(tables, query_ref, cache_ref, proj_ref, marks_ref, bufs, pause):
    (kept, query, load, ones, masked, marks, scores, weights, tops, dens, scales, acc, sums, stats) = bufs
    pages = cache_ref.shape[2] // PAGE
    factor = math.log2(math.e) / math.sqrt(HD)
    lanes = lax.broadcasted_iota(jnp.int32, (TREE, 128), 1)
    columns = lax.broadcasted_iota(jnp.int32, (TREE, 256), 1)
    copies = [
        pltpu.make_async_copy(
            cache_ref.at[0, i, pl.ds(p * PAGE, PAGE)], kept.at[i, p], load.at[i * pages + p]
        )
        for i in range(2)
        for p in range(pages)
    ]
    copies.append(pltpu.make_async_copy(query_ref, query, load.at[2 * pages]))
    for copy in copies:
        copy.start()
    yield

    def inside(w, i):
        begin = window(w)[1] + HD * i
        return (columns >= begin) & (columns < begin + HD)

    for w in range(8):
        for i in range(2):
            ones[w, pl.ds(TREE * i, TREE)] = (
                inside(w, i).astype(jnp.float32).astype(jnp.bfloat16)
            )
    for i in range(2):
        kept[i, pages, pl.ds(0, TREE)] = proj_ref[:, pl.ds((1 + i) * WIDTH, WIDTH)]
        kept[i, pages, pl.ds(TREE, PAGE - TREE)] = jnp.zeros((PAGE - TREE, WIDTH), jnp.bfloat16)
    marks[...] = jnp.zeros_like(marks)
    marks[:, pl.ds(0, TREE)] = marks_ref[...]
    tops[...] = jnp.full_like(tops, LOWEST)
    dens[...] = jnp.zeros_like(dens)
    acc[...] = jnp.zeros_like(acc)
    sums[pages + 1] = jnp.zeros((TREE, WIDTH), jnp.bfloat16)
    stats[pages + 1] = jnp.where(lanes < 64, LOWEST, 0.0)
    for copy in copies:
        copy.wait()

    def step(j, carry):
        start, length, owner = tables[1, j], tables[2, j], tables[4, j]
        page, fresh, tree = tables[5, j], tables[6, j] > 0, tables[8, j] > 0
        for w in range(8):
            picked = query[owner, pl.ds(0, TREE), pl.ds(window(w)[0], 256)]
            for i in range(2):
                half = pl.ds(TREE * i, TREE)
                masked[w, half] = picked * ones[w, half]
        for w in range(8):
            scores[pl.ds(PAIR * w, PAIR), :] = dot_t(
                masked[w], kept[0, page, :, pl.ds(window(w)[0], 256)]
            )
        near = (lanes + start < length).astype(jnp.float32)
        seen = jnp.where(tree, marks[...], near)
        shown = jnp.concatenate([seen] * 4, axis=0) > 0.5
        for part in range(4):
            rows = pl.ds(2 * PAIR * part, 2 * PAIR)
            part_scores = jnp.where(shown, scores[rows, :] * factor, LOWEST)
            before = jnp.where(fresh, LOWEST, tops[rows, :])
            top = jnp.maximum(before, jnp.ceil(jnp.max(part_scores, axis=1, keepdims=True)))
            weight = jnp.where(shown, jnp.exp2(part_scores - top), 0.0)
            scale = jnp.where(fresh, 0.0, jnp.exp2(before - top))
            tops[rows, :] = top
            scales[rows, :] = scale
            dens[rows, :] = dens[rows, :] * scale + jnp.sum(weight, axis=1, keepdims=True)
            weights[rows, :] = weight.astype(jnp.bfloat16)
        carried = None
        for w in range(8):
            rows = pl.ds(PAIR * w, PAIR)
            added = jnp.dot(
                weights[rows, :],
                kept[1, page, :, pl.ds(window(w)[0], 256)],
                preferred_element_type=jnp.float32,
            )
            scale = scales[rows, :]
            total = acc[w] * jnp.concatenate([scale, scale], axis=1) + added
            acc[w] = total
            picked = jnp.where(
                inside(w, 0), total[:TREE], jnp.where(inside(w, 1), total[TREE:], 0.0)
            )
            head = picked[:, :128]
            if w % 4:
                head = head + carried
            carried = picked[:, 128:]
            sums[j, :, pl.ds(window(w)[0], 128)] = head.astype(jnp.bfloat16)
            if w % 4 == 3:
                sums[j, :, pl.ds(window(w)[0] + 128, 128)] = carried.astype(jnp.bfloat16)
        row = jnp.full((TREE, 128), LOWEST, jnp.float32)
        for head in range(H):
            rows = pl.ds(TREE * head, TREE)
            row = jnp.where(lanes == head, tops[rows, :], row)
            row = jnp.where(lanes == 64 + head, dens[rows, :], row)
        stats[j] = row
        return carry

    first = 0
    for last in pause + (pages + 1,):
        lax.fori_loop(first, last, step, 0)
        first = last
        if last <= pages:
            yield


PAIR_ORDER = (
    [(2, b) for b in range(4)]
    + [(1, 2), (1, 3), (-1, 0), (-1, 1)]
    + [(1, 0), (1, 1), (-1, 2), (-1, 3)]
    + [(0, b) for b in range(4)]
)
REDUCE = numbered(
    [f"{kind}{i}{s}" for kind, n in (("P", 16), ("T", 4), ("L", 4), ("R", 4)) for i in range(n) for s in "ns"]
    + [f"{kind}{s}" for kind in ("t0", "t1", "l", "r") for s in "ns"]
)


PAUSES = (3, 6, 9, 12, 14)
ADVANCES = (8, 12, 16, 18, 20, 22)


def split_stats(stats):
    return stats, pltpu.roll(stats, 64, 1)


def combine(parts, spread):
    stats = [split_stats(s) for _, s in parts]
    lanes = lax.broadcasted_iota(jnp.int32, stats[0][0].shape, 1)
    top = stats[0][0]
    for s, _ in stats[1:]:
        top = jnp.maximum(top, s)
    total = None
    num = None
    for (n, _), (s, d) in zip(parts, stats):
        scale = jnp.where(lanes < H, jnp.exp2(jnp.minimum(s - top, 0.0)), 0.0)
        wide = jnp.dot(scale.astype(jnp.bfloat16), spread, preferred_element_type=jnp.float32)
        d = d * scale
        n = n.astype(jnp.float32) * wide
        total = d if total is None else total + d
        num = n if num is None else num + n
    return num, top, total


def join_stats(top, total):
    lanes = lax.broadcasted_iota(jnp.int32, top.shape, 1)
    return jnp.where(lanes < H, top, pltpu.roll(jnp.where(lanes < H, total, 0.0), 64, 1))


def reduce_steps(spot, tables, sums, stats, out, spread, bufs, ssem, rsem):
    pair_n, pair_s, work_n, work_s, thru_n, thru_s, left_n, left_s, right_n, right_s = bufs[:10]
    fin_n, fin_s, two_n, two_s, out_n, out_s = bufs[10:]
    sent = {}
    send = sender(sent, ssem, rsem, REDUCE)

    def put(event, src_n, src_s, dst_n, dst_s, who):
        send(event + "n", src_n, dst_n, who)
        send(event + "s", src_s, dst_s, who)

    def took(event):
        sent[event + "n"].wait_recv()
        sent[event + "s"].wait_recv()

    right, left = spot.at(1, 0), spot.at(-1, 0)
    up, down = spot.at(0, 1), spot.at(0, -1)
    other = (1 - spot.core) * 16
    mine = spot.core * 16
    for i, (a, b) in enumerate(PAIR_ORDER):
        found = tables[9, other + spot.chip(b, a)]
        out_n[i] = sums[found]
        out_s[i] = stats[found]
        put(f"P{i}", out_n.at[i], out_s.at[i], pair_n.at[i], pair_s.at[i], spot.sibling)
    yield

    def store(dst_n, dst_s, parts):
        n, top, total = combine(parts, spread())
        dst_n[...] = n.astype(jnp.bfloat16)
        dst_s[...] = join_stats(top, total)

    place = {pair: i for i, pair in enumerate(PAIR_ORDER)}
    for i, (a, b) in enumerate(PAIR_ORDER):
        took(f"P{i}")
        found = tables[9, mine + spot.chip(a, b)]
        store(
            work_n.at[i], work_s.at[i], [(sums[found], stats[found]), (pair_n[i], pair_s[i])]
        )
        if a == 2:
            put(
                f"T{b}", work_n.at[i], work_s.at[i], thru_n.at[b], thru_s.at[b],
                right if b < 2 else left,
            )
        elif (a == 1 and b >= 2):
            put(f"L{b}", work_n.at[i], work_s.at[i], left_n.at[b], left_s.at[b], right)
        elif (a == -1 and b < 2):
            put(f"R{b}", work_n.at[i], work_s.at[i], right_n.at[b], right_s.at[b], left)
        yield
    for b in range(4):
        took(f"T{b}")
        a = 1 if b < 2 else -1
        i = place[(a, b)]
        store(
            work_n.at[i], work_s.at[i], [(work_n[i], work_s[i]), (thru_n[b], thru_s[b])]
        )
        if a == 1:
            put(f"L{b}", work_n.at[i], work_s.at[i], left_n.at[b], left_s.at[b], right)
        else:
            put(f"R{b}", work_n.at[i], work_s.at[i], right_n.at[b], right_s.at[b], left)
        yield
    cuts = (pl.ds(0, 32), pl.ds(32, 16))
    for b in (2, 1, 3, 0):
        took(f"L{b}")
        took(f"R{b}")
        i = place[(0, b)]
        store(
            fin_n.at[b],
            fin_s.at[b],
            [(work_n[i], work_s[i]), (left_n[b], left_s[b]), (right_n[b], right_s[b])],
        )
        if b == 2:
            for half, who in ((0, up), (1, down)):
                put(
                    f"t{half}",
                    fin_n.at[2, cuts[half]],
                    fin_s.at[2, cuts[half]],
                    two_n.at[0, cuts[half]],
                    two_s.at[0, cuts[half]],
                    who,
                )
        yield
    for half, b in ((0, 1), (1, 3)):
        took(f"t{half}")
        rows = cuts[half]
        store(
            fin_n.at[b, rows],
            fin_s.at[b, rows],
            [(fin_n[b, rows], fin_s[b, rows]), (two_n[0, rows], two_s[0, rows])],
        )
        if b == 1:
            put("l", fin_n.at[1], fin_s.at[1], two_n.at[1], two_s.at[1], up)
        else:
            put("r", fin_n.at[3], fin_s.at[3], two_n.at[2], two_s.at[2], down)
        yield
    took("l")
    took("r")
    n, top, total = combine(
        [(fin_n[0], fin_s[0]), (two_n[1], two_s[1]), (two_n[2], two_s[2])], spread()
    )
    lanes = lax.broadcasted_iota(jnp.int32, total.shape, 1)
    inverse = jnp.where(lanes < H, 1.0 / jnp.where(lanes < H, total, 1.0), 0.0)
    wide = jnp.dot(
        inverse,
        spread().astype(jnp.float32),
        preferred_element_type=jnp.float32,
        precision=lax.Precision.HIGHEST,
    )
    out[...] = (n * wide).astype(jnp.bfloat16)
    for event in REDUCE:
        sent[event].wait_send()


def attend_and_reduce(tables, gathered, cache, projected, marks, spread, shards, collective_id):
    count = len(shards)
    pages = cache.shape[2] // PAGE

    def block(n):
        return [
            pltpu.VMEM((n, TREE, WIDTH), jnp.bfloat16),
            pltpu.VMEM((n, TREE, 128), jnp.float32),
        ]

    parts = [
        [pltpu.SemaphoreType.DMA((len(REDUCE),))] * 2,
        gather_sems(count),
        attend_scratch(pages),
        block(16) + block(16) + block(4) + block(4) + block(4) + block(4) + block(3) + block(16),
    ]

    def kernel(tables_ref, query_ref, cache_ref, proj_ref, marks_ref, spread_ref, *refs):
        ins = refs[:count]
        out = refs[count]
        outs = refs[count + 1 : 2 * count + 1]
        left = list(refs[2 * count + 1 :])
        scratch = []
        for part in parts:
            scratch.append(left[: len(part)])
            left = left[len(part) :]
        (ssem, rsem), gather_scratch, attend_bufs, reduce_bufs = scratch
        spot = Spot()
        work = attend_steps(
            tables_ref, query_ref, cache_ref, proj_ref, marks_ref, attend_bufs, PAUSES
        )
        next(work)
        greet_plane(spot)
        gathers = gather_all(spot, ins, outs, *gather_scratch)

        def advance():
            for one in gathers:
                next(one, None)

        advance()
        for _ in work:
            advance()
        for i, _ in enumerate(
            reduce_steps(
                spot,
                tables_ref,
                attend_bufs[-2],
                attend_bufs[-1],
                out,
                lambda: spread_ref[...],
                reduce_bufs,
                lambda e: ssem.at[e],
                lambda e: rsem.at[e],
            )
        ):
            if i in ADVANCES:
                advance()
        run_all(gathers)

    return pl.pallas_call(
        kernel,
        out_shape=[jax.ShapeDtypeStruct((TREE, WIDTH), jnp.bfloat16)]
        + [jax.ShapeDtypeStruct((BLK,) + s.shape, s.dtype) for s in shards],
        in_specs=[pl.BlockSpec(memory_space=pltpu.SMEM), ANY, ANY, VMEM, VMEM, VMEM] + [VMEM] * count,
        out_specs=[VMEM] + [ANY] * count,
        scratch_shapes=[ref for part in parts for ref in part],
        compiler_params=pltpu.CompilerParams(
            collective_id=collective_id,
            has_side_effects=True,
        ),
        name="attend_and_reduce",
    )(tables, gathered, cache, projected, marks, spread, *shards)


RETURN = numbered(["TA", "TB", "L", "R", "OA", "OB"])


def column_kernel(exchange):
    def kernel(block, out, thru, ssem, rsem, lsem):
        at = lax.axis_index("req")
        above, far, below = (at + 1) % 4, (at + 2) % 4, (at + 3) % 4
        barrier = pltpu.get_barrier_semaphore()
        for who in (above, below):
            pl.semaphore_signal(barrier, inc=1, device_id={"req": who}, device_id_type=MESH)
        pl.semaphore_wait(barrier, 2)
        sent = {}
        upper, lower = pl.ds(0, 32), pl.ds(32, TREE - 32)

        def put(event, src, dst, who):
            copy = pltpu.make_async_remote_copy(
                src_ref=src,
                dst_ref=dst,
                send_sem=ssem.at[RETURN[event]],
                recv_sem=rsem.at[RETURN[event]],
                device_id={"req": who},
                device_id_type=MESH,
            )
            copy.start()
            sent[event] = copy

        if exchange:
            put("TA", block.at[far, upper], thru.at[upper], above)
            put("TB", block.at[far, lower], thru.at[lower], below)
        put("L", block.at[above] if exchange else block, out.at[at], above)
        put("R", block.at[below] if exchange else block, out.at[at], below)
        local = pltpu.make_async_copy(block.at[at] if exchange else block, out.at[at], lsem)
        local.start()
        sent["TA" if exchange else "L"].wait_recv()
        put("OA", thru.at[upper] if exchange else out.at[below, upper], out.at[below, upper], above)
        sent["TB" if exchange else "R"].wait_recv()
        put("OB", thru.at[lower] if exchange else out.at[above, lower], out.at[above, lower], below)
        local.wait()
        for event in ("L", "R", "OA", "OB") if exchange else ("OA", "OB"):
            sent[event].wait_recv()
        for copy in sent.values():
            copy.wait_send()

    return kernel


def over_column(block, exchange, collective_id, name):
    shape = block.shape if exchange else (4,) + block.shape
    return pl.pallas_call(
        column_kernel(exchange),
        out_shape=jax.ShapeDtypeStruct(shape, block.dtype),
        in_specs=[VMEM],
        out_specs=VMEM,
        scratch_shapes=[
            pltpu.VMEM(block.shape[-2:], block.dtype),
            pltpu.SemaphoreType.DMA((len(RETURN),)),
            pltpu.SemaphoreType.DMA((len(RETURN),)),
            pltpu.SemaphoreType.DMA,
        ],
        compiler_params=pltpu.CompilerParams(
            collective_id=collective_id, has_side_effects=True
        ),
        name=name,
    )(block)


def on_device(
    tree_input,
    cache,
    page_table,
    lengths,
    parents,
    accept_leaf,
    w_qkv,
    w_out,
    w_up,
    w_down,
    w_draft,
    w_patch,
):
    width = WIDTH
    pool_pages = cache.shape[2] // PAGE
    draft_mine = lax.dynamic_index_in_dim(
        w_draft.transpose(0, 2, 1), lax.axis_index("req"), 0, keepdims=False
    )
    patch, projected, pack, tables, pages, marks = prepare(
        w_qkv.T, w_patch.T, tree_input, page_table, lengths, accept_leaf, parents, pool_pages
    )
    gathered, *full_early = all_gather(
        [pack, w_out.T, ],
        {0: QUERY_CUTS},
        2,
        "gather_query",
    )
    spread = (
        jnp.arange(128, dtype=jnp.int32)[:, None]
        == jnp.arange(width, dtype=jnp.int32)[None, :] // HD
    ).astype(jnp.bfloat16)
    attended, *full_late = attend_and_reduce(
        tables,
        gathered,
        cache,
        projected,
        marks,
        spread,
        [w_up.T, w_down, draft_mine],
        3,
    )
    full_out, full_up, full_down, full_draft, patch = (
        w.reshape(width, width) for w in (*full_early, *full_late, patch)
    )
    proj = dot_t(attended, full_out).astype(jnp.bfloat16)
    mid = (tree_input.astype(jnp.float32) + proj.astype(jnp.float32)).astype(jnp.bfloat16)
    hidden = jax.nn.gelu(dot_t(rms_rows(mid), full_up)).astype(jnp.bfloat16)
    feedforward = jnp.dot(hidden, full_down, preferred_element_type=jnp.float32)
    layer_out = (mid.astype(jnp.float32) + feedforward).astype(jnp.bfloat16)
    rows = over_column(layer_out, False, 4, "gather_rows").reshape(4 * TREE, width)
    head, cache_new = draft_and_append(pages, gathered, cache, rows, full_draft, patch)
    drafts = over_column(head.reshape(4, TREE, width), True, 5, "return_rows")
    return (layer_out, drafts, cache_new)


def solution(mesh):
    in_specs = (
        P(("req", "blk"), None),
        P("req", None, "blk", None),
        P("req", None),
        P("req", None),
        P(("req", "blk"), None),
        P("req", None),
        P(None, "blk"),
        P(None, "blk"),
        P(None, "blk"),
        P("blk", None),
        P(None, None, "blk"),
        P(None, "req"),
    )
    out_specs = (
        P(("req", "blk"), None),
        P(None, ("req", "blk"), None),
        P("req", None, "blk", None),
    )
    return jax.shard_map(
        on_device, mesh=mesh, in_specs=in_specs, out_specs=out_specs, check_vma=False
    )
```
